32 devices in a mesh: dp: 4 (over y, x), store: 8 (over z, core).
Axes of the slice: x: 2, y: 2, z: 4, core: 2. Of those that a mesh axis runs over, the one named last changes fastest.
Arguments:
- inputs: bfloat16 [4096, 1024], P(('dp', 'store')), may hold values from -6 to 6
- lengths: int32 [32], P(('dp', 'store')), may hold values from 64 to 128, as said below
- targets: int32 [4096], P('dp'), may hold values from 0 to 34303
- attn_qkv: bfloat16 [3, 1024, 1024], replicated, may hold values from -0.1875 to 0.1875
- attn_out: bfloat16 [1024, 1024], replicated, may hold values from -1 to 1
- ffn_up: bfloat16 [1024, 4096], replicated, may hold values from -0.1875 to 0.1875
- ffn_down: bfloat16 [4096, 1024], replicated, may hold values from -0.09375 to 0.09375
- norm_gains: float32 [3, 1024], replicated, may hold values from 0.25 to 1.75
- norm_shifts: float32 [3, 1024], replicated, may hold values from -1.5 to 1.5
- biases: float32 [4, 1024], replicated, may hold values from -1.5 to 1.5
- up_bias: float32 [4096], replicated, may hold values from -1.5 to 1.5
- cluster_proj: bfloat16 [1024, 2], replicated, may hold values from -0.1875 to 0.1875
- proj_first: bfloat16 [1024, 256], replicated, may hold values from -0.1875 to 0.1875
- proj_second: bfloat16 [1024, 64], replicated, may hold values from -0.1875 to 0.1875
- head_words: bfloat16 [1024, 2560], P(None, 'store'), may hold values from -0.1875 to 0.1875
- tail_first: bfloat16 [256, 5120], P(None, 'store'), may hold values from -0.375 to 0.375
- tail_second: bfloat16 [64, 26624], P(None, 'store'), may hold values from -0.75 to 0.75
- store_keys: bfloat16 [32768, 1024], P('store'), may hold values from -6 to 6
- block_rows: int32 [4, 8, 8, 128], P('dp', 'store'), may hold values from 0 to 4095
- near_slots: int32 [4, 8, 128, 8, 16], P('dp', 'store'), may hold values from 0 to 127, as said below
- near_words: int32 [4096, 128], P(('dp', 'store')), may hold values from 0 to 32703
Outputs:
- token_loss: float32 [4096], P(('dp', 'store'))
- input_grad: float32 [4096, 1024], P(('dp', 'store'))
- qkv_grad: float32 [3, 1024, 1024], P(None, 'store')
- out_grad: float32 [1024, 1024], P('store')
- up_grad: float32 [1024, 4096], P('store')
- down_grad: float32 [4096, 1024], P('store')
- gains_grad: float32 [3, 1024], P(None, 'store')
- shifts_grad: float32 [3, 1024], P(None, 'store')
- biases_grad: float32 [4, 1024], P(None, 'store')
- up_bias_grad: float32 [4096], P('store')
- cluster_grad: float32 [1024, 2], P('store')
- first_proj_grad: float32 [1024, 256], P('store')
- second_proj_grad: float32 [1024, 64], P('store')
- head_grad: float32 [1024, 2560], P(None, 'store')
- first_tail_grad: float32 [256, 5120], P(None, 'store')
- second_tail_grad: float32 [64, 26624], P(None, 'store')
The draws below stay inside these ranges and needn't reach their ends.
Inputs may be any that keep to these rules, and one draw needn't show every extreme that they name: `lengths`: some sequence has exactly 128 tokens in every draw. `near_slots`: the 16 candidates of one token at one owner are distinct.
All inputs are finite; a program needn't handle non-finite values.
Results may differ from the reference program's by a relative error of at most 0.025.
Values may be sent and summed in bfloat16 or wider, within the bound.
No kernel may reach another device: no remote copies, remote signals or barrier semaphores. Data moves between devices by JAX's collectives and lax.ppermute only.
A program may use at most 320 MiB of HBM per device.

```python
import math
import jax
import jax.numpy as jnp
from jax import lax

D = 1024
HEADS = 16
HD = 64
FF = 4096
P1D = 256
P2D = 64
T1_DEV = 640
T2_DEV = 3328
TOK_DEV = 128
DS_DEV = 4096
NB = 128
KB = 16
K = 128
HEAD = 2560
V1 = 5120
V2 = 26624
VOCAB = 34304
NSEQ = 32
TOKENS = 4096
STORE_ROWS = 32768
N_DP = 4
N_STORE = 8


store_word_cap = 32704


def draw_lengths(key, part):
    base_len = jax.random.randint(jax.random.fold_in(key, 1), (NSEQ,), TOK_DEV // 2, TOK_DEV + 1)
    chosen_seq = jax.random.randint(jax.random.fold_in(key, 2), (), 0, NSEQ)
    return jnp.where(jnp.arange(NSEQ) == chosen_seq, TOK_DEV, base_len).astype(jnp.int32)


def word_draw(key):
    base_key = jax.random.fold_in(key, 17)
    branch = jax.random.randint(jax.random.fold_in(base_key, 1), (TOKENS,), 0, 2)
    common = jax.random.randint(jax.random.fold_in(base_key, 2), (TOKENS,), 0, 64)
    spread = jax.random.randint(jax.random.fold_in(base_key, 3), (TOKENS,), 0, VOCAB)
    return jnp.where(branch == 0, common, spread).astype(jnp.int32)


def draw_targets(key, part):
    return word_draw(key)


def draw_near_words(key, part):
    own_words = word_draw(key)
    word_limit = min(VOCAB, store_word_cap)
    base_key = jax.random.fold_in(key, 29)
    hit_rate = jax.random.randint(jax.random.fold_in(base_key, 1), (TOKENS, 1), 0, 9)
    rolled = jax.random.randint(jax.random.fold_in(base_key, 2), (TOKENS, K), 0, 16)
    others = jax.random.randint(jax.random.fold_in(base_key, 3), (TOKENS, K), 0, word_limit)
    hits = (rolled < hit_rate) & (own_words[:, None] < word_limit)
    return jnp.where(hits, own_words[:, None], others).astype(jnp.int32)


def draw_near_slots(key, part):
    shape_base = (N_DP, N_STORE, TOK_DEV, N_STORE, 1)
    start_slot = jax.random.randint(jax.random.fold_in(key, 41), shape_base, 0, NB)
    stride = 2 * jax.random.randint(jax.random.fold_in(key, 42), shape_base, 0, NB // 2) + 1
    return ((start_slot + stride * jnp.arange(KB)) % NB).astype(jnp.int32)


def with_ends(array, stream_key, least, largest):
    place = [jax.random.randint(jax.random.fold_in(stream_key, axis), (), 0, length) for axis, length in enumerate(array.shape)]
    widest = array.shape.index(max(array.shape))
    next_to = place[:widest] + [(place[widest] + 1) % array.shape[widest]] + place[widest + 1:]
    return array.at[tuple(place)].set(least).at[tuple(next_to)].set(largest)


def steps_of(rng, shape, cuts, smallest, high):
    def one(position, parts):
        heights = jax.random.uniform(jax.random.fold_in(jax.random.fold_in(rng, 6), position), (parts,), jnp.float32, smallest / len(cuts), high / len(cuts))
        return jnp.repeat(jnp.exp(heights), shape[position] // parts).reshape((-1,) + (1,) * (len(shape) - position - 1))

    loudness = one(*cuts[0])
    for cut in cuts[1:]:
        loudness = loudness * one(*cut)
    return loudness


def normal_values(own_key, dims, deviation, reach, cuts=(), held_as=jnp.bfloat16):
    level = steps_of(own_key, dims, cuts, -0.22, 0.18) if cuts else 1.0
    values = jax.random.normal(own_key, dims, jnp.float32) * deviation * level
    return jnp.minimum(jnp.maximum(values, -reach), reach).astype(held_as)


def setup_inputs(seed: int = 0) -> dict:
    key_list = jax.random.split(jax.random.key(seed), 22)
    inputs = normal_values(key_list[0], (TOKENS, D), 1.0, 6.0, ((0, 32),))
    lengths = draw_lengths(jax.random.fold_in(key_list[21], 71), 0)
    targets = draw_targets(jax.random.fold_in(key_list[21], 71), 0)
    attn_qkv = normal_values(key_list[3], (3, D, D), D ** -0.5, 0.1875)
    attn_out = normal_values(key_list[4], (D, D), (D // 32) ** -0.5, 1.0)
    ffn_up = normal_values(key_list[5], (D, FF), D ** -0.5, 0.1875)
    ffn_down = normal_values(key_list[6], (FF, D), FF ** -0.5, 0.09375)
    norm_gains = jnp.clip(1.0 + 0.15 * jax.random.normal(key_list[7], (3, D), jnp.float32), 0.25, 1.75)
    norm_shifts = normal_values(key_list[8], (3, D), 0.3, 1.5, (), jnp.float32)
    biases = normal_values(key_list[9], (4, D), 0.3, 1.5, (), jnp.float32)
    up_bias = normal_values(key_list[10], (FF,), 0.3, 1.5, (), jnp.float32)
    cluster_proj = normal_values(key_list[11], (D, 2), D ** -0.5, 0.1875)
    proj_first = normal_values(key_list[12], (D, P1D), D ** -0.5, 0.1875)
    proj_second = normal_values(key_list[13], (D, P2D), D ** -0.5, 0.1875)
    head_words = normal_values(key_list[14], (D, HEAD), D ** -0.5, 0.1875, ((1, 8),))
    tail_first = normal_values(key_list[15], (P1D, V1), P1D ** -0.5, 0.375, ((1, 8),))
    tail_second = normal_values(key_list[16], (P2D, V2), P2D ** -0.5, 0.75, ((1, 8),))
    store_keys = normal_values(key_list[17], (STORE_ROWS, D), 1.0, 6.0, ((0, 8),))
    block_rows = with_ends(jax.random.randint(key_list[18], (N_DP, N_STORE, N_STORE, NB), 0, DS_DEV), jax.random.fold_in(key_list[18], 1), 0, DS_DEV - 1).astype(jnp.int32)
    near_slots = draw_near_slots(jax.random.fold_in(key_list[21], 71), 0)
    near_words = draw_near_words(jax.random.fold_in(key_list[21], 71), 0)
    return dict(inputs=inputs, lengths=lengths, targets=targets, attn_qkv=attn_qkv, attn_out=attn_out, ffn_up=ffn_up, ffn_down=ffn_down, norm_gains=norm_gains, norm_shifts=norm_shifts, biases=biases, up_bias=up_bias, cluster_proj=cluster_proj, proj_first=proj_first, proj_second=proj_second, head_words=head_words, tail_first=tail_first, tail_second=tail_second, store_keys=store_keys, block_rows=block_rows, near_slots=near_slots, near_words=near_words)


@jax.custom_vjp
def low(v):
    return lax.optimization_barrier(v.astype(jnp.bfloat16)).astype(jnp.float32)

@jax.custom_vjp
def low_back(v):
    return v

def low_keep(v):
    return (low(v), None)

def low_pass(kept, grad):
    return (grad,)

def back_keep(v):
    return (v, None)

def back_low(kept, grad):
    return (low(grad),)
low.defvjp(low_keep, low_pass)
low_back.defvjp(back_keep, back_low)
EPS = 1e-05
NEAR_WEIGHT = 0.25
NEG_FILL = -1e+30
HIGH = lax.Precision.HIGHEST

def layer_norm(values, gain_row, shift_row):
    row_mean = lax.optimization_barrier(jnp.mean(values, axis=-1, keepdims=True))
    centred = values - row_mean
    variance = lax.optimization_barrier(jnp.mean(centred * centred, axis=-1, keepdims=True))
    return centred * lax.rsqrt(variance + EPS) * gain_row + shift_row

def matmul(left, right):
    return jnp.dot(left, right, precision=HIGH)

def pick_column(logits, where_col):
    columns = jnp.arange(logits.shape[1])
    return lax.optimization_barrier(jnp.sum(jnp.where(columns[None, :] == where_col[:, None], logits, 0.0), axis=1))

def sequence_loss(weights, seq_in, seq_inputs, store_keys, key_norms):
    attn_qkv, attn_out, ffn_up, ffn_down, norm_gains, norm_shifts, biases, up_bias, cluster_proj, proj_first, proj_second, head_words, tail_first, tail_second = weights
    length, target_seq, near_seq, row_ids, slot_ids = seq_inputs
    positions = jnp.arange(TOK_DEV)
    valid_mask = (positions < length).astype(jnp.float32)
    allowed = (positions[None, :] <= positions[:, None]) & (positions[None, :] < length)
    normed = low(layer_norm(seq_in, norm_gains[0], norm_shifts[0]))
    query_rows = low(low_back(matmul(normed, attn_qkv[0]) + biases[0])).reshape(TOK_DEV, HEADS, HD)
    key_rows = low(low_back(matmul(normed, attn_qkv[1]))).reshape(TOK_DEV, HEADS, HD)
    valued = low(low_back(matmul(normed, attn_qkv[2]) + biases[1])).reshape(TOK_DEV, HEADS, HD)
    scores = jnp.einsum('thd,shd->hts', query_rows, key_rows, precision=HIGH) * HD ** (-0.5)
    scores = low_back(jnp.where(allowed[None], scores, NEG_FILL))
    attn_probs = jax.nn.softmax(scores, axis=-1)
    mixed_rows = jnp.einsum('hts,shd->thd', low(attn_probs), valued, precision=HIGH).reshape(TOK_DEV, D)
    mixed_rows = low(low_back(mixed_rows))
    first_sum = seq_in + low_back(matmul(mixed_rows, attn_out) + biases[2])
    second_in = low(layer_norm(first_sum, norm_gains[1], norm_shifts[1]))
    pre_act = low_back(matmul(second_in, ffn_up) + up_bias)
    activation = low(jnp.maximum(pre_act, 0.0))
    second_sum = first_sum + low_back(matmul(activation, ffn_down) + biases[3])
    hidden = low(layer_norm(second_sum, norm_gains[2], norm_shifts[2]))
    cluster = matmul(hidden, cluster_proj)
    tail_in_one = low(matmul(hidden, proj_first))
    tail_in_two = low(matmul(hidden, proj_second))
    head_logits = low_back(matmul(hidden, head_words))
    one_copies = low_back(jnp.broadcast_to(tail_in_one[:, None, :], (TOK_DEV, N_STORE, P1D)))
    two_copies = low_back(jnp.broadcast_to(tail_in_two[:, None, :], (TOK_DEV, N_STORE, P2D)))
    first_logits = low_back(jnp.einsum('tnk,knv->tnv', one_copies, tail_first.reshape(P1D, N_STORE, T1_DEV), precision=HIGH)).reshape(TOK_DEV, V1)
    second_logits = low_back(jnp.einsum('tnk,knv->tnv', two_copies, tail_second.reshape(P2D, N_STORE, T2_DEV), precision=HIGH)).reshape(TOK_DEV, V2)
    in_first = ((target_seq >= HEAD) & (target_seq < HEAD + V1)).astype(jnp.float32)
    in_second = (target_seq >= HEAD + V1).astype(jnp.float32)
    picked = pick_column(head_logits, target_seq) + pick_column(first_logits, target_seq - HEAD) + pick_column(second_logits, target_seq - HEAD - V1)
    log_head = jnp.log(lax.optimization_barrier(jnp.sum(jnp.exp(head_logits), axis=1)) + lax.optimization_barrier(jnp.sum(jnp.exp(cluster), axis=1)))
    log_first = jnp.log(lax.optimization_barrier(jnp.sum(jnp.exp(first_logits), axis=1)))
    log_second = jnp.log(lax.optimization_barrier(jnp.sum(jnp.exp(second_logits), axis=1)))
    log_model = picked - log_head + in_first * (cluster[:, 0] - log_first) + in_second * (cluster[:, 1] - log_second)
    block_keys = store_keys[row_ids].astype(jnp.float32)
    block_norms = key_norms[row_ids]
    key_scale = 1.0 / math.sqrt(D)
    dense_dots = jnp.einsum('td,nbd->tnb', hidden, block_keys, precision=HIGH)
    scaled = dense_dots * key_scale - block_norms[None] * (0.5 * key_scale)
    chosen = low_back(jnp.take_along_axis(scaled, slot_ids, axis=2).reshape(TOK_DEV, K))
    near_probs = jax.nn.softmax(chosen, axis=1)
    matched = (near_seq == target_seq[:, None]).astype(jnp.float32)
    near_mass = lax.optimization_barrier(jnp.sum(near_probs * matched, axis=1))
    mixture = NEAR_WEIGHT * near_mass + (1.0 - NEAR_WEIGHT) * jnp.exp(log_model)
    return -valid_mask * jnp.log(mixture)

def reference(inputs, lengths, targets, attn_qkv, attn_out, ffn_up, ffn_down, norm_gains, norm_shifts, biases, up_bias, cluster_proj, proj_first, proj_second, head_words, tail_first, tail_second, store_keys, block_rows, near_slots, near_words):
    weights = tuple((weight.astype(jnp.float32) for weight in (attn_qkv, attn_out, ffn_up, ffn_down, norm_gains, norm_shifts, biases, up_bias, cluster_proj, proj_first, proj_second, head_words, tail_first, tail_second)))
    seq_block = inputs.astype(jnp.float32).reshape(NSEQ, TOK_DEV, D)
    offsets = (jnp.arange(N_STORE) * DS_DEV).astype(jnp.int32)
    row_ids = block_rows.transpose(0, 2, 1, 3).reshape(NSEQ, N_STORE, NB).astype(jnp.int32) + offsets[None, :, None]
    slot_ids = near_slots.transpose(0, 3, 2, 1, 4).reshape(NSEQ, TOK_DEV, N_STORE, KB).astype(jnp.int32)
    seq_inputs = (lengths, targets.reshape(NSEQ, TOK_DEV), near_words.reshape(NSEQ, TOK_DEV, K), row_ids, slot_ids)
    key_norms = lax.optimization_barrier(jnp.sum(jnp.square(store_keys.astype(jnp.float32)), axis=1))

    def objective(weight_set, seq_all):

        def per_sequence(seq_item):
            seq_in, seq_data = seq_item
            return sequence_loss(weight_set, seq_in, seq_data, store_keys, key_norms)
        losses = lax.map(jax.checkpoint(per_sequence), (seq_all, seq_inputs))
        return (jnp.sum(losses), losses)
    summed, pull_back, losses = jax.vjp(objective, weights, seq_block, has_aux=True)
    weight_grads, seq_grads = pull_back(jnp.ones_like(summed))
    return (losses.reshape(TOKENS), seq_grads.reshape(TOKENS, D), weight_grads[0], weight_grads[1], weight_grads[2], weight_grads[3], weight_grads[4], weight_grads[5], weight_grads[6], weight_grads[7], weight_grads[8], weight_grads[9], weight_grads[10], weight_grads[11], weight_grads[12], weight_grads[13])
```

```python
import math

import jax
import jax.numpy as jnp
from jax import lax
from jax.experimental import pallas as pl
from jax.experimental.pallas import tpu as pltpu
from jax.sharding import Mesh
from jax.sharding import PartitionSpec as P

HEADS = 16
HD = 64


EPS = 1e-05
NEAR_WEIGHT = 0.25
NEG_FILL = -1e30
HIGH = lax.Precision.HIGHEST
STORE = ("line", "core")
LOW = jnp.bfloat16
WIDE = jnp.float32
CHUNK = 1024


def product(left, right):
    return jnp.dot(left, right, preferred_element_type=WIDE)


def product_tn(left, right):
    return lax.dot_general(left, right, (((0,), (0,)), ((), ())), preferred_element_type=WIDE)


def product_nt(left, right):
    return lax.dot_general(left, right, (((1,), (1,)), ((), ())), preferred_element_type=WIDE)


def norm_forward(values, gain_row, shift_row):
    row_mean = jnp.mean(values, axis=-1, keepdims=True)
    centred = values - row_mean
    inverse = lax.rsqrt(jnp.mean(centred * centred, axis=-1, keepdims=True) + EPS)
    unit_rows = centred * inverse
    return (unit_rows * gain_row + shift_row, unit_rows, inverse)


def norm_backward(grad_out, unit_rows, inverse, gain_row):
    scaled = grad_out * gain_row
    grad_in = inverse * (
        scaled
        - jnp.mean(scaled, axis=-1, keepdims=True)
        - unit_rows * jnp.mean(scaled * unit_rows, axis=-1, keepdims=True)
    )
    return (grad_in, jnp.sum(grad_out * unit_rows, axis=0), jnp.sum(grad_out, axis=0))


def attention_scores(query_low, key_low, allowed):
    scores = jnp.einsum(
        "thd,shd->hts", query_low, key_low, preferred_element_type=WIDE
    ) * HD ** (-0.5)
    return jnp.where(allowed[None], scores, NEG_FILL)


def swap_partner(value, axis, bit):
    count = lax.axis_size(axis)
    return lax.ppermute(value, axis, [(k, k ^ bit) for k in range(count)])


def halving_order():
    lines = lax.axis_size("line")
    line_bits = lines.bit_length() - 1
    offsets = []
    for place in range(2 * lines):
        core_off = place >> line_bits
        rest = place & (lines - 1)
        line_off = sum(((rest >> k) & 1) << (line_bits - 1 - k) for k in range(line_bits))
        offsets.append(line_off * 2 + core_off)
    return offsets


def halve_store(keep, send):
    lines = lax.axis_size("line")
    received = swap_partner(send, "core", 1)
    current = keep.astype(WIDE) + received.astype(WIDE)
    bit = 1
    while bit < lines:
        half = current.shape[0] // 2
        received = swap_partner(current[half:].astype(LOW), "line", bit)
        current = current[:half] + received.astype(WIDE)
        bit *= 2
    return current[0]


def tile_kernel(order_ref, left_ref, right_ref, out_ref):
    out_ref[0] = lax.dot_general(
        left_ref[...], right_ref[...], (((0,), (0,)), ((), ())), preferred_element_type=WIDE
    ).astype(out_ref.dtype)


def grad_tiles(order, left_all, first_col, width, right):
    tokens, columns = right.shape
    blocks = order.shape[0]
    base = first_col // width
    return pl.pallas_call(
        tile_kernel,
        grid_spec=pltpu.PrefetchScalarGridSpec(
            num_scalar_prefetch=1,
            grid=(blocks,),
            in_specs=[
                pl.BlockSpec((tokens, width), lambda r, order: (0, base + order[r])),
                pl.BlockSpec((tokens, columns), lambda r, order: (0, 0)),
            ],
            out_specs=pl.BlockSpec((1, width, columns), lambda r, order: (r, 0, 0)),
        ),
        out_shape=jax.ShapeDtypeStruct((blocks, width, columns), LOW),
        name="grad_tiles",
    )(order, left_all, right)


def weight_grad(my_index, left_all, first_col, rows, right_parts):
    tokens = left_all.shape[0]
    blocks = lax.axis_size("line") * 2
    right = right_parts.reshape(tokens, right_parts.shape[2])
    order = jnp.bitwise_xor(my_index, jnp.array(halving_order(), jnp.int32))
    width = rows // blocks
    if width % 128 == 0:
        send = grad_tiles(order[blocks // 2 :], left_all, first_col, width, right)
        keep = grad_tiles(order[: blocks // 2], left_all, first_col, width, right)
    else:
        tile = product_tn(left_all[:, first_col : first_col + rows], right).astype(LOW)
        tile = jnp.take(tile.reshape(blocks, width, -1), order, axis=0)
        keep, send = tile[: blocks // 2], tile[blocks // 2 :]
    return halve_store(keep, send)


def join_kernel(order_ref, *refs):
    out_ref = refs[-1]
    for k, ref in enumerate(refs[:-1]):

        @pl.when(pl.program_id(0) == k)
        def _():
            out_ref[...] = ref[...].astype(WIDE)


def join_columns(own, groups=1):
    count = lax.axis_size("dp")
    rows = own.shape[0]
    width = own.shape[1] // groups
    own = own.astype(LOW)
    pieces = [own] + [swap_partner(own, "dp", q) for q in range(1, count)]
    order = jnp.bitwise_xor(lax.axis_index("dp"), jnp.arange(count, dtype=jnp.int32))
    if rows % 8 == 0 and width % 128 == 0:
        return pl.pallas_call(
            join_kernel,
            grid_spec=pltpu.PrefetchScalarGridSpec(
                num_scalar_prefetch=1,
                grid=(count, groups),
                in_specs=[
                    pl.BlockSpec((rows, width), lambda q, g, order: (0, g)) for _ in pieces
                ],
                out_specs=pl.BlockSpec(
                    (None, rows, width), lambda q, g, order: (g, 0, order[q])
                ),
            ),
            out_shape=jax.ShapeDtypeStruct((groups, rows, count * width), WIDE),
            name="join_columns",
        )(order, *pieces)
    joined = jnp.take(jnp.stack(pieces), order, axis=0)
    joined = joined.reshape(count, rows, groups, width).transpose(2, 1, 0, 3)
    return joined.reshape(groups, rows, count * width).astype(WIDE)


def exchange_columns(value):
    count = lax.axis_size("dp")
    tokens, columns = value.shape
    parts = value.reshape(tokens, count, columns // count).transpose(1, 0, 2)
    return lax.all_to_all(parts, "dp", 0, 0)


def shards(
    inputs,
    lengths,
    targets,
    attn_qkv,
    attn_out,
    ffn_up,
    ffn_down,
    norm_gains,
    norm_shifts,
    biases,
    up_bias,
    cluster_proj,
    proj_first,
    proj_second,
    head_words,
    tail_first,
    tail_second,
    store_keys,
    block_rows,
    near_slots,
    near_words,
):
    tokens_here = inputs.shape[0]
    d_model = inputs.shape[1]
    dp_count = lax.axis_size("dp")
    sources = lax.axis_size("line") * 2
    my_index = lax.axis_index("line") * 2 + lax.axis_index("core")
    group_rows = tokens_here * sources
    head_cols = head_words.shape[1]
    first_cols = tail_first.shape[1]
    second_cols = tail_second.shape[1]
    head_total = head_cols * sources
    first_total = first_cols * sources
    ff_width = ffn_up.shape[1]
    positions = jnp.arange(tokens_here)
    length_now = lengths[0]
    valid_mask = (positions < length_now).astype(WIDE)
    allowed = (positions[None, :] <= positions[:, None]) & (positions[None, :] < length_now)

    block_in = inputs.astype(WIDE)
    normed, unit_one, inv_one = norm_forward(block_in, norm_gains[0], norm_shifts[0])
    normed_low = normed.astype(LOW)
    projected = jnp.einsum("td,cde->cte", normed_low, attn_qkv, preferred_element_type=WIDE)
    query_low = (projected[0] + biases[0]).astype(LOW).reshape(tokens_here, HEADS, HD)
    key_low = projected[1].astype(LOW).reshape(tokens_here, HEADS, HD)
    value_low = (projected[2] + biases[1]).astype(LOW).reshape(tokens_here, HEADS, HD)
    scores = attention_scores(query_low, key_low, allowed)
    top_score = jnp.max(scores, axis=-1, keepdims=True)
    log_total = top_score + jnp.log(jnp.sum(jnp.exp(scores - top_score), axis=-1, keepdims=True))
    attn_probs = jnp.exp(scores - log_total)
    mixed_low = (
        jnp.einsum("hts,shd->thd", attn_probs.astype(LOW), value_low, preferred_element_type=WIDE)
        .reshape(tokens_here, d_model)
        .astype(LOW)
    )
    first_sum = block_in + product(mixed_low, attn_out) + biases[2]
    second_norm, unit_two, inv_two = norm_forward(first_sum, norm_gains[1], norm_shifts[1])
    second_low = second_norm.astype(LOW)
    pre_act = product(second_low, ffn_up) + up_bias
    act_low = jnp.maximum(pre_act, 0.0).astype(LOW)
    second_sum = first_sum + product(act_low, ffn_down) + biases[3]
    final_norm, unit_three, inv_three = norm_forward(second_sum, norm_gains[2], norm_shifts[2])
    hidden_low = final_norm.astype(LOW)
    cluster_logits = lax.dot_general(
        cluster_proj, hidden_low, (((0,), (1,)), ((), ())), preferred_element_type=WIDE
    )

    rows_all = lax.all_gather(hidden_low, STORE, axis=0, tiled=True)

    key_block = jnp.take(store_keys, block_rows[0, 0].reshape(-1), axis=0)
    key_scale = 1.0 / math.sqrt(d_model)
    key_wide = key_block.astype(WIDE)
    norm_block = jnp.sum(key_wide * key_wide, axis=1).reshape(sources, -1)
    near_count = norm_block.shape[1]
    key_block = key_block.reshape(sources, near_count, d_model)
    slots_t = near_slots[0, 0].transpose(1, 2, 0)
    slot_count = slots_t.shape[1]
    words_t = near_words.T
    row_ids = jnp.arange(near_count)

    left_low = jnp.concatenate([act_low, second_low, mixed_low, normed_low], axis=1)
    left_low, rows_all = lax.optimization_barrier((left_low, rows_all))
    left_all = lax.all_gather(left_low, "dp", axis=0, tiled=True)

    dense_dots = jnp.einsum(
        "jnd,jtd->jnt",
        key_block,
        rows_all.reshape(sources, tokens_here, d_model),
        preferred_element_type=WIDE,
    )
    scored = dense_dots * key_scale - norm_block[:, :, None] * (0.5 * key_scale)
    chosen = jnp.sum(
        jnp.where(
            slots_t[:, :, None, :] == row_ids[None, None, :, None], scored[:, None, :, :], 0.0
        ),
        axis=2,
    )

    chunk = min(CHUNK, group_rows)
    chunk_count = group_rows // chunk

    def over_chunks(function, *arrays):
        if chunk_count == 1:
            return function(*arrays)
        split = [a.reshape((chunk_count, chunk) + a.shape[1:]) for a in arrays]
        return lax.map(lambda items: function(*items), tuple(split))

    def word_places(words_here):
        head_pos = words_here - my_index * head_cols
        first_pos = words_here - head_total - my_index * first_cols
        second_pos = words_here - head_total - first_total - my_index * second_cols
        return head_pos, first_pos, second_pos

    def logits_of(rows_here):
        ones_here = product(rows_here, proj_first).astype(LOW)
        twos_here = product(rows_here, proj_second).astype(LOW)
        return (
            ones_here,
            twos_here,
            product(rows_here, head_words),
            product(ones_here, tail_first),
            product(twos_here, tail_second),
        )

    def is_word(logits, where_col):
        return jnp.arange(logits.shape[1])[None, :] == where_col[:, None]

    def word_stats(rows_here, words_here):
        places = word_places(words_here)
        logits = logits_of(rows_here)[2:]
        picked = sum(
            jnp.sum(jnp.where(is_word(item, place), item, 0.0), axis=1)
            for item, place in zip(logits, places)
        )
        return jnp.stack([jnp.sum(jnp.exp(item), axis=1) for item in logits] + [picked], axis=1)

    row_stats = over_chunks(word_stats, rows_all, targets).reshape(sources, tokens_here, 4)
    outgoing = jnp.concatenate([chosen, row_stats.transpose(0, 2, 1)], axis=1)
    incoming = lax.all_to_all(outgoing, STORE, 0, 0)

    near_scores = incoming[:, :slot_count].reshape(sources * slot_count, tokens_here)
    own_stats = jnp.sum(incoming[:, slot_count:], axis=0)
    own_words = lax.dynamic_slice_in_dim(targets, my_index * tokens_here, tokens_here, 0)
    in_first = ((own_words >= head_total) & (own_words < head_total + first_total)).astype(WIDE)
    in_second = (own_words >= head_total + first_total).astype(WIDE)
    head_sum = own_stats[0] + jnp.sum(jnp.exp(cluster_logits), axis=0)
    log_head = jnp.log(head_sum)
    log_first = jnp.log(own_stats[1])
    log_second = jnp.log(own_stats[2])
    log_model = (
        own_stats[3]
        - log_head
        + in_first * (cluster_logits[0] - log_first)
        + in_second * (cluster_logits[1] - log_second)
    )
    near_top = jnp.max(near_scores, axis=0, keepdims=True)
    near_exp = jnp.exp(near_scores - near_top)
    near_probs = near_exp / jnp.sum(near_exp, axis=0, keepdims=True)
    matched = (words_t == own_words[None, :]).astype(WIDE)
    near_mass = jnp.sum(near_probs * matched, axis=0)
    model_prob = jnp.exp(log_model)
    mixture = NEAR_WEIGHT * near_mass + (1.0 - NEAR_WEIGHT) * model_prob
    token_loss = -valid_mask * jnp.log(mixture)
    model_weight = valid_mask * (1.0 - NEAR_WEIGHT) * model_prob / mixture
    near_weight = valid_mask * NEAR_WEIGHT / mixture
    score_grad = -near_weight[None, :] * near_probs * (matched - near_mass[None, :])
    coef = jnp.stack([model_weight, log_head, log_first, log_second])
    returning = jnp.concatenate(
        [
            score_grad.reshape(sources, slot_count, tokens_here),
            jnp.broadcast_to(coef[None], (sources,) + coef.shape),
        ],
        axis=1,
    )
    returned = lax.all_to_all(returning, STORE, 0, 0)

    grads_back = returned[:, :slot_count].astype(LOW)
    coef_all = returned[:, slot_count:].transpose(0, 2, 1).reshape(group_rows, 4)
    dense_grad = jnp.sum(
        jnp.where(
            slots_t[:, :, None, :] == row_ids[None, None, :, None], grads_back[:, :, None, :], 0.0
        ).astype(WIDE),
        axis=1,
    ).astype(LOW)
    near_term = (
        jnp.einsum("jnt,jnd->jtd", dense_grad, key_block, preferred_element_type=WIDE).reshape(
            group_rows, d_model
        )
        * key_scale
    )

    def word_grads(rows_here, words_here, coef_here):
        places = word_places(words_here)
        ones_here, twos_here, *logits = logits_of(rows_here)
        first_here = ((words_here >= head_total) & (words_here < head_total + first_total)).astype(
            WIDE
        )
        second_here = (words_here >= head_total + first_total).astype(WIDE)
        weights = (
            coef_here[:, 0],
            coef_here[:, 0] * first_here,
            coef_here[:, 0] * second_here,
        )
        head_grad, first_grad, second_grad = (
            (
                weight[:, None]
                * (jnp.exp(item - coef_here[:, n + 1][:, None]) - is_word(item, place).astype(WIDE))
            ).astype(LOW)
            for n, (weight, item, place) in enumerate(zip(weights, logits, places))
        )
        back_one = product_nt(first_grad, tail_first).astype(LOW)
        back_two = product_nt(second_grad, tail_second).astype(LOW)
        row_term = (
            product_nt(head_grad, head_words)
            + product_nt(back_one, proj_first)
            + product_nt(back_two, proj_second)
        )
        return row_term, (
            (rows_here, head_grad),
            (ones_here, first_grad),
            (twos_here, second_grad),
            (rows_here, back_one),
            (rows_here, back_two),
        )

    def summed_products(pairs):
        return [product_tn(left, right) for left, right in pairs]

    lines = lax.axis_size("line")
    line = lax.axis_index("line")
    core = lax.axis_index("core")
    if lines == 4:
        half = group_rows // 2
        pair = line >> 1

        def side(which):
            start = which * half
            rows_here = lax.dynamic_slice_in_dim(rows_all, start, half, 0)
            words_here = lax.dynamic_slice_in_dim(targets, start, half, 0)
            coef_here = lax.dynamic_slice_in_dim(coef_all, start, half, 0)
            near_here = lax.dynamic_slice_in_dim(near_term, start, half, 0)
            row_term, pairs = word_grads(rows_here, words_here, coef_here)
            terms = (row_term + near_here).astype(LOW).reshape(2, 2, tokens_here, d_model)
            other = lax.dynamic_index_in_dim(terms, 1 - core, 1, keepdims=False)
            mine = lax.dynamic_index_in_dim(terms, core, 1, keepdims=False)
            both = mine.astype(WIDE) + swap_partner(other, "core", 1).astype(WIDE)
            same = lax.dynamic_index_in_dim(both, line & 1, 0, keepdims=False)
            cross = lax.dynamic_index_in_dim(both, 1 - (line & 1), 0, keepdims=False)
            return same, cross, pairs

        far_same, far_cross, far_pairs = side(1 - pair)
        from_two = swap_partner(far_same.astype(LOW), "line", 2)
        from_three = swap_partner(far_cross.astype(LOW), "line", 3)
        near_same, near_cross, near_pairs = side(pair)
        from_one = swap_partner(near_cross.astype(LOW), "line", 1)
        far_accs = summed_products(far_pairs)
        near_accs = summed_products(near_pairs)
        word_accs = [a + b for a, b in zip(far_accs, near_accs)]
        row_back = (
            near_same + from_one.astype(WIDE) + from_two.astype(WIDE) + from_three.astype(WIDE)
        )
    else:

        def chunk_grads(*items):
            row_term, pairs = word_grads(*items)
            return (row_term, *summed_products(pairs))

        vocab_terms, *word_accs = over_chunks(chunk_grads, rows_all, targets, coef_all)
        if chunk_count > 1:
            word_accs = [jnp.sum(item, axis=0) for item in word_accs]
        row_terms = (vocab_terms.reshape(group_rows, d_model) + near_term).astype(LOW)
        row_back = lax.psum_scatter(row_terms, STORE, scatter_dimension=0, tiled=True).astype(WIDE)
    head_acc, first_acc, second_acc, pone_acc, ptwo_acc = word_accs

    own_rows = d_model // sources
    proj_acc = jnp.concatenate([pone_acc, ptwo_acc], axis=1).astype(LOW)
    proj_blocks = jnp.take(
        proj_acc.reshape(sources, own_rows, proj_acc.shape[1]),
        jnp.bitwise_xor(my_index, jnp.array(halving_order(), jnp.int32)),
        axis=0,
    )
    proj_own = halve_store(proj_blocks[: sources // 2], proj_blocks[sources // 2 :])
    word_sums = lax.psum(
        tuple(item.astype(LOW) for item in (head_acc, first_acc, second_acc, proj_own)), "dp"
    )
    head_out, first_out, second_out, proj_out = (item.astype(WIDE) for item in word_sums)

    cluster_rows = model_weight[None, :] * (
        jnp.exp(cluster_logits - log_head[None, :]) - jnp.stack([in_first, in_second])
    )
    hidden_grad = row_back + lax.dot_general(
        cluster_rows, cluster_proj.astype(WIDE), (((0,), (1,)), ((), ())), precision=HIGH
    )
    cluster_acc = jnp.dot(cluster_rows, hidden_low.astype(WIDE), precision=HIGH)
    second_grad, gain_three, shift_three = norm_backward(
        hidden_grad, unit_three, inv_three, norm_gains[2]
    )
    down_in = second_grad.astype(LOW)
    down_parts = exchange_columns(down_in)
    bias_down = jnp.sum(down_in.astype(WIDE), axis=0)
    act_grad = product_nt(down_in, ffn_down)
    pre_grad = jnp.where(pre_act > 0, act_grad, 0.0).astype(LOW)
    up_parts = exchange_columns(pre_grad)
    up_bias_acc = jnp.sum(pre_grad.astype(WIDE), axis=0)
    norm_two_grad = product_nt(pre_grad, ffn_up)
    back_second, gain_two, shift_two = norm_backward(
        norm_two_grad, unit_two, inv_two, norm_gains[1]
    )
    first_grad_sum = second_grad + back_second
    attn_in = first_grad_sum.astype(LOW)
    out_parts = exchange_columns(attn_in)
    bias_attn = jnp.sum(attn_in.astype(WIDE), axis=0)
    mixed_grad = product_nt(attn_in, attn_out).astype(LOW).reshape(tokens_here, HEADS, HD)
    prob_grad = jnp.einsum("thd,shd->hts", mixed_grad, value_low, preferred_element_type=WIDE)
    row_delta = jnp.sum(attn_probs * prob_grad, axis=-1, keepdims=True)
    attn_score_grad = (attn_probs * (prob_grad - row_delta)).astype(LOW)
    query_grad = (
        jnp.einsum("hts,shd->thd", attn_score_grad, key_low, preferred_element_type=WIDE)
        * HD ** (-0.5)
    ).astype(LOW)
    key_grad = (
        jnp.einsum("hts,thd->shd", attn_score_grad, query_low, preferred_element_type=WIDE)
        * HD ** (-0.5)
    ).astype(LOW)
    value_grad = jnp.einsum(
        "hts,thd->shd", attn_probs.astype(LOW), mixed_grad, preferred_element_type=WIDE
    ).astype(LOW)
    stacked = jnp.stack([query_grad, key_grad, value_grad]).reshape(3, tokens_here, d_model)
    head_width = d_model // dp_count
    qkv_parts = lax.all_to_all(
        stacked.reshape(3, tokens_here, dp_count, head_width)
        .transpose(2, 1, 0, 3)
        .reshape(dp_count, tokens_here, 3 * head_width),
        "dp",
        0,
        0,
    )
    normed_grad = jnp.einsum("cte,cde->td", stacked, attn_qkv, preferred_element_type=WIDE)
    back_first, gain_one, shift_one = norm_backward(normed_grad, unit_one, inv_one, norm_gains[0])
    input_grad = first_grad_sum + back_first
    stacked_f = stacked.astype(WIDE)

    marks = [0, ff_width, ff_width + d_model, ff_width + 2 * d_model]
    down_own = weight_grad(my_index, left_all, marks[0], ff_width, down_parts)
    up_own = weight_grad(my_index, left_all, marks[1], d_model, up_parts)
    out_own = weight_grad(my_index, left_all, marks[2], d_model, out_parts)
    qkv_own = weight_grad(my_index, left_all, marks[3], d_model, qkv_parts)
    down_out = join_columns(down_own)[0]
    up_out = join_columns(up_own)[0]
    out_out = join_columns(out_own)[0]
    qkv_out = join_columns(qkv_own, 3)

    def by_store(value):
        rows = value.shape[0] if value.ndim > 1 else 1
        return value.reshape(rows, sources, -1).transpose(1, 0, 2).reshape(sources, -1)

    small = jnp.concatenate(
        [
            by_store(jnp.stack([gain_one, gain_two, gain_three])),
            by_store(jnp.stack([shift_one, shift_two, shift_three])),
            by_store(
                jnp.stack(
                    [jnp.sum(stacked_f[0], axis=0), jnp.sum(stacked_f[2], axis=0), bias_attn, bias_down]
                )
            ),
            by_store(up_bias_acc),
            by_store(cluster_acc),
        ],
        axis=1,
    )
    small = jnp.broadcast_to(small[None], (dp_count,) + small.shape)
    small = small.reshape(dp_count * sources, -1, min(128, own_rows))
    small_sum = jnp.sum(lax.all_to_all(small, ("dp",) + STORE, 0, 0), axis=0).reshape(-1)
    sizes = [3 * own_rows, 3 * own_rows, 4 * own_rows, ff_width // sources, 2 * own_rows]
    ends = [0]
    for size in sizes:
        ends.append(ends[-1] + size)
    gains_out, shifts_out, biases_out, upb_out, cluster_out = (
        small_sum[a:b] for a, b in zip(ends[:-1], ends[1:])
    )
    return (
        token_loss,
        input_grad,
        qkv_out,
        out_out,
        up_out,
        down_out,
        gains_out.reshape(3, own_rows),
        shifts_out.reshape(3, own_rows),
        biases_out.reshape(4, own_rows),
        upb_out,
        cluster_out.reshape(2, own_rows).T,
        proj_out[:, : proj_first.shape[1]],
        proj_out[:, proj_first.shape[1] :],
        head_out,
        first_out,
        second_out,
    )


def solution(mesh):
    dp_count = mesh.shape["dp"]
    store_count = mesh.shape["store"]
    split = Mesh(mesh.devices.reshape(dp_count, store_count // 2, 2), ("dp",) + STORE)
    everyone = ("dp",) + STORE
    return jax.shard_map(
        shards,
        mesh=split,
        in_specs=(
            P(everyone, None),
            P(everyone),
            P("dp"),
            P(),
            P(),
            P(),
            P(),
            P(),
            P(),
            P(),
            P(),
            P(),
            P(),
            P(),
            P(None, STORE),
            P(None, STORE),
            P(None, STORE),
            P(STORE, None),
            P("dp", STORE, None, None),
            P("dp", STORE, None, None, None),
            P(everyone, None),
        ),
        out_specs=(
            P(everyone),
            P(everyone, None),
            P(None, STORE, None),
            P(STORE, None),
            P(STORE, None),
            P(STORE, None),
            P(None, STORE),
            P(None, STORE),
            P(None, STORE),
            P(STORE),
            P(STORE, None),
            P(STORE, None),
            P(STORE, None),
            P(None, STORE),
            P(None, STORE),
            P(None, STORE),
        ),
        check_vma=False,
    )
```

```python
import math

import jax
import jax.numpy as jnp
from jax import lax
from jax.experimental import pallas as pl
from jax.experimental.pallas import tpu as pltpu
from jax.sharding import Mesh
from jax.sharding import PartitionSpec as P

HEADS = 16
HD = 64


EPS = 1e-05
NEAR_WEIGHT = 0.25
NEG_FILL = -1e30
HIGH = lax.Precision.HIGHEST
STORE = ("line", "core")
LOW = jnp.bfloat16
WIDE = jnp.float32
SECOND_TILE = 256


def product(left, right):
    return jnp.dot(left, right, preferred_element_type=WIDE)


def product_tn(left, right):
    return lax.dot_general(left, right, (((0,), (0,)), ((), ())), preferred_element_type=WIDE)


def product_nt(left, right):
    return lax.dot_general(left, right, (((1,), (1,)), ((), ())), preferred_element_type=WIDE)


def norm_forward(values, gain_row, shift_row):
    row_mean = jnp.mean(values, axis=-1, keepdims=True)
    centred = values - row_mean
    inverse = lax.rsqrt(jnp.mean(centred * centred, axis=-1, keepdims=True) + EPS)
    unit_rows = centred * inverse
    return (unit_rows * gain_row + shift_row, unit_rows, inverse)


def norm_backward(grad_out, unit_rows, inverse, gain_row):
    scaled = grad_out * gain_row
    grad_in = inverse * (
        scaled
        - jnp.mean(scaled, axis=-1, keepdims=True)
        - unit_rows * jnp.mean(scaled * unit_rows, axis=-1, keepdims=True)
    )
    return (grad_in, jnp.sum(grad_out * unit_rows, axis=0, keepdims=True), jnp.sum(grad_out, axis=0, keepdims=True))


def swap_partner(value, axis, bit):
    count = lax.axis_size(axis)
    return lax.ppermute(value, axis, [(k, k ^ bit) for k in range(count)])


def after(value, *others):
    return lax.optimization_barrier((value, *others))[0]


class Halving:
    def __init__(self, blocks):
        lines = lax.axis_size("line")
        line = lax.axis_index("line")
        self.rest = blocks.shape[1:]
        self.current = blocks.reshape((lines, 2) + self.rest)
        self.steps = [(lax.axis_index("core"), "core", 1)]
        bit = 1
        while bit < lines:
            self.steps.append(((line // bit) & 1, "line", bit))
            bit *= 2
        self.received = None
        self.send()

    def send(self):
        mine, axis, bit = self.steps.pop(0)
        value = self.current
        outgoing = lax.dynamic_index_in_dim(value, 1 - mine, 1, keepdims=False).astype(LOW)
        self.outgoing = outgoing
        self.current = lax.dynamic_index_in_dim(value, mine, 1, keepdims=False)
        self.received = swap_partner(outgoing, axis, bit)

    def add(self, *others):
        received = after(self.received, *others) if others else self.received
        self.current = self.current.astype(WIDE) + received.astype(WIDE)
        if self.steps:
            self.current = self.current.reshape((-1, 2) + self.rest)
            self.send()
        return self.outgoing

    def finish(self, *others):
        while self.steps:
            self.add(*others)
        self.add(*others)
        return self.current[0].astype(LOW)


def grad_tile(left, right_parts):
    blocks = lax.axis_size("line") * 2
    right = right_parts.reshape(left.shape[0], right_parts.shape[2])
    tile = product_tn(left, right).astype(LOW)
    return tile.reshape(blocks, -1, right.shape[1])


def gather_dp(own):
    count = lax.axis_size("dp")
    return [own] + [swap_partner(own, "dp", q) for q in range(1, count)]


def join_pieces(pieces, axis, start, width, join_axis):
    count = len(pieces)
    me = lax.axis_index("dp")
    pieces = [lax.slice_in_dim(piece, start, start + width, axis=axis) for piece in pieces]
    bit = 1
    while bit < count:
        is_set = (me // bit) & 1 == 1
        pieces = [jnp.where(is_set, pieces[k ^ bit], pieces[k]) for k in range(count)]
        bit *= 2
    return jnp.concatenate([piece.astype(WIDE) for piece in pieces], axis=join_axis)


def exchange_columns(value):
    count = lax.axis_size("dp")
    tokens, columns = value.shape
    parts = value.reshape(tokens, count, columns // count).transpose(1, 0, 2)
    return lax.all_to_all(parts, "dp", 0, 0)


def cost(micros):
    return pl.CostEstimate(flops=int(micros * 9e8), transcendentals=0, bytes_accessed=1 << 20)


def head_masks(width):
    lanes = lax.broadcasted_iota(jnp.int32, (1, width), 1)
    return [(lanes // HD) % 2 == half for half in range(2)]


def masked_softmax(scores, allowed):
    scores = jnp.where(allowed, scores * HD ** (-0.5), NEG_FILL)
    exps = jnp.exp(scores - jnp.max(scores, axis=-1, keepdims=True))
    return exps / jnp.sum(exps, axis=-1, keepdims=True)


def seen_keys(tokens, length):
    rows = lax.broadcasted_iota(jnp.int32, (tokens, tokens), 0)
    cols = lax.broadcasted_iota(jnp.int32, (tokens, tokens), 1)
    return (cols <= rows) & (cols < length)


def attention_kernel(
    length_ref,
    in_ref,
    qkv_ref,
    out_w_ref,
    gains_ref,
    shifts_ref,
    biases_ref,
    group_bias_ref,
    query_ref,
    key_ref,
    value_ref,
    mixed_ref,
    normed_ref,
    first_ref,
    second_ref,
    normed_scr,
    acc_scr,
):
    step = pl.program_id(0)
    tokens = in_ref.shape[0]
    width = query_ref.shape[1]

    @pl.when(step == 0)
    def _():
        block_in = in_ref[...].astype(WIDE)
        normed = norm_forward(block_in, gains_ref[0:1], shifts_ref[0:1])[0].astype(LOW)
        normed_scr[...] = normed
        normed_ref[...] = normed
        acc_scr[...] = block_in + biases_ref[2:3]

    normed = normed_scr[...]
    query = (product(normed, qkv_ref[0]) + group_bias_ref[0:1]).astype(LOW)
    key = product(normed, qkv_ref[1]).astype(LOW)
    value = (product(normed, qkv_ref[2]) + group_bias_ref[1:2]).astype(LOW)
    query_ref[...] = query
    key_ref[...] = key
    value_ref[...] = value
    allowed = seen_keys(tokens, length_ref[0])
    masks = head_masks(128)
    zero = jnp.zeros((tokens, 128), LOW)
    for pair in range(width // 128):
        cols = slice(pair * 128, (pair + 1) * 128)
        q_pair, k_pair, v_pair = query[:, cols], key[:, cols], value[:, cols]
        mixed = jnp.zeros((tokens, 128), WIDE)
        for mask in masks:
            probs = masked_softmax(product_nt(q_pair, jnp.where(mask, k_pair, zero)), allowed)
            mixed = mixed + product(probs.astype(LOW), jnp.where(mask, v_pair, zero))
        mixed_ref[:, cols] = mixed.astype(LOW)
    acc_scr[...] += product(mixed_ref[...], out_w_ref[...])

    @pl.when(step == pl.num_programs(0) - 1)
    def _():
        first_sum = acc_scr[...]
        first_ref[...] = first_sum
        second_ref[...] = norm_forward(first_sum, gains_ref[1:2], shifts_ref[1:2])[0].astype(LOW)


def attention_block(length, inputs, attn_qkv, attn_out, gains, shifts, biases):
    tokens, width = inputs.shape
    group = min(256, width)
    full = pl.BlockSpec((tokens, width), lambda g, n: (0, 0))
    part = pl.BlockSpec((tokens, group), lambda g, n: (0, g))
    low = jax.ShapeDtypeStruct((tokens, width), LOW)
    return pl.pallas_call(
        attention_kernel,
        grid_spec=pltpu.PrefetchScalarGridSpec(
            num_scalar_prefetch=1,
            grid=(width // group,),
            in_specs=[
                full,
                pl.BlockSpec((3, width, group), lambda g, n: (0, 0, g)),
                pl.BlockSpec((group, width), lambda g, n: (g, 0)),
                pl.BlockSpec(gains.shape, lambda g, n: (0, 0)),
                pl.BlockSpec(shifts.shape, lambda g, n: (0, 0)),
                pl.BlockSpec(biases.shape, lambda g, n: (0, 0)),
                pl.BlockSpec((biases.shape[0], group), lambda g, n: (0, g)),
            ],
            out_specs=[part, part, part, part, full, full, full],
            scratch_shapes=[pltpu.VMEM((tokens, width), LOW), pltpu.VMEM((tokens, width), WIDE)],
        ),
        out_shape=[low, low, low, low, low, jax.ShapeDtypeStruct((tokens, width), WIDE), low],
        cost_estimate=cost(9),
        name="attention_block",
    )(length, inputs, attn_qkv, attn_out, gains, shifts, biases, biases)


def feed_forward_kernel(
    second_ref, up_ref, down_ref, up_bias_ref, first_ref, gains_ref, shifts_ref, biases_ref,
    act_ref, sum_ref, hidden_ref, acc_scr
):
    step = pl.program_id(0)

    @pl.when(step == 0)
    def _():
        acc_scr[...] = first_ref[...] + biases_ref[3:4]

    pre_act = product(second_ref[...], up_ref[...]) + up_bias_ref[...]
    act = jnp.maximum(pre_act, 0.0).astype(LOW)
    act_ref[...] = act
    acc_scr[...] += product(act, down_ref[...])

    @pl.when(step == pl.num_programs(0) - 1)
    def _():
        total = acc_scr[...]
        sum_ref[...] = total
        hidden_ref[...] = norm_forward(total, gains_ref[2:3], shifts_ref[2:3])[0].astype(LOW)


def feed_forward(second_low, ffn_up, ffn_down, up_bias, first_sum, gains, shifts, biases):
    tokens, width = second_low.shape
    inner = ffn_up.shape[1]
    block = min(1024, inner)
    full = pl.BlockSpec((tokens, width), lambda g: (0, 0))
    return pl.pallas_call(
        feed_forward_kernel,
        grid=(inner // block,),
        in_specs=[
            full,
            pl.BlockSpec((width, block), lambda g: (0, g)),
            pl.BlockSpec((block, width), lambda g: (g, 0)),
            pl.BlockSpec((1, block), lambda g: (0, g)),
            full,
            pl.BlockSpec(gains.shape, lambda g: (0, 0)),
            pl.BlockSpec(shifts.shape, lambda g: (0, 0)),
            pl.BlockSpec(biases.shape, lambda g: (0, 0)),
        ],
        out_specs=[pl.BlockSpec((tokens, block), lambda g: (0, g)), full, full],
        out_shape=[
            jax.ShapeDtypeStruct((tokens, inner), LOW),
            jax.ShapeDtypeStruct((tokens, width), WIDE),
            jax.ShapeDtypeStruct((tokens, width), LOW),
        ],
        scratch_shapes=[pltpu.VMEM((tokens, width), WIDE)],
        cost_estimate=cost(9),
        name="feed_forward",
    )(second_low, ffn_up, ffn_down, up_bias.reshape(1, inner), first_sum, gains, shifts, biases)


def norm_stats(values):
    centred = values - jnp.mean(values, axis=-1, keepdims=True)
    inverse = lax.rsqrt(jnp.mean(centred * centred, axis=-1, keepdims=True) + EPS)
    return centred * inverse, inverse


def feed_back_kernel(
    down_in_ref, act_ref, up_ref, down_ref, grad_ref, first_ref, gains_ref,
    parts_ref, first_grad_ref, attn_in_ref, up_bias_ref, sums_ref, acc_scr, down_t_scr
):
    step = pl.program_id(0)

    @pl.when(step == 0)
    def _():
        acc_scr[...] = jnp.zeros_like(acc_scr)
        down_t_scr[...] = down_in_ref[...].T

    act_grad = product(down_ref[...], down_t_scr[...]).T
    pre_grad = jnp.where(act_ref[...].astype(WIDE) > 0, act_grad, 0.0).astype(LOW)
    parts = parts_ref.shape[0]
    per_part = pl.num_programs(0) // parts
    block = pre_grad.shape[1]
    column = pl.multiple_of((step % per_part) * block, block)
    parts_ref[step // per_part, :, pl.ds(column, block)] = pre_grad
    up_bias_ref[...] = jnp.sum(pre_grad.astype(WIDE), axis=0, keepdims=True)
    acc_scr[...] += product(up_ref[...], pre_grad.T)

    @pl.when(step == pl.num_programs(0) - 1)
    def _():
        unit_rows, inverse = norm_stats(first_ref[...])
        back, gain, shift = norm_backward(acc_scr[...].T, unit_rows, inverse, gains_ref[1:2])
        first_grad = grad_ref[...] + back
        attn_in = first_grad.astype(LOW)
        first_grad_ref[...] = first_grad
        attn_in_ref[...] = attn_in
        part = attn_in.shape[1] // parts
        for k in range(parts):
            parts_ref[k, :, per_part * block :] = attn_in[:, k * part : (k + 1) * part]
        sums_ref[0:1] = gain
        sums_ref[1:2] = shift
        sums_ref[2:3] = jnp.sum(attn_in.astype(WIDE), axis=0, keepdims=True)


def feed_back(down_in, act_low, ffn_up, ffn_down, second_grad, first_sum, gains, parts):
    tokens, width = down_in.shape
    inner = ffn_up.shape[1]
    block = min(1024, inner // parts)
    full = pl.BlockSpec((tokens, width), lambda g: (0, 0))
    return pl.pallas_call(
        feed_back_kernel,
        grid=(inner // block,),
        in_specs=[
            full,
            pl.BlockSpec((tokens, block), lambda g: (0, g)),
            pl.BlockSpec((width, block), lambda g: (0, g)),
            pl.BlockSpec((block, width), lambda g: (g, 0)),
            full,
            full,
            pl.BlockSpec(gains.shape, lambda g: (0, 0)),
        ],
        out_specs=[
            pl.BlockSpec((parts, tokens, (inner + width) // parts), lambda g: (0, 0, 0)),
            full,
            full,
            pl.BlockSpec((1, block), lambda g: (0, g)),
            pl.BlockSpec((8, width), lambda g: (0, 0)),
        ],
        out_shape=[
            jax.ShapeDtypeStruct((parts, tokens, (inner + width) // parts), LOW),
            jax.ShapeDtypeStruct((tokens, width), WIDE),
            jax.ShapeDtypeStruct((tokens, width), LOW),
            jax.ShapeDtypeStruct((1, inner), WIDE),
            jax.ShapeDtypeStruct((8, width), WIDE),
        ],
        scratch_shapes=[pltpu.VMEM((width, tokens), WIDE), pltpu.VMEM((width, tokens), LOW)],
        cost_estimate=cost(9),
        name="feed_back",
    )(down_in, act_low, ffn_up, ffn_down, second_grad, first_sum, gains)


def attention_back_kernel(
    length_ref, attn_in_ref, out_w_ref, query_ref, key_ref, value_ref, parts_ref, sums_ref,
    attn_t_scr
):
    tokens = attn_in_ref.shape[0]
    width = query_ref.shape[1]

    @pl.when(pl.program_id(0) == 0)
    def _():
        attn_t_scr[...] = attn_in_ref[...].T

    mixed_grad = product(out_w_ref[...], attn_t_scr[...]).T.astype(LOW)
    allowed = seen_keys(tokens, length_ref[0])
    masks = head_masks(128)
    zero = jnp.zeros((tokens, 128), LOW)
    for pair in range(width // 128):
        cols = slice(pair * 128, (pair + 1) * 128)
        q_pair, k_pair, v_pair = query_ref[:, cols], key_ref[:, cols], value_ref[:, cols]
        m_pair = mixed_grad[:, cols]
        totals = [jnp.zeros((tokens, 128), WIDE) for _ in range(3)]
        for mask in masks:
            k_one = jnp.where(mask, k_pair, zero)
            probs = masked_softmax(product_nt(q_pair, k_one), allowed)
            prob_grad = product_nt(m_pair, jnp.where(mask, v_pair, zero))
            delta = jnp.sum(probs * prob_grad, axis=-1, keepdims=True)
            score_grad = (probs * (prob_grad - delta)).astype(LOW)
            totals[0] += product(score_grad, k_one)
            totals[1] += product_tn(score_grad, jnp.where(mask, q_pair, zero))
            totals[2] += product_tn(probs.astype(LOW), jnp.where(mask, m_pair, zero))
        for kind, total in enumerate(totals):
            scale = HD ** (-0.5) if kind < 2 else 1.0
            grad = (total * scale).astype(LOW)
            parts_ref[:, kind * width + pair * 128 : kind * width + (pair + 1) * 128] = grad
            if kind != 1:
                sums_ref[kind : kind + 1, cols] = jnp.sum(
                    grad.astype(WIDE), axis=0, keepdims=True
                )


def attention_back(length, attn_in, attn_out, query, key, value, parts):
    tokens, width = attn_in.shape
    group = width // parts
    part = pl.BlockSpec((tokens, group), lambda g, n: (0, g))
    return pl.pallas_call(
        attention_back_kernel,
        grid_spec=pltpu.PrefetchScalarGridSpec(
            num_scalar_prefetch=1,
            grid=(parts,),
            in_specs=[
                pl.BlockSpec((tokens, width), lambda g, n: (0, 0)),
                pl.BlockSpec((group, width), lambda g, n: (g, 0)),
                part,
                part,
                part,
            ],
            out_specs=[
                pl.BlockSpec((None, tokens, 3 * group), lambda g, n: (g, 0, 0)),
                pl.BlockSpec((8, group), lambda g, n: (0, g)),
            ],
            scratch_shapes=[pltpu.VMEM((width, tokens), LOW)],
        ),
        out_shape=[
            jax.ShapeDtypeStruct((parts, tokens, 3 * group), LOW),
            jax.ShapeDtypeStruct((8, width), WIDE),
        ],
        cost_estimate=cost(9),
        name="attention_back",
    )(length, attn_in, attn_out, query, key, value)


def to_columns(rows):
    short = 128 - rows.shape[0]
    padded = jnp.concatenate([rows, jnp.zeros((short, rows.shape[1]), rows.dtype)], axis=0)
    return padded.T


def word_columns(words_ref):
    columns = [to_columns(words_ref[k])[:, 0:1] for k in range(words_ref.shape[0])]
    return jnp.concatenate(columns, axis=0).astype(jnp.int32)


def is_word(logits, where_col, first_col=0):
    return lax.broadcasted_iota(jnp.int32, logits.shape, 1) == where_col - first_col


def stats_kernel(
    base_ref, rows_ref, words_ref, keys_ref, norms_ref, slots_ref, head_ref, first_ref,
    second_ref, proj_one_ref, proj_two_ref, stats_ref, ones_ref, twos_ref
):
    rows = rows_ref[...]
    pair = words_ref.shape[0]
    tokens = words_ref.shape[2]
    words = word_columns(words_ref)
    ones = product(rows, proj_one_ref[...]).astype(LOW)
    twos = product(rows, proj_two_ref[...]).astype(LOW)
    ones_ref[...] = ones
    twos_ref[...] = twos
    picked = jnp.zeros((rows.shape[0], 1), WIDE)
    sums = []
    for place, (left, words_w) in enumerate(
        ((rows, head_ref), (ones, first_ref), (twos, second_ref))
    ):
        columns = words_w.shape[1]
        tile = SECOND_TILE if columns % SECOND_TILE == 0 else columns
        total = jnp.zeros((rows.shape[0], tile), WIDE)
        chosen = jnp.zeros((rows.shape[0], tile), WIDE)
        where_col = words - base_ref[place]
        for start in range(0, columns, tile):
            logits = product(left, words_w[:, start : start + tile])
            total = total + jnp.exp(logits)
            chosen = chosen + jnp.where(is_word(logits, where_col, start), logits, 0.0)
        sums.append(jnp.sum(total, axis=1, keepdims=True))
        picked = picked + jnp.sum(chosen, axis=1, keepdims=True)
    sums.append(picked)
    lanes = lax.broadcasted_iota(jnp.int32, (rows.shape[0], 128), 1)
    table = jnp.zeros((rows.shape[0], 128), WIDE)
    for place, column in enumerate(sums):
        table = jnp.where(lanes == place, column, table)
    slot_count = slots_ref.shape[1]
    scale = 1.0 / math.sqrt(rows.shape[1])
    for k in range(pair):
        keys = keys_ref[k]
        norms = norms_ref[k][:, 0:1]
        scored = product_nt(keys, rows[k * tokens : (k + 1) * tokens]) * scale
        scored = scored - norms * (0.5 * scale)
        ids = lax.broadcasted_iota(jnp.int32, scored.shape, 0)
        for m in range(slot_count):
            hit = ids == slots_ref[k, m : m + 1, :]
            stats_ref[k, m : m + 1, :] = jnp.sum(
                jnp.where(hit, scored, 0.0), axis=0, keepdims=True
            )
        stats_ref[k, slot_count : slot_count + 8, :] = table[k * tokens : (k + 1) * tokens].T[0:8]


def whole_spec(array):
    return pl.BlockSpec(array.shape, lambda *_: (0,) * array.ndim)


def word_stats(base, rows_all, words_f, key_block, norms, slots_t, weights, pair):
    sources, slot_count, tokens = slots_t.shape
    count = key_block.shape[1]
    width = rows_all.shape[1]
    chunk = pair * tokens
    ones = weights[3].shape[1]
    twos = weights[4].shape[1]
    return pl.pallas_call(
        stats_kernel,
        grid_spec=pltpu.PrefetchScalarGridSpec(
            num_scalar_prefetch=1,
            grid=(sources // pair,),
            in_specs=[
                pl.BlockSpec((chunk, width), lambda g, b: (g, 0)),
                pl.BlockSpec((pair, 1, tokens), lambda g, b: (g, 0, 0)),
                pl.BlockSpec((pair, count, width), lambda g, b: (g, 0, 0)),
                pl.BlockSpec((pair, count, 128), lambda g, b: (g, 0, 0)),
                pl.BlockSpec((pair, slot_count, tokens), lambda g, b: (g, 0, 0)),
            ]
            + [whole_spec(w) for w in weights],
            out_specs=[
                pl.BlockSpec((pair, slot_count + 8, tokens), lambda g, b: (g, 0, 0)),
                pl.BlockSpec((chunk, ones), lambda g, b: (g, 0)),
                pl.BlockSpec((chunk, twos), lambda g, b: (g, 0)),
            ],
        ),
        out_shape=[
            jax.ShapeDtypeStruct((sources, slot_count + 8, tokens), WIDE),
            jax.ShapeDtypeStruct((rows_all.shape[0], ones), LOW),
            jax.ShapeDtypeStruct((rows_all.shape[0], twos), LOW),
        ],
        cost_estimate=cost(13),
        name="word_stats",
    )(base, rows_all, words_f, key_block, norms, slots_t, *weights)


def word_grads_kernel(
    order_ref, base_ref, rows_ref, ones_ref, twos_ref, returned_ref, words_ref, keys_ref,
    slots_ref, head_ref, first_ref, second_ref, head_t_ref, first_t_ref, second_t_ref,
    proj_one_ref, proj_two_ref, *refs
):
    mine_ref, other_ref, head_g_ref, first_g_ref, second_g_ref, back_ref, terms_scr = refs[-7:]
    rows = rows_ref[...]
    pair = words_ref.shape[0]
    tokens = words_ref.shape[2]
    slot_count = slots_ref.shape[1]
    words = word_columns(words_ref)
    coefs = [to_columns(returned_ref[k, slot_count : slot_count + 8, :]) for k in range(pair)]
    coefs = jnp.concatenate(coefs, axis=0)
    weight = coefs[:, 0:1]
    in_first = (words >= base_ref[3]) & (words < base_ref[4])
    in_second = words >= base_ref[4]
    scales = (
        weight,
        jnp.where(in_first, weight, 0.0),
        jnp.where(in_second, weight, 0.0),
    )
    lefts = (rows, ones_ref[...], twos_ref[...])
    term = None
    back_start = 0
    for place, (words_w, words_t, out_ref, proj_ref) in enumerate(
        (
            (head_ref, head_t_ref, head_g_ref, None),
            (first_ref, first_t_ref, first_g_ref, proj_one_ref),
            (second_ref, second_t_ref, second_g_ref, proj_two_ref),
        )
    ):
        columns = words_w.shape[1]
        tile = SECOND_TILE if columns % SECOND_TILE == 0 else columns
        where_col = words - base_ref[place]
        scale = scales[place]
        log_sum = coefs[:, place + 1 : place + 2]
        back = None
        for start in range(0, columns, tile):
            tile_w = words_w[:, start : start + tile]
            logits = product(lefts[place], tile_w)
            hit = is_word(logits, where_col, start)
            grad = scale * jnp.exp(logits - log_sum) - jnp.where(hit, scale, 0.0)
            grad = grad.astype(LOW)
            out_ref[:, start : start + tile] = grad
            part = product(grad, words_t[start : start + tile, :])
            back = part if back is None else back + part
        if proj_ref is None:
            term = back
        else:
            back = back.astype(LOW)
            back_ref[:, back_start : back_start + back.shape[1]] = back
            back_start += back.shape[1]
            term = term + product(back, proj_ref[...])
    key_scale = 1.0 / math.sqrt(rows.shape[1])
    count = keys_ref.shape[1]
    ids = lax.broadcasted_iota(jnp.int32, (count, tokens), 0)
    for k in range(pair):
        dense = jnp.zeros((count, tokens), WIDE)
        for m in range(slot_count):
            hit = ids == slots_ref[k, m : m + 1, :]
            dense = jnp.where(hit, returned_ref[k, m : m + 1, :], dense)
        near = product_tn(dense.astype(LOW), keys_ref[k]) * key_scale
        terms_scr[k] = (term[k * tokens : (k + 1) * tokens] + near).astype(LOW)
    if pair == 2:
        core = base_ref[5]
        mine_ref[0] = terms_scr[core]
        other_ref[0] = terms_scr[1 - core]
    else:
        mine_ref[0] = terms_scr[0]
        other_ref[0] = terms_scr[0]


def word_grads(order, base, rows_all, ones_all, twos_all, returned, words_f, key_block, slots_t,
               weights, pair, earlier=None):
    sources, slot_count, tokens = slots_t.shape
    count = key_block.shape[1]
    width = rows_all.shape[1]
    chunk = pair * tokens
    total = rows_all.shape[0]
    steps = order.shape[0]
    sizes = [weights[k].shape[1] for k in range(3)] + [weights[6].shape[0] + weights[7].shape[0]]

    def by_row(columns):
        return pl.BlockSpec((chunk, columns), lambda g, o, b: (o[g], 0))

    kept = [] if earlier is None else list(earlier)
    inputs = [rows_all, ones_all, twos_all, returned, words_f, key_block, slots_t, *weights, *kept]
    n_plain = len(inputs) - len(kept) + 2
    return pl.pallas_call(
        word_grads_kernel,
        grid_spec=pltpu.PrefetchScalarGridSpec(
            num_scalar_prefetch=2,
            grid=(steps,),
            in_specs=[
                by_row(width),
                by_row(ones_all.shape[1]),
                by_row(twos_all.shape[1]),
                pl.BlockSpec((pair, slot_count + 8, tokens), lambda g, o, b: (o[g], 0, 0)),
                pl.BlockSpec((pair, 1, tokens), lambda g, o, b: (o[g], 0, 0)),
                pl.BlockSpec((pair, count, width), lambda g, o, b: (o[g], 0, 0)),
                pl.BlockSpec((pair, slot_count, tokens), lambda g, o, b: (o[g], 0, 0)),
            ]
            + [whole_spec(w) for w in weights]
            + [pl.BlockSpec(memory_space=pl.ANY) for _ in kept],
            out_specs=[
                pl.BlockSpec((1, tokens, width), lambda g, o, b: (g, 0, 0)),
                pl.BlockSpec((1, tokens, width), lambda g, o, b: (g, 0, 0)),
            ]
            + [by_row(size) for size in sizes],
            scratch_shapes=[pltpu.VMEM((pair, tokens, width), LOW)],
        ),
        out_shape=[
            jax.ShapeDtypeStruct((steps, tokens, width), LOW),
            jax.ShapeDtypeStruct((steps, tokens, width), LOW),
        ]
        + [jax.ShapeDtypeStruct((total, size), LOW) for size in sizes],
        input_output_aliases={n_plain + k: 2 + k for k in range(len(kept))},
        cost_estimate=cost(10),
        name="word_grads",
    )(order, base, *inputs)


def word_sums_kernel(
    rows_ref, ones_ref, twos_ref, head_g_ref, first_g_ref, second_g_ref, back_ref,
    packed_ref, proj_ref, *scratch
):
    step = pl.program_id(0)
    pairs = (
        (head_g_ref, rows_ref),
        (ones_ref, first_g_ref),
        (twos_ref, second_g_ref),
        (rows_ref, back_ref),
    )
    for (left, right), acc in zip(pairs, scratch):
        part = product_tn(left[...], right[...])

        @pl.when(step == 0)
        def _():
            acc[...] = part

        @pl.when(step > 0)
        def _():
            acc[...] += part

    @pl.when(step == pl.num_programs(0) - 1)
    def _():
        proj_ref[...] = scratch[3][...].astype(LOW)
        place = 0
        for acc in scratch[:3]:
            rows, columns = acc.shape
            for start in range(0, columns, 128):
                packed_ref[place : place + rows, :] = acc[:, start : start + 128].astype(LOW)
                place += rows


def word_sums(rows_all, ones_all, twos_all, grads):
    total = rows_all.shape[0]
    chunk = min(512, total)
    inputs = [rows_all, ones_all, twos_all, *grads]
    shapes = [
        (grads[0].shape[1], rows_all.shape[1]),
        (ones_all.shape[1], grads[1].shape[1]),
        (twos_all.shape[1], grads[2].shape[1]),
        (rows_all.shape[1], grads[3].shape[1]),
    ]
    packed_rows = sum(rows * columns for rows, columns in shapes[:3]) // 128
    out_shapes = [(packed_rows, 128), shapes[3]]
    packed, proj = pl.pallas_call(
        word_sums_kernel,
        grid=(total // chunk,),
        in_specs=[pl.BlockSpec((chunk, item.shape[1]), lambda g: (g, 0)) for item in inputs],
        out_specs=[pl.BlockSpec(shape, lambda g: (0, 0)) for shape in out_shapes],
        out_shape=[jax.ShapeDtypeStruct(shape, LOW) for shape in out_shapes],
        scratch_shapes=[pltpu.VMEM(shape, WIDE) for shape in shapes],
        cost_estimate=cost(10),
        name="word_sums",
    )(*inputs)
    return packed, proj, shapes[:3]


def unpack_kernel(me_ref, parts_ref, *outs):
    count, part_rows, _ = parts_ref.shape
    me = me_ref[0]
    place = 0
    for out in outs:
        rows, columns = out.shape
        for start in range(0, columns, 128):
            done = 0
            while done < rows:
                part, offset = divmod(place + done, part_rows)
                size = min(rows - done, part_rows - offset)
                out[done : done + size, start : start + 128] = parts_ref[
                    part ^ me, offset : offset + size, :
                ].astype(WIDE)
                done += size
            place += rows


def unpack_words(parts, shapes):
    return pl.pallas_call(
        unpack_kernel,
        grid_spec=pltpu.PrefetchScalarGridSpec(
            num_scalar_prefetch=1,
            grid=(1,),
            in_specs=[whole_spec(parts)],
            out_specs=[pl.BlockSpec(shape, lambda *_: (0, 0)) for shape in shapes],
        ),
        out_shape=[jax.ShapeDtypeStruct(shape, WIDE) for shape in shapes],
        cost_estimate=cost(3),
        name="unpack_words",
    )(lax.axis_index("dp").astype(jnp.int32).reshape(1), parts)


def key_norms_kernel(keys_ref, norms_ref):
    for k in range(keys_ref.shape[0]):
        wide = keys_ref[k].astype(WIDE)
        norms = jnp.sum(wide * wide, axis=1, keepdims=True)
        norms_ref[k] = jnp.broadcast_to(norms, norms_ref.shape[1:])


def key_norms(key_block):
    sources, count, width = key_block.shape
    pair = min(2, sources)
    return pl.pallas_call(
        key_norms_kernel,
        grid=(sources // pair,),
        in_specs=[pl.BlockSpec((pair, count, width), lambda g: (g, 0, 0))],
        out_specs=pl.BlockSpec((pair, count, 128), lambda g: (g, 0, 0)),
        out_shape=jax.ShapeDtypeStruct((sources, count, 128), WIDE),
        cost_estimate=cost(20),
        name="key_norms",
    )(key_block)


def input_back_kernel(
    parts_ref, qkv_ref, in_ref, grad_ref, gains_ref, input_grad_ref, sums_ref, acc_scr
):
    step = pl.program_id(0)

    @pl.when(step == 0)
    def _():
        acc_scr[...] = jnp.zeros_like(acc_scr)

    group = qkv_ref.shape[2]
    total = acc_scr[...]
    for kind in range(3):
        total = total + product(
            qkv_ref[kind], parts_ref[:, kind * group : (kind + 1) * group].T
        )
    acc_scr[...] = total

    @pl.when(step == pl.num_programs(0) - 1)
    def _():
        unit_rows, inverse = norm_stats(in_ref[...].astype(WIDE))
        back, gain, shift = norm_backward(acc_scr[...].T, unit_rows, inverse, gains_ref[0:1])
        input_grad_ref[...] = grad_ref[...] + back
        sums_ref[0:1] = gain
        sums_ref[1:2] = shift


def input_back(parts, attn_qkv, inputs, first_grad, gains):
    count, tokens, _ = parts.shape
    width = inputs.shape[1]
    group = width // count
    full = pl.BlockSpec((tokens, width), lambda g: (0, 0))
    return pl.pallas_call(
        input_back_kernel,
        grid=(count,),
        in_specs=[
            pl.BlockSpec((None, tokens, 3 * group), lambda g: (g, 0, 0)),
            pl.BlockSpec((3, width, group), lambda g: (0, 0, g)),
            full,
            full,
            pl.BlockSpec(gains.shape, lambda g: (0, 0)),
        ],
        out_specs=[full, pl.BlockSpec((8, width), lambda g: (0, 0))],
        out_shape=[
            jax.ShapeDtypeStruct((tokens, width), WIDE),
            jax.ShapeDtypeStruct((8, width), WIDE),
        ],
        scratch_shapes=[pltpu.VMEM((width, tokens), WIDE)],
        cost_estimate=cost(7),
        name="input_back",
    )(parts, attn_qkv, inputs, first_grad, gains)


def shards(
    inputs,
    lengths,
    targets,
    attn_qkv,
    attn_out,
    ffn_up,
    ffn_down,
    norm_gains,
    norm_shifts,
    biases,
    up_bias,
    cluster_proj,
    proj_first,
    proj_second,
    head_words,
    tail_first,
    tail_second,
    store_keys,
    block_rows,
    near_slots,
    near_words,
):
    tokens_here = inputs.shape[0]
    d_model = inputs.shape[1]
    dp_count = lax.axis_size("dp")
    sources = lax.axis_size("line") * 2
    my_index = lax.axis_index("line") * 2 + lax.axis_index("core")
    group_rows = tokens_here * sources
    head_cols = head_words.shape[1]
    first_cols = tail_first.shape[1]
    second_cols = tail_second.shape[1]
    head_total = head_cols * sources
    first_total = first_cols * sources
    ff_width = ffn_up.shape[1]
    valid_mask = (jnp.arange(tokens_here) < lengths[0]).astype(WIDE)

    query_low, key_low, value_low, mixed_low, normed_low, first_sum, second_low = attention_block(
        lengths, inputs, attn_qkv, attn_out, norm_gains, norm_shifts, biases
    )
    act_low, second_sum, hidden_low = feed_forward(
        second_low, ffn_up, ffn_down, up_bias, first_sum, norm_gains, norm_shifts, biases
    )
    cluster_logits = lax.dot_general(
        cluster_proj, hidden_low, (((0,), (1,)), ((), ())), preferred_element_type=WIDE
    )

    rows_all = lax.all_gather(hidden_low, STORE, axis=0, tiled=True)

    key_block = jnp.take(store_keys, block_rows[0, 0].reshape(-1), axis=0, mode="clip")
    key_block = key_block.reshape(sources, -1, d_model)
    slots_t = near_slots[0, 0].transpose(1, 2, 0)
    slot_count = slots_t.shape[1]
    words_t = near_words.T

    weights = (head_words, tail_first, tail_second, proj_first, proj_second)
    back_weights = weights[:3] + tuple(w.T for w in weights)
    norms = key_norms(key_block)

    left_low = jnp.concatenate([act_low, second_low, mixed_low, normed_low], axis=1)
    left_low, rows_all, norms, slots_t, words_t, back_weights = lax.optimization_barrier(
        (left_low, rows_all, norms, slots_t, words_t, back_weights)
    )
    left_all = lax.all_gather(left_low, "dp", axis=0, tiled=True)

    core = lax.axis_index("core")
    words_f = targets.astype(WIDE).reshape(sources, 1, tokens_here)
    base = jnp.stack(
        [
            my_index * head_cols,
            head_total + my_index * first_cols,
            head_total + first_total + my_index * second_cols,
            jnp.int32(head_total),
            jnp.int32(head_total + first_total),
            core,
        ]
    ).astype(jnp.int32)
    outgoing, ones_all, twos_all = word_stats(
        base, rows_all, words_f, key_block, norms, slots_t, back_weights[:3] + weights[3:], 2
    )
    incoming = lax.all_to_all(outgoing, STORE, 0, 0)

    near_scores = incoming[:, :slot_count].reshape(sources * slot_count, tokens_here)
    own_stats = jnp.sum(incoming[:, slot_count : slot_count + 4], axis=0)
    own_words = lax.dynamic_slice_in_dim(targets, my_index * tokens_here, tokens_here, 0)
    in_first = ((own_words >= head_total) & (own_words < head_total + first_total)).astype(WIDE)
    in_second = (own_words >= head_total + first_total).astype(WIDE)
    head_sum = own_stats[0] + jnp.sum(jnp.exp(cluster_logits), axis=0)
    log_head = jnp.log(head_sum)
    log_first = jnp.log(own_stats[1])
    log_second = jnp.log(own_stats[2])
    log_model = (
        own_stats[3]
        - log_head
        + in_first * (cluster_logits[0] - log_first)
        + in_second * (cluster_logits[1] - log_second)
    )
    near_top = jnp.max(near_scores, axis=0, keepdims=True)
    near_exp = jnp.exp(near_scores - near_top)
    near_probs = near_exp / jnp.sum(near_exp, axis=0, keepdims=True)
    matched = (words_t == own_words[None, :]).astype(WIDE)
    near_mass = jnp.sum(near_probs * matched, axis=0)
    model_prob = jnp.exp(log_model)
    mixture = NEAR_WEIGHT * near_mass + (1.0 - NEAR_WEIGHT) * model_prob
    token_loss = -valid_mask * jnp.log(mixture)
    model_weight = valid_mask * (1.0 - NEAR_WEIGHT) * model_prob / mixture
    near_weight = valid_mask * NEAR_WEIGHT / mixture
    score_grad = -near_weight[None, :] * near_probs * (matched - near_mass[None, :])
    coef = jnp.stack([model_weight, log_head, log_first, log_second] + 4 * [model_weight])
    returning = jnp.concatenate(
        [
            score_grad.reshape(sources, slot_count, tokens_here),
            jnp.broadcast_to(coef[None], (sources,) + coef.shape),
        ],
        axis=1,
    )
    returned = lax.all_to_all(returning, STORE, 0, 0)

    lines = lax.axis_size("line")
    line = lax.axis_index("line")

    def owner_grads(order, earlier=None):
        mine, other, *grads = word_grads(
            jnp.stack(order).astype(jnp.int32),
            base,
            rows_all,
            ones_all,
            twos_all,
            returned,
            words_f,
            key_block,
            slots_t,
            back_weights,
            2,
            earlier,
        )
        return mine.astype(WIDE) + swap_partner(other, "core", 1).astype(WIDE), grads

    if lines == 4:
        far, far_grads = owner_grads([line ^ 2, line ^ 3])
        far = far.astype(LOW)
        zero = jnp.zeros_like(far[0])
        far_parts = jnp.stack(
            [
                jnp.where(line == (k ^ 2), far[0], jnp.where(line == (k ^ 3), far[1], zero))
                for k in range(lines)
            ]
        )
        from_far = jnp.sum(lax.all_to_all(far_parts, "line", 0, 0).astype(WIDE), axis=0)
        far_grads, far = lax.optimization_barrier((far_grads, far))
        near, word_terms = owner_grads([line ^ 1, line], far_grads)
        near_low = near[0].astype(LOW)
        from_one = swap_partner(near_low, "line", 1)
        word_terms, near_low = lax.optimization_barrier((word_terms, near_low))
        row_back = near[1] + from_one.astype(WIDE) + from_far
    else:
        terms, word_terms = owner_grads(list(range(lines)))
        row_back = lax.psum_scatter(terms.astype(LOW), "line", scatter_dimension=0).astype(WIDE)
    word_packed, proj_acc, word_shapes = word_sums(rows_all, ones_all, twos_all, word_terms)

    own_rows = d_model // sources
    proj_width = proj_acc.shape[1]
    sub_rows = own_rows // dp_count
    proj_parts = proj_acc.reshape(sources, dp_count, sub_rows, proj_width).transpose(1, 0, 2, 3)
    dp_index = lax.axis_index("dp")
    proj_sum = lax.dynamic_index_in_dim(proj_parts, dp_index, 0, keepdims=False).astype(WIDE)
    for q in range(1, dp_count):
        part = lax.dynamic_index_in_dim(proj_parts, dp_index ^ q, 0, keepdims=False)
        proj_sum = proj_sum + swap_partner(part, "dp", q).astype(WIDE)
    cluster_rows = model_weight[None, :] * (
        jnp.exp(cluster_logits - log_head[None, :]) - jnp.stack([in_first, in_second])
    )
    hidden_grad = row_back + lax.dot_general(
        cluster_rows, cluster_proj.astype(WIDE), (((0,), (1,)), ((), ())), precision=HIGH
    )
    cluster_acc = jnp.dot(cluster_rows, hidden_low.astype(WIDE), precision=HIGH)
    unit_three, inv_three = norm_stats(second_sum)
    second_grad, gain_three, shift_three = norm_backward(
        hidden_grad, unit_three, inv_three, norm_gains[2]
    )
    down_in = second_grad.astype(LOW)
    down_parts = exchange_columns(down_in)
    bias_down = jnp.sum(down_in.astype(WIDE), axis=0, keepdims=True)
    act_grad = product_nt(down_in, ffn_down)
    pre_grad = jnp.where(act_low.astype(WIDE) > 0, act_grad, 0.0).astype(LOW)
    up_bias_acc = jnp.sum(pre_grad.astype(WIDE), axis=0, keepdims=True)
    marks = [0, ff_width, ff_width + d_model, ff_width + 2 * d_model, ff_width + 3 * d_model]
    lefts = [left_all[:, a:b] for a, b in zip(marks[:-1], marks[1:])]
    down = Halving(grad_tile(lefts[0], after(down_parts, pre_grad)))
    norm_two_grad = product_nt(after(pre_grad, down.outgoing), ffn_up)
    unit_two, inv_two = norm_stats(first_sum)
    back_second, gain_two, shift_two = norm_backward(
        norm_two_grad, unit_two, inv_two, norm_gains[1]
    )
    first_grad_sum = second_grad + back_second
    attn_in = first_grad_sum.astype(LOW)
    bias_attn = jnp.sum(attn_in.astype(WIDE), axis=0, keepdims=True)
    mark = down.add(attn_in)
    up_width = ff_width // dp_count
    head_width = d_model // dp_count
    up_send = jnp.stack(
        [
            jnp.concatenate(
                [
                    pre_grad[:, k * up_width : (k + 1) * up_width],
                    attn_in[:, k * head_width : (k + 1) * head_width],
                ],
                axis=1,
            )
            for k in range(dp_count)
        ]
    )
    up_parts = lax.all_to_all(up_send, "dp", 0, 0)
    stacked_parts, sums_three = attention_back(
        lengths, after(attn_in, up_send, mark), attn_out, query_low, key_low, value_low, dp_count
    )
    mark = down.add(stacked_parts)
    qkv_parts = lax.all_to_all(after(stacked_parts, up_parts), "dp", 0, 0)
    word_send = after(word_packed.reshape(dp_count, -1, 128), qkv_parts)
    word_parts = lax.all_to_all(word_send, "dp", 0, 0)
    word_own = jnp.sum(word_parts.astype(WIDE), axis=0).astype(LOW)
    proj_rows = sub_rows * proj_width // (up_width + head_width)
    proj_block = proj_sum.astype(LOW).reshape(sources, proj_rows, up_width + head_width)
    up_parts = after(up_parts, mark)
    up = Halving(
        jnp.concatenate(
            [
                jnp.concatenate(
                    [
                        grad_tile(lefts[1], up_parts[:, :, :up_width]),
                        grad_tile(lefts[2], up_parts[:, :, up_width:]),
                    ],
                    axis=2,
                ),
                proj_block,
            ],
            axis=1,
        )
    )
    input_grad, sums_one = input_back(
        after(stacked_parts, up.outgoing), attn_qkv, inputs, first_grad_sum, norm_gains
    )
    down_own = down.finish(input_grad)
    mark = up.add(input_grad, down_own)

    def by_store(value):
        rows = value.shape[0]
        return value.reshape(rows, sources, -1).transpose(1, 0, 2).reshape(sources, -1)

    small = jnp.concatenate(
        [
            by_store(jnp.concatenate([sums_one[0:1], gain_two, gain_three])),
            by_store(jnp.concatenate([sums_one[1:2], shift_two, shift_three])),
            by_store(jnp.concatenate([sums_three[0:1], sums_three[2:3], bias_attn, bias_down])),
            by_store(up_bias_acc),
            by_store(cluster_acc),
        ],
        axis=1,
    )
    small_count = small.shape[1]
    small_rows = -(-small_count // (3 * head_width))
    if own_rows % 128 == 0:
        small_rows = -(-small_rows // 8) * 8
    small = jnp.pad(small, ((0, 0), (0, small_rows * 3 * head_width - small_count)))
    small = small.reshape(sources, small_rows, 3 * head_width).astype(LOW)
    qkv = Halving(
        jnp.concatenate([grad_tile(lefts[3], after(qkv_parts, mark)), small], axis=1)
    )
    down_cols = down_own.shape[1]
    down_rows = down_own.shape[0]
    lane_blocks = [down_own[:, k : k + 128] for k in range(0, down_cols, 128)]
    down_pieces = gather_dp(jnp.concatenate(lane_blocks + [word_own], axis=0))
    mark = qkv.add(qkv.outgoing)
    mark = up.add(mark)
    mark = qkv.add(mark)
    down_pieces = after(down_pieces, mark)
    word_start = down_rows * len(lane_blocks)
    down_out = join_pieces(
        [
            jnp.concatenate(
                [piece[k : k + down_rows] for k in range(0, word_start, down_rows)], axis=1
            )
            for piece in down_pieces
        ],
        1,
        0,
        down_cols,
        1,
    )
    up_own = up.finish(down_out)
    up_pieces = gather_dp(up_own)
    word_pieces = after(down_pieces, up_own)
    head_t, first_out, second_out = unpack_words(
        jnp.stack([piece[word_start:] for piece in word_pieces]), word_shapes
    )
    head_out = head_t.T
    qkv_own = qkv.finish(head_t)
    qkv_pieces = gather_dp(qkv_own)
    up_pieces = after(up_pieces, qkv_own)
    up_main = [piece[:own_rows] for piece in up_pieces]
    up_out = join_pieces(up_main, 1, 0, up_width, 1)
    out_out = join_pieces(up_main, 1, up_width, head_width, 1)
    proj_out = join_pieces(
        [piece[own_rows:].reshape(sub_rows, proj_width) for piece in up_pieces],
        0,
        0,
        sub_rows,
        0,
    )
    qkv_main = [piece[:own_rows] for piece in qkv_pieces]
    qkv_out = jnp.stack(
        [join_pieces(qkv_main, 1, kind * head_width, head_width, 1) for kind in range(3)]
    )
    small_sum = sum(piece[own_rows:].astype(WIDE) for piece in qkv_pieces).reshape(-1)
    sizes = [3 * own_rows, 3 * own_rows, 4 * own_rows, ff_width // sources, 2 * own_rows]
    ends = [0]
    for size in sizes:
        ends.append(ends[-1] + size)
    gains_out, shifts_out, biases_out, upb_out, cluster_out = (
        small_sum[a:b] for a, b in zip(ends[:-1], ends[1:])
    )
    return (
        token_loss,
        input_grad,
        qkv_out,
        out_out,
        up_out,
        down_out,
        gains_out.reshape(3, own_rows),
        shifts_out.reshape(3, own_rows),
        biases_out.reshape(4, own_rows),
        upb_out,
        cluster_out.reshape(2, own_rows).T,
        proj_out[:, : proj_first.shape[1]],
        proj_out[:, proj_first.shape[1] :],
        head_out,
        first_out,
        second_out,
    )


def solution(mesh):
    dp_count = mesh.shape["dp"]
    store_count = mesh.shape["store"]
    split = Mesh(mesh.devices.reshape(dp_count, store_count // 2, 2), ("dp",) + STORE)
    everyone = ("dp",) + STORE
    return jax.shard_map(
        shards,
        mesh=split,
        in_specs=(
            P(everyone, None),
            P(everyone),
            P("dp"),
            P(),
            P(),
            P(),
            P(),
            P(),
            P(),
            P(),
            P(),
            P(),
            P(),
            P(),
            P(None, STORE),
            P(None, STORE),
            P(None, STORE),
            P(STORE, None),
            P("dp", STORE, None, None),
            P("dp", STORE, None, None, None),
            P(everyone, None),
        ),
        out_specs=(
            P(everyone),
            P(everyone, None),
            P(None, STORE, None),
            P(STORE, None),
            P(STORE, None),
            P(STORE, None),
            P(None, STORE),
            P(None, STORE),
            P(None, STORE),
            P(STORE),
            P(STORE, None),
            P(STORE, None),
            P(STORE, None),
            P(None, STORE),
            P(None, STORE),
            P(None, STORE),
        ),
        check_vma=False,
    )
```

```python
import math

import jax
import jax.numpy as jnp
from jax import lax
from jax.experimental import pallas as pl
from jax.experimental.pallas import tpu as pltpu
from jax.sharding import Mesh
from jax.sharding import PartitionSpec as P

HEADS = 16
HD = 64


EPS = 1e-05
NEAR_WEIGHT = 0.25
NEG_FILL = -1e30
HIGH = lax.Precision.HIGHEST
STORE = ("line", "core")
LOW = jnp.bfloat16
WIDE = jnp.float32
SECOND_TILE = 256


def product(left, right):
    return jnp.dot(left, right, preferred_element_type=WIDE)


def product_tn(left, right):
    return lax.dot_general(left, right, (((0,), (0,)), ((), ())), preferred_element_type=WIDE)


def product_nt(left, right):
    return lax.dot_general(left, right, (((1,), (1,)), ((), ())), preferred_element_type=WIDE)


def norm_forward(values, gain_row, shift_row):
    row_mean = jnp.mean(values, axis=-1, keepdims=True)
    centred = values - row_mean
    inverse = lax.rsqrt(jnp.mean(centred * centred, axis=-1, keepdims=True) + EPS)
    unit_rows = centred * inverse
    return (unit_rows * gain_row + shift_row, unit_rows, inverse)


def norm_backward(grad_out, unit_rows, inverse, gain_row):
    scaled = grad_out * gain_row
    grad_in = inverse * (
        scaled
        - jnp.mean(scaled, axis=-1, keepdims=True)
        - unit_rows * jnp.mean(scaled * unit_rows, axis=-1, keepdims=True)
    )
    return (grad_in, jnp.sum(grad_out * unit_rows, axis=0, keepdims=True), jnp.sum(grad_out, axis=0, keepdims=True))


def swap_partner(value, axis, bit):
    count = lax.axis_size(axis)
    return lax.ppermute(value, axis, [(k, k ^ bit) for k in range(count)])


def after(value, *others):
    return lax.optimization_barrier((value, *others))[0]


class Halving:
    def __init__(self, blocks):
        lines = lax.axis_size("line")
        line = lax.axis_index("line")
        self.rest = blocks.shape[1:]
        self.current = blocks.reshape((lines, 2) + self.rest)
        self.steps = [(lax.axis_index("core"), "core", 1)]
        bit = 1
        while bit < lines:
            self.steps.append(((line // bit) & 1, "line", bit))
            bit *= 2
        self.received = None
        self.send()

    def send(self):
        mine, axis, bit = self.steps.pop(0)
        value = self.current
        outgoing = lax.dynamic_index_in_dim(value, 1 - mine, 1, keepdims=False).astype(LOW)
        self.outgoing = outgoing
        self.current = lax.dynamic_index_in_dim(value, mine, 1, keepdims=False)
        self.received = swap_partner(outgoing, axis, bit)

    def add(self, *others):
        received = after(self.received, *others) if others else self.received
        self.current = self.current.astype(WIDE) + received.astype(WIDE)
        if self.steps:
            self.current = self.current.reshape((-1, 2) + self.rest)
            self.send()
        return self.outgoing

    def finish(self, *others):
        while self.steps:
            self.add(*others)
        self.add(*others)
        return self.current[0].astype(LOW)


def grad_tile(left, right_parts):
    blocks = lax.axis_size("line") * 2
    right = right_parts.reshape(left.shape[0], right_parts.shape[2])
    tile = product_tn(left, right).astype(LOW)
    return tile.reshape(blocks, -1, right.shape[1])


def gather_dp(own):
    count = lax.axis_size("dp")
    return [own] + [swap_partner(own, "dp", q) for q in range(1, count)]


def join_pieces(pieces, axis, start, width, join_axis):
    count = len(pieces)
    me = lax.axis_index("dp")
    pieces = [lax.slice_in_dim(piece, start, start + width, axis=axis) for piece in pieces]
    bit = 1
    while bit < count:
        is_set = (me // bit) & 1 == 1
        pieces = [jnp.where(is_set, pieces[k ^ bit], pieces[k]) for k in range(count)]
        bit *= 2
    return jnp.concatenate([piece.astype(WIDE) for piece in pieces], axis=join_axis)


def exchange_columns(value):
    count = lax.axis_size("dp")
    tokens, columns = value.shape
    parts = value.reshape(tokens, count, columns // count).transpose(1, 0, 2)
    return lax.all_to_all(parts, "dp", 0, 0)


def cost(micros):
    return pl.CostEstimate(flops=int(micros * 9e8), transcendentals=0, bytes_accessed=1 << 20)


def head_masks(width):
    lanes = lax.broadcasted_iota(jnp.int32, (1, width), 1)
    return [(lanes // HD) % 2 == half for half in range(2)]


def masked_softmax(scores, allowed):
    scores = jnp.where(allowed, scores * HD ** (-0.5), NEG_FILL)
    exps = jnp.exp(scores - jnp.max(scores, axis=-1, keepdims=True))
    return exps / jnp.sum(exps, axis=-1, keepdims=True)


def seen_keys(tokens, length):
    rows = lax.broadcasted_iota(jnp.int32, (tokens, tokens), 0)
    cols = lax.broadcasted_iota(jnp.int32, (tokens, tokens), 1)
    return (cols <= rows) & (cols < length)


def block_kernel(
    length_ref, in_ref, qkv_ref, out_w_ref, up_bias_ref, gains_ref, shifts_ref, biases_ref,
    group_bias_ref, up_hbm, down_hbm,
    query_ref, key_ref, value_ref, mixed_ref, normed_ref, first_ref, second_ref, act_ref, sum_ref,
    hidden_ref, acc_scr, up_scr, down_scr, sems
):
    step = pl.program_id(0)
    tokens, width = in_ref.shape
    group = query_ref.shape[1]
    groups = width // group
    blocks = up_scr.shape[0]
    block = up_scr.shape[2]

    def fetches(place):
        start = place * block
        return (
            pltpu.make_async_copy(
                up_hbm.at[:, pl.ds(start, block)], up_scr.at[place], sems.at[0, place]
            ),
            pltpu.make_async_copy(
                down_hbm.at[pl.ds(start, block), :], down_scr.at[place], sems.at[1, place]
            ),
        )

    @pl.when(step == 0)
    def _():
        for place in range(blocks):
            for fetch in fetches(place):
                fetch.start()
        block_in = in_ref[...].astype(WIDE)
        normed_ref[...] = norm_forward(block_in, gains_ref[0:1], shifts_ref[0:1])[0].astype(LOW)
        acc_scr[...] = block_in + biases_ref[2:3]

    @pl.when(step < groups)
    def _():
        normed = normed_ref[...]
        query = (product(normed, qkv_ref[0]) + group_bias_ref[0:1]).astype(LOW)
        key = product(normed, qkv_ref[1]).astype(LOW)
        value = (product(normed, qkv_ref[2]) + group_bias_ref[1:2]).astype(LOW)
        query_ref[...] = query
        key_ref[...] = key
        value_ref[...] = value
        allowed = seen_keys(tokens, length_ref[0])
        masks = head_masks(128)
        zero = jnp.zeros((tokens, 128), LOW)
        for pair in range(group // 128):
            cols = slice(pair * 128, (pair + 1) * 128)
            q_pair, k_pair, v_pair = query[:, cols], key[:, cols], value[:, cols]
            mixed = jnp.zeros((tokens, 128), WIDE)
            for mask in masks:
                probs = masked_softmax(product_nt(q_pair, jnp.where(mask, k_pair, zero)), allowed)
                mixed = mixed + product(probs.astype(LOW), jnp.where(mask, v_pair, zero))
            mixed_ref[:, cols] = mixed.astype(LOW)
        acc_scr[...] += product(mixed_ref[...], out_w_ref[...])

    @pl.when(step == groups - 1)
    def _():
        first_sum = acc_scr[...]
        first_ref[...] = first_sum
        second_ref[...] = norm_forward(first_sum, gains_ref[1:2], shifts_ref[1:2])[0].astype(LOW)
        acc_scr[...] = first_sum + biases_ref[3:4]

    @pl.when(step >= groups)
    def _():
        place = step - groups
        for fetch in fetches(place):
            fetch.wait()
        pre_act = product(second_ref[...], up_scr[place]) + up_bias_ref[...]
        act = jnp.maximum(pre_act, 0.0).astype(LOW)
        act_ref[...] = act
        acc_scr[...] += product(act, down_scr[place])

    @pl.when(step == pl.num_programs(0) - 1)
    def _():
        total = acc_scr[...]
        sum_ref[...] = total
        hidden_ref[...] = norm_forward(total, gains_ref[2:3], shifts_ref[2:3])[0].astype(LOW)


def block_forward(
    length, inputs, attn_qkv, attn_out, ffn_up, ffn_down, up_bias, gains, shifts, biases
):
    tokens, width = inputs.shape
    inner = ffn_up.shape[1]
    group = min(256, width)
    groups = width // group
    block = min(1024, inner)
    blocks = inner // block
    full = pl.BlockSpec((tokens, width), lambda g, n: (0, 0))
    part = pl.BlockSpec((tokens, group), lambda g, n: (0, jnp.minimum(g, groups - 1)))
    low = jax.ShapeDtypeStruct((tokens, width), LOW)
    wide = jax.ShapeDtypeStruct((tokens, width), WIDE)
    return pl.pallas_call(
        block_kernel,
        grid_spec=pltpu.PrefetchScalarGridSpec(
            num_scalar_prefetch=1,
            grid=(groups + blocks,),
            in_specs=[
                full,
                pl.BlockSpec((3, width, group), lambda g, n: (0, 0, jnp.minimum(g, groups - 1))),
                pl.BlockSpec((group, width), lambda g, n: (jnp.minimum(g, groups - 1), 0)),
                pl.BlockSpec((1, block), lambda g, n: (0, jnp.maximum(g - groups, 0))),
                pl.BlockSpec(gains.shape, lambda g, n: (0, 0)),
                pl.BlockSpec(shifts.shape, lambda g, n: (0, 0)),
                pl.BlockSpec(biases.shape, lambda g, n: (0, 0)),
                pl.BlockSpec(
                    (biases.shape[0], group), lambda g, n: (0, jnp.minimum(g, groups - 1))
                ),
                pl.BlockSpec(memory_space=pl.ANY),
                pl.BlockSpec(memory_space=pl.ANY),
            ],
            out_specs=[part, part, part, part, full, full, full]
            + [pl.BlockSpec((tokens, block), lambda g, n: (0, jnp.maximum(g - groups, 0)))]
            + [full, full],
            scratch_shapes=[
                pltpu.VMEM((tokens, width), WIDE),
                pltpu.VMEM((blocks, width, block), LOW),
                pltpu.VMEM((blocks, block, width), LOW),
                pltpu.SemaphoreType.DMA((2, blocks)),
            ],
        ),
        out_shape=[low, low, low, low, low, wide, low]
        + [jax.ShapeDtypeStruct((tokens, inner), LOW), wide, low],
        cost_estimate=cost(16),
        name="block_forward",
    )(
        length, inputs, attn_qkv, attn_out, up_bias.reshape(1, inner), gains, shifts, biases,
        biases, ffn_up, ffn_down
    )


def norm_stats(values):
    centred = values - jnp.mean(values, axis=-1, keepdims=True)
    inverse = lax.rsqrt(jnp.mean(centred * centred, axis=-1, keepdims=True) + EPS)
    return centred * inverse, inverse


def attention_back_kernel(
    length_ref, attn_in_ref, out_w_ref, query_ref, key_ref, value_ref, parts_ref, sums_ref,
    attn_t_scr
):
    tokens = attn_in_ref.shape[0]
    width = query_ref.shape[1]

    @pl.when(pl.program_id(0) == 0)
    def _():
        attn_t_scr[...] = attn_in_ref[...].T

    mixed_grad = product(out_w_ref[...], attn_t_scr[...]).T.astype(LOW)
    allowed = seen_keys(tokens, length_ref[0])
    masks = head_masks(128)
    zero = jnp.zeros((tokens, 128), LOW)
    for pair in range(width // 128):
        cols = slice(pair * 128, (pair + 1) * 128)
        q_pair, k_pair, v_pair = query_ref[:, cols], key_ref[:, cols], value_ref[:, cols]
        m_pair = mixed_grad[:, cols]
        totals = [jnp.zeros((tokens, 128), WIDE) for _ in range(3)]
        for mask in masks:
            k_one = jnp.where(mask, k_pair, zero)
            probs = masked_softmax(product_nt(q_pair, k_one), allowed)
            prob_grad = product_nt(m_pair, jnp.where(mask, v_pair, zero))
            delta = jnp.sum(probs * prob_grad, axis=-1, keepdims=True)
            score_grad = (probs * (prob_grad - delta)).astype(LOW)
            totals[0] += product(score_grad, k_one)
            totals[1] += product_tn(score_grad, jnp.where(mask, q_pair, zero))
            totals[2] += product_tn(probs.astype(LOW), jnp.where(mask, m_pair, zero))
        for kind, total in enumerate(totals):
            scale = HD ** (-0.5) if kind < 2 else 1.0
            grad = (total * scale).astype(LOW)
            parts_ref[:, kind * width + pair * 128 : kind * width + (pair + 1) * 128] = grad
            if kind != 1:
                sums_ref[kind : kind + 1, cols] = jnp.sum(
                    grad.astype(WIDE), axis=0, keepdims=True
                )


def attention_back(length, attn_in, attn_out, query, key, value, parts):
    tokens, width = attn_in.shape
    group = width // parts
    part = pl.BlockSpec((tokens, group), lambda g, n: (0, g))
    return pl.pallas_call(
        attention_back_kernel,
        grid_spec=pltpu.PrefetchScalarGridSpec(
            num_scalar_prefetch=1,
            grid=(parts,),
            in_specs=[
                pl.BlockSpec((tokens, width), lambda g, n: (0, 0)),
                pl.BlockSpec((group, width), lambda g, n: (g, 0)),
                part,
                part,
                part,
            ],
            out_specs=[
                pl.BlockSpec((None, tokens, 3 * group), lambda g, n: (g, 0, 0)),
                pl.BlockSpec((8, group), lambda g, n: (0, g)),
            ],
            scratch_shapes=[pltpu.VMEM((width, tokens), LOW)],
        ),
        out_shape=[
            jax.ShapeDtypeStruct((parts, tokens, 3 * group), LOW),
            jax.ShapeDtypeStruct((8, width), WIDE),
        ],
        cost_estimate=cost(9),
        name="attention_back",
    )(length, attn_in, attn_out, query, key, value)


def to_columns(rows):
    short = 128 - rows.shape[0]
    padded = jnp.concatenate([rows, jnp.zeros((short, rows.shape[1]), rows.dtype)], axis=0)
    return padded.T


def word_columns(words_ref):
    columns = [to_columns(words_ref[k])[:, 0:1] for k in range(words_ref.shape[0])]
    return jnp.concatenate(columns, axis=0).astype(jnp.int32)


def is_word(where_wide, first_col):
    lanes = lax.broadcasted_iota(jnp.int32, (1, where_wide.shape[1]), 1) + first_col
    return where_wide == lanes


def stats_kernel(
    base_ref, rows_ref, words_ref, keys_ref, norms_ref, slots_ref, head_ref, first_ref,
    second_ref, proj_one_ref, proj_two_ref, stats_ref, ones_ref, twos_ref
):
    rows = rows_ref[...]
    pair = words_ref.shape[0]
    tokens = words_ref.shape[2]
    words = word_columns(words_ref)
    ones = product(rows, proj_one_ref[...]).astype(LOW)
    twos = product(rows, proj_two_ref[...]).astype(LOW)
    ones_ref[...] = ones
    twos_ref[...] = twos
    picked = jnp.zeros((rows.shape[0], 1), WIDE)
    sums = []
    for place, (left, words_w) in enumerate(
        ((rows, head_ref), (ones, first_ref), (twos, second_ref))
    ):
        columns = words_w.shape[1]
        tile = SECOND_TILE if columns % SECOND_TILE == 0 else columns
        total = jnp.zeros((rows.shape[0], tile), WIDE)
        chosen = jnp.zeros((rows.shape[0], tile), WIDE)
        where_wide = jnp.broadcast_to(words - base_ref[place], (rows.shape[0], tile))
        for start in range(0, columns, tile):
            logits = product(left, words_w[:, start : start + tile])
            total = total + jnp.exp(logits)
            chosen = jnp.where(is_word(where_wide, start), logits, chosen)
        sums.append(jnp.sum(total, axis=1, keepdims=True))
        picked = picked + jnp.sum(chosen, axis=1, keepdims=True)
    sums.append(picked)
    lanes = lax.broadcasted_iota(jnp.int32, (rows.shape[0], 128), 1)
    table = jnp.zeros((rows.shape[0], 128), WIDE)
    for place, column in enumerate(sums):
        table = jnp.where(lanes == place, column, table)
    slot_count = slots_ref.shape[1]
    scale = 1.0 / math.sqrt(rows.shape[1])
    for k in range(pair):
        keys = keys_ref[k]
        norms = norms_ref[k][:, 0:1]
        scored = product_nt(keys, rows[k * tokens : (k + 1) * tokens]) * scale
        scored = scored - norms * (0.5 * scale)
        ids = lax.broadcasted_iota(jnp.int32, scored.shape, 0)
        for m in range(slot_count):
            hit = ids == slots_ref[k, m : m + 1, :]
            stats_ref[k, m : m + 1, :] = jnp.sum(
                jnp.where(hit, scored, 0.0), axis=0, keepdims=True
            )
        stats_ref[k, slot_count : slot_count + 8, :] = table[k * tokens : (k + 1) * tokens].T[0:8]


def whole_spec(array):
    return pl.BlockSpec(array.shape, lambda *_: (0,) * array.ndim)


def word_stats(base, rows_all, words_f, key_block, norms, slots_t, weights, pair):
    sources, slot_count, tokens = slots_t.shape
    count = key_block.shape[1]
    width = rows_all.shape[1]
    chunk = pair * tokens
    ones = weights[3].shape[1]
    twos = weights[4].shape[1]
    return pl.pallas_call(
        stats_kernel,
        grid_spec=pltpu.PrefetchScalarGridSpec(
            num_scalar_prefetch=1,
            grid=(sources // pair,),
            in_specs=[
                pl.BlockSpec((chunk, width), lambda g, b: (g, 0)),
                pl.BlockSpec((pair, 1, tokens), lambda g, b: (g, 0, 0)),
                pl.BlockSpec((pair, count, width), lambda g, b: (g, 0, 0)),
                pl.BlockSpec((pair, count, 128), lambda g, b: (g, 0, 0)),
                pl.BlockSpec((pair, slot_count, tokens), lambda g, b: (g, 0, 0)),
            ]
            + [whole_spec(w) for w in weights],
            out_specs=[
                pl.BlockSpec((pair, slot_count + 8, tokens), lambda g, b: (g, 0, 0)),
                pl.BlockSpec((chunk, ones), lambda g, b: (g, 0)),
                pl.BlockSpec((chunk, twos), lambda g, b: (g, 0)),
            ],
        ),
        out_shape=[
            jax.ShapeDtypeStruct((sources, slot_count + 8, tokens), WIDE),
            jax.ShapeDtypeStruct((rows_all.shape[0], ones), LOW),
            jax.ShapeDtypeStruct((rows_all.shape[0], twos), LOW),
        ],
        cost_estimate=cost(13),
        name="word_stats",
    )(base, rows_all, words_f, key_block, norms, slots_t, *weights)


def word_grads_kernel(
    order_ref, base_ref, rows_ref, ones_ref, twos_ref, returned_ref, words_ref, keys_ref,
    slots_ref, head_ref, first_ref, second_ref, first_t_ref, second_t_ref, mixed_t_ref, *refs
):
    (
        mine_ref, other_ref, head_g_ref, first_g_ref, second_g_ref, back_ref, terms_scr, mixed_scr
    ) = refs[-8:]
    rows = rows_ref[...]
    pair = words_ref.shape[0]
    tokens = words_ref.shape[2]
    slot_count = slots_ref.shape[1]
    words = word_columns(words_ref)
    coefs = [to_columns(returned_ref[k, slot_count : slot_count + 8, :]) for k in range(pair)]
    coefs = jnp.concatenate(coefs, axis=0)
    weight = coefs[:, 0:1]
    in_first = (words >= base_ref[3]) & (words < base_ref[4])
    in_second = words >= base_ref[4]
    scales = (
        weight,
        jnp.where(in_first, weight, 0.0),
        jnp.where(in_second, weight, 0.0),
    )
    lefts = (rows, ones_ref[...], twos_ref[...])
    for place, (words_w, out_ref) in enumerate(
        ((head_ref, head_g_ref), (first_ref, first_g_ref), (second_ref, second_g_ref))
    ):
        columns = words_w.shape[1]
        tile = SECOND_TILE if columns % SECOND_TILE == 0 else columns
        where_wide = jnp.broadcast_to(words - base_ref[place], (rows.shape[0], tile))
        scale = scales[place]
        log_sum = coefs[:, place + 1 : place + 2] - jnp.log(scale)

        def one_tile(tile_w, start):
            logits = product(lefts[place], tile_w)
            hit = is_word(where_wide, start)
            return (jnp.exp(logits - log_sum) - jnp.where(hit, scale, 0.0)).astype(LOW)

        if columns == tile:
            out_ref[...] = one_tile(words_w[...], 0)
        else:

            for start in range(0, columns, tile):
                out_ref[:, start : start + tile] = one_tile(
                    words_w[:, start : start + tile], start
                )

    ones = ones_ref.shape[1]
    heads = head_g_ref.shape[1]
    mixed_scr[:, ones : ones + heads] = head_g_ref[...]
    back_one = product(first_g_ref[...], first_t_ref[...]).astype(LOW)
    mixed_scr[:, 0:ones] = back_one
    back_ref[:, 0:ones] = back_one
    back_two = product(second_g_ref[...], second_t_ref[...]).astype(LOW)
    mixed_scr[:, ones + heads :] = back_two
    back_ref[:, ones:] = back_two
    term = product(mixed_scr[...], mixed_t_ref[...])
    key_scale = 1.0 / math.sqrt(rows.shape[1])
    count = keys_ref.shape[1]
    ids = lax.broadcasted_iota(jnp.int32, (count, tokens), 0)
    for k in range(pair):
        dense = jnp.zeros((count, tokens), WIDE)
        for m in range(slot_count):
            hit = ids == slots_ref[k, m : m + 1, :]
            dense = jnp.where(hit, returned_ref[k, m : m + 1, :], dense)
        near = product_tn(dense.astype(LOW), keys_ref[k]) * key_scale
        terms_scr[k] = (term[k * tokens : (k + 1) * tokens] + near).astype(LOW)
    if pair == 2:
        core = base_ref[5]
        mine_ref[0] = terms_scr[core]
        other_ref[0] = terms_scr[1 - core]
    else:
        mine_ref[0] = terms_scr[0]
        other_ref[0] = terms_scr[0]


def word_grads(order, base, rows_all, ones_all, twos_all, returned, words_f, key_block, slots_t,
               weights, pair):
    sources, slot_count, tokens = slots_t.shape
    count = key_block.shape[1]
    width = rows_all.shape[1]
    chunk = pair * tokens
    total = rows_all.shape[0]
    steps = order.shape[0]
    sizes = [weights[k].shape[1] for k in range(3)]
    sizes.append(weights[5].shape[0] - sizes[0])

    def by_row(columns):
        return pl.BlockSpec((chunk, columns), lambda g, o, b: (o[g], 0))

    inputs = [rows_all, ones_all, twos_all, returned, words_f, key_block, slots_t, *weights]
    return pl.pallas_call(
        word_grads_kernel,
        grid_spec=pltpu.PrefetchScalarGridSpec(
            num_scalar_prefetch=2,
            grid=(steps,),
            in_specs=[
                by_row(width),
                by_row(ones_all.shape[1]),
                by_row(twos_all.shape[1]),
                pl.BlockSpec((pair, slot_count + 8, tokens), lambda g, o, b: (o[g], 0, 0)),
                pl.BlockSpec((pair, 1, tokens), lambda g, o, b: (o[g], 0, 0)),
                pl.BlockSpec((pair, count, width), lambda g, o, b: (o[g], 0, 0)),
                pl.BlockSpec((pair, slot_count, tokens), lambda g, o, b: (o[g], 0, 0)),
            ]
            + [whole_spec(w) for w in weights],
            out_specs=[
                pl.BlockSpec((1, tokens, width), lambda g, o, b: (g, 0, 0)),
                pl.BlockSpec((1, tokens, width), lambda g, o, b: (g, 0, 0)),
            ]
            + [by_row(size) for size in sizes],
            scratch_shapes=[
                pltpu.VMEM((pair, tokens, width), LOW),
                pltpu.VMEM((chunk, weights[5].shape[0]), LOW),
            ],
        ),
        out_shape=[
            jax.ShapeDtypeStruct((steps, tokens, width), LOW),
            jax.ShapeDtypeStruct((steps, tokens, width), LOW),
        ]
        + [jax.ShapeDtypeStruct((total, size), LOW) for size in sizes],
        cost_estimate=cost(10),
        name="word_grads",
    )(order, base, *inputs)


def word_sums_kernel(
    rows_ref, ones_ref, twos_ref, head_g_ref, first_g_ref, second_g_ref, back_ref,
    packed_ref, proj_ref, *scratch
):
    step = pl.program_id(0)
    pairs = (
        (head_g_ref, rows_ref),
        (ones_ref, first_g_ref),
        (twos_ref, second_g_ref),
        (rows_ref, back_ref),
    )

    @pl.when(step == 0)
    def _():
        for acc in scratch:
            acc[...] = jnp.zeros_like(acc)

    for (left, right), acc in zip(pairs, scratch):
        acc[...] += product_tn(left[...], right[...])

    @pl.when(step == pl.num_programs(0) - 1)
    def _():
        proj_ref[...] = scratch[3][...].astype(LOW)
        place = 0
        for acc in scratch[:3]:
            rows, columns = acc.shape
            for start in range(0, columns, 128):
                packed_ref[place : place + rows, :] = acc[:, start : start + 128].astype(LOW)
                place += rows


def word_sums(rows_all, ones_all, twos_all, grads):
    total = rows_all.shape[0]
    chunk = min(512, total)
    inputs = [rows_all, ones_all, twos_all, *grads]
    shapes = [
        (grads[0].shape[1], rows_all.shape[1]),
        (ones_all.shape[1], grads[1].shape[1]),
        (twos_all.shape[1], grads[2].shape[1]),
        (rows_all.shape[1], grads[3].shape[1]),
    ]
    packed_rows = sum(rows * columns for rows, columns in shapes[:3]) // 128
    out_shapes = [(packed_rows, 128), shapes[3]]
    packed, proj = pl.pallas_call(
        word_sums_kernel,
        grid=(total // chunk,),
        in_specs=[pl.BlockSpec((chunk, item.shape[1]), lambda g: (g, 0)) for item in inputs],
        out_specs=[pl.BlockSpec(shape, lambda g: (0, 0)) for shape in out_shapes],
        out_shape=[jax.ShapeDtypeStruct(shape, LOW) for shape in out_shapes],
        scratch_shapes=[pltpu.VMEM(shape, WIDE) for shape in shapes],
        cost_estimate=cost(10),
        name="word_sums",
    )(*inputs)
    return packed, proj, shapes[:3]


def unpack_kernel(me_ref, parts_ref, *outs):
    count, part_rows, _ = parts_ref.shape
    me = me_ref[0]
    place = 0
    for out in outs:
        rows, columns = out.shape
        for start in range(0, columns, 128):
            done = 0
            while done < rows:
                part, offset = divmod(place + done, part_rows)
                size = min(rows - done, part_rows - offset)
                out[done : done + size, start : start + 128] = parts_ref[
                    part ^ me, offset : offset + size, :
                ].astype(WIDE)
                done += size
            place += rows


def unpack_words(parts, shapes):
    return pl.pallas_call(
        unpack_kernel,
        grid_spec=pltpu.PrefetchScalarGridSpec(
            num_scalar_prefetch=1,
            grid=(1,),
            in_specs=[whole_spec(parts)],
            out_specs=[pl.BlockSpec(shape, lambda *_: (0, 0)) for shape in shapes],
        ),
        out_shape=[jax.ShapeDtypeStruct(shape, WIDE) for shape in shapes],
        cost_estimate=cost(3),
        compiler_params=pltpu.CompilerParams(vmem_limit_bytes=12 << 20),
        name="unpack_words",
    )(lax.axis_index("dp").astype(jnp.int32).reshape(1), parts)


def key_norms_kernel(keys_ref, norms_ref):
    for k in range(keys_ref.shape[0]):
        wide = keys_ref[k].astype(WIDE)
        norms = jnp.sum(wide * wide, axis=1, keepdims=True)
        norms_ref[k] = jnp.broadcast_to(norms, norms_ref.shape[1:])


def key_norms(key_block):
    sources, count, width = key_block.shape
    pair = min(2, sources)
    return pl.pallas_call(
        key_norms_kernel,
        grid=(sources // pair,),
        in_specs=[pl.BlockSpec((pair, count, width), lambda g: (g, 0, 0))],
        out_specs=pl.BlockSpec((pair, count, 128), lambda g: (g, 0, 0)),
        out_shape=jax.ShapeDtypeStruct((sources, count, 128), WIDE),
        cost_estimate=cost(20),
        compiler_params=pltpu.CompilerParams(vmem_limit_bytes=8 << 20),
        name="key_norms",
    )(key_block)


def input_back_kernel(
    parts_ref, qkv_ref, in_ref, grad_ref, gains_ref, input_grad_ref, sums_ref, acc_scr
):
    step = pl.program_id(0)

    @pl.when(step == 0)
    def _():
        acc_scr[...] = jnp.zeros_like(acc_scr)

    group = qkv_ref.shape[2]
    total = acc_scr[...]
    for kind in range(3):
        total = total + product(
            qkv_ref[kind], parts_ref[:, kind * group : (kind + 1) * group].T
        )
    acc_scr[...] = total

    @pl.when(step == pl.num_programs(0) - 1)
    def _():
        unit_rows, inverse = norm_stats(in_ref[...].astype(WIDE))
        back, gain, shift = norm_backward(acc_scr[...].T, unit_rows, inverse, gains_ref[0:1])
        input_grad_ref[...] = grad_ref[...] + back
        sums_ref[0:1] = gain
        sums_ref[1:2] = shift


def input_back(parts, attn_qkv, inputs, first_grad, gains):
    count, tokens, _ = parts.shape
    width = inputs.shape[1]
    group = width // count
    full = pl.BlockSpec((tokens, width), lambda g: (0, 0))
    return pl.pallas_call(
        input_back_kernel,
        grid=(count,),
        in_specs=[
            pl.BlockSpec((None, tokens, 3 * group), lambda g: (g, 0, 0)),
            pl.BlockSpec((3, width, group), lambda g: (0, 0, g)),
            full,
            full,
            pl.BlockSpec(gains.shape, lambda g: (0, 0)),
        ],
        out_specs=[full, pl.BlockSpec((8, width), lambda g: (0, 0))],
        out_shape=[
            jax.ShapeDtypeStruct((tokens, width), WIDE),
            jax.ShapeDtypeStruct((8, width), WIDE),
        ],
        scratch_shapes=[pltpu.VMEM((width, tokens), WIDE)],
        cost_estimate=cost(7),
        name="input_back",
    )(parts, attn_qkv, inputs, first_grad, gains)


def shards(
    inputs,
    lengths,
    targets,
    attn_qkv,
    attn_out,
    ffn_up,
    ffn_down,
    norm_gains,
    norm_shifts,
    biases,
    up_bias,
    cluster_proj,
    proj_first,
    proj_second,
    head_words,
    tail_first,
    tail_second,
    store_keys,
    block_rows,
    near_slots,
    near_words,
):
    tokens_here = inputs.shape[0]
    d_model = inputs.shape[1]
    dp_count = lax.axis_size("dp")
    sources = lax.axis_size("line") * 2
    my_index = lax.axis_index("line") * 2 + lax.axis_index("core")
    group_rows = tokens_here * sources
    head_cols = head_words.shape[1]
    first_cols = tail_first.shape[1]
    second_cols = tail_second.shape[1]
    head_total = head_cols * sources
    first_total = first_cols * sources
    ff_width = ffn_up.shape[1]
    valid_mask = (jnp.arange(tokens_here) < lengths[0]).astype(WIDE)

    (
        query_low, key_low, value_low, mixed_low, normed_low, first_sum, second_low, act_low,
        second_sum, hidden_low
    ) = block_forward(
        lengths, inputs, attn_qkv, attn_out, ffn_up, ffn_down, up_bias, norm_gains, norm_shifts,
        biases
    )
    cluster_logits = lax.dot_general(
        cluster_proj, hidden_low, (((0,), (1,)), ((), ())), preferred_element_type=WIDE
    )

    rows_all = lax.all_gather(hidden_low, STORE, axis=0, tiled=True)

    key_block = jnp.take(store_keys, block_rows[0, 0].reshape(-1), axis=0, mode="clip")
    key_block = key_block.reshape(sources, -1, d_model)
    slots_t = near_slots[0, 0].transpose(1, 2, 0)
    slot_count = slots_t.shape[1]
    words_t = near_words.T

    weights = (head_words, tail_first, tail_second, proj_first, proj_second)
    back_weights = weights[:3] + (
        tail_first.T,
        tail_second.T,
        jnp.concatenate([proj_first.T, head_words.T, proj_second.T], axis=0),
    )
    norms = key_norms(key_block)

    left_low = jnp.concatenate([act_low, second_low, mixed_low, normed_low], axis=1)
    left_low, rows_all, norms, slots_t, words_t, back_weights = lax.optimization_barrier(
        (left_low, rows_all, norms, slots_t, words_t, back_weights)
    )
    left_all = lax.all_gather(left_low, "dp", axis=0, tiled=True)

    core = lax.axis_index("core")
    words_f = targets.astype(WIDE).reshape(sources, 1, tokens_here)
    base = jnp.stack(
        [
            my_index * head_cols,
            head_total + my_index * first_cols,
            head_total + first_total + my_index * second_cols,
            jnp.int32(head_total),
            jnp.int32(head_total + first_total),
            core,
        ]
    ).astype(jnp.int32)
    outgoing, ones_all, twos_all = word_stats(
        base, rows_all, words_f, key_block, norms, slots_t, back_weights[:3] + weights[3:], 2
    )
    incoming = lax.all_to_all(outgoing, STORE, 0, 0)

    near_scores = incoming[:, :slot_count].reshape(sources * slot_count, tokens_here)
    own_stats = jnp.sum(incoming[:, slot_count : slot_count + 4], axis=0)
    own_words = lax.dynamic_slice_in_dim(targets, my_index * tokens_here, tokens_here, 0)
    in_first = ((own_words >= head_total) & (own_words < head_total + first_total)).astype(WIDE)
    in_second = (own_words >= head_total + first_total).astype(WIDE)
    head_sum = own_stats[0] + jnp.sum(jnp.exp(cluster_logits), axis=0)
    log_head = jnp.log(head_sum)
    log_first = jnp.log(own_stats[1])
    log_second = jnp.log(own_stats[2])
    log_model = (
        own_stats[3]
        - log_head
        + in_first * (cluster_logits[0] - log_first)
        + in_second * (cluster_logits[1] - log_second)
    )
    near_top = jnp.max(near_scores, axis=0, keepdims=True)
    near_exp = jnp.exp(near_scores - near_top)
    near_probs = near_exp / jnp.sum(near_exp, axis=0, keepdims=True)
    matched = (words_t == own_words[None, :]).astype(WIDE)
    near_mass = jnp.sum(near_probs * matched, axis=0)
    model_prob = jnp.exp(log_model)
    mixture = NEAR_WEIGHT * near_mass + (1.0 - NEAR_WEIGHT) * model_prob
    token_loss = -valid_mask * jnp.log(mixture)
    model_weight = valid_mask * (1.0 - NEAR_WEIGHT) * model_prob / mixture
    near_weight = valid_mask * NEAR_WEIGHT / mixture
    score_grad = -near_weight[None, :] * near_probs * (matched - near_mass[None, :])
    coef = jnp.stack([model_weight, log_head, log_first, log_second] + 4 * [model_weight])
    returning = jnp.concatenate(
        [
            score_grad.reshape(sources, slot_count, tokens_here),
            jnp.broadcast_to(coef[None], (sources,) + coef.shape),
        ],
        axis=1,
    )
    returned = lax.all_to_all(returning, STORE, 0, 0)

    lines = lax.axis_size("line")
    mine, other, *word_terms = word_grads(
        jnp.arange(lines, dtype=jnp.int32),
        base,
        rows_all,
        ones_all,
        twos_all,
        returned,
        words_f,
        key_block,
        slots_t,
        back_weights,
        2,
    )
    both = (mine.astype(WIDE) + swap_partner(other, "core", 1).astype(WIDE)).astype(LOW)
    row_parts = lax.all_to_all(both, "line", 0, 0)
    row_back = jnp.sum(row_parts.astype(WIDE), axis=0)
    word_terms, both = lax.optimization_barrier((word_terms, both))
    word_packed, proj_acc, word_shapes = word_sums(rows_all, ones_all, twos_all, word_terms)

    own_rows = d_model // sources
    proj_width = proj_acc.shape[1]
    sub_rows = own_rows // dp_count
    proj_parts = proj_acc.reshape(sources, dp_count, sub_rows, proj_width).transpose(1, 0, 2, 3)
    dp_index = lax.axis_index("dp")
    proj_sum = lax.dynamic_index_in_dim(proj_parts, dp_index, 0, keepdims=False).astype(WIDE)
    for q in range(1, dp_count):
        part = lax.dynamic_index_in_dim(proj_parts, dp_index ^ q, 0, keepdims=False)
        proj_sum = proj_sum + swap_partner(part, "dp", q).astype(WIDE)
    cluster_rows = model_weight[None, :] * (
        jnp.exp(cluster_logits - log_head[None, :]) - jnp.stack([in_first, in_second])
    )
    hidden_grad = row_back + lax.dot_general(
        cluster_rows, cluster_proj.astype(WIDE), (((0,), (1,)), ((), ())), precision=HIGH
    )
    cluster_acc = jnp.dot(cluster_rows, hidden_low.astype(WIDE), precision=HIGH)
    unit_three, inv_three = norm_stats(second_sum)
    second_grad, gain_three, shift_three = norm_backward(
        hidden_grad, unit_three, inv_three, norm_gains[2]
    )
    down_in = second_grad.astype(LOW)
    down_parts = exchange_columns(down_in)
    bias_down = jnp.sum(down_in.astype(WIDE), axis=0, keepdims=True)
    act_grad = product_nt(down_in, ffn_down)
    pre_grad = jnp.where(act_low.astype(WIDE) > 0, act_grad, 0.0).astype(LOW)
    up_bias_acc = jnp.sum(pre_grad.astype(WIDE), axis=0, keepdims=True)
    marks = [0, ff_width, ff_width + d_model, ff_width + 2 * d_model, ff_width + 3 * d_model]
    lefts = [left_all[:, a:b] for a, b in zip(marks[:-1], marks[1:])]
    down = Halving(grad_tile(lefts[0], after(down_parts, pre_grad)))
    norm_two_grad = product_nt(after(pre_grad, down.outgoing), ffn_up)
    unit_two, inv_two = norm_stats(first_sum)
    back_second, gain_two, shift_two = norm_backward(
        norm_two_grad, unit_two, inv_two, norm_gains[1]
    )
    first_grad_sum = second_grad + back_second
    attn_in = first_grad_sum.astype(LOW)
    bias_attn = jnp.sum(attn_in.astype(WIDE), axis=0, keepdims=True)
    mark = down.add(attn_in)
    up_width = ff_width // dp_count
    head_width = d_model // dp_count
    up_send = jnp.stack(
        [
            jnp.concatenate(
                [
                    pre_grad[:, k * up_width : (k + 1) * up_width],
                    attn_in[:, k * head_width : (k + 1) * head_width],
                ],
                axis=1,
            )
            for k in range(dp_count)
        ]
    )
    up_parts = lax.all_to_all(up_send, "dp", 0, 0)
    stacked_parts, sums_three = attention_back(
        lengths, after(attn_in, up_send, mark), attn_out, query_low, key_low, value_low, dp_count
    )
    mark = down.add(stacked_parts)
    qkv_parts = lax.all_to_all(after(stacked_parts, up_parts), "dp", 0, 0)
    word_send = after(word_packed.reshape(dp_count, -1, 128), qkv_parts)
    word_parts = lax.all_to_all(word_send, "dp", 0, 0)
    proj_rows = sub_rows * proj_width // (up_width + head_width)
    proj_block = proj_sum.astype(LOW).reshape(sources, proj_rows, up_width + head_width)
    up_parts = after(up_parts, mark)
    up = Halving(
        jnp.concatenate(
            [
                jnp.concatenate(
                    [
                        grad_tile(lefts[1], up_parts[:, :, :up_width]),
                        grad_tile(lefts[2], up_parts[:, :, up_width:]),
                    ],
                    axis=2,
                ),
                proj_block,
            ],
            axis=1,
        )
    )
    input_grad, sums_one = input_back(
        after(stacked_parts, up.outgoing, qkv_parts), attn_qkv, inputs, first_grad_sum, norm_gains
    )
    down_own = down.finish(input_grad)
    mark = up.add(input_grad, down_own)

    def by_store(value):
        rows = value.shape[0]
        return value.reshape(rows, sources, -1).transpose(1, 0, 2).reshape(sources, -1)

    small = jnp.concatenate(
        [
            by_store(jnp.concatenate([sums_one[0:1], gain_two, gain_three])),
            by_store(jnp.concatenate([sums_one[1:2], shift_two, shift_three])),
            by_store(jnp.concatenate([sums_three[0:1], sums_three[2:3], bias_attn, bias_down])),
            by_store(up_bias_acc),
            by_store(cluster_acc),
        ],
        axis=1,
    )
    small_count = small.shape[1]
    small_rows = -(-small_count // (3 * head_width))
    if own_rows % 128 == 0:
        small_rows = -(-small_rows // 8) * 8
    small = jnp.pad(small, ((0, 0), (0, small_rows * 3 * head_width - small_count)))
    small = small.reshape(sources, small_rows, 3 * head_width).astype(LOW)
    qkv = Halving(
        jnp.concatenate([grad_tile(lefts[3], after(qkv_parts, mark)), small], axis=1)
    )
    down_pieces = gather_dp(down_own)
    mark = qkv.add(qkv.outgoing)
    mark = up.add(mark)
    word_own = jnp.sum(after(word_parts, mark).astype(WIDE), axis=0).astype(LOW)
    mark = qkv.add(word_own)
    word_pieces = gather_dp(word_own)
    down_out = join_pieces(after(down_pieces, mark), 1, 0, head_width, 1)
    up_own = up.finish(down_out)
    up_pieces = gather_dp(up_own)
    word_pieces = after(word_pieces, up_own)
    head_t, first_out, second_out = unpack_words(jnp.stack(word_pieces), word_shapes)
    head_out = head_t.T
    qkv_own = qkv.finish(head_t)
    qkv_pieces = gather_dp(qkv_own)
    up_pieces = after(up_pieces, qkv_own)
    up_main = [piece[:own_rows] for piece in up_pieces]
    up_out = join_pieces(up_main, 1, 0, up_width, 1)
    out_out = join_pieces(up_main, 1, up_width, head_width, 1)
    proj_out = join_pieces(
        [piece[own_rows:].reshape(sub_rows, proj_width) for piece in up_pieces],
        0,
        0,
        sub_rows,
        0,
    )
    qkv_main = [piece[:own_rows] for piece in qkv_pieces]
    qkv_out = jnp.stack(
        [join_pieces(qkv_main, 1, kind * head_width, head_width, 1) for kind in range(3)]
    )
    small_sum = sum(piece[own_rows:].astype(WIDE) for piece in qkv_pieces).reshape(-1)
    sizes = [3 * own_rows, 3 * own_rows, 4 * own_rows, ff_width // sources, 2 * own_rows]
    ends = [0]
    for size in sizes:
        ends.append(ends[-1] + size)
    gains_out, shifts_out, biases_out, upb_out, cluster_out = (
        small_sum[a:b] for a, b in zip(ends[:-1], ends[1:])
    )
    return (
        token_loss,
        input_grad,
        qkv_out,
        out_out,
        up_out,
        down_out,
        gains_out.reshape(3, own_rows),
        shifts_out.reshape(3, own_rows),
        biases_out.reshape(4, own_rows),
        upb_out,
        cluster_out.reshape(2, own_rows).T,
        proj_out[:, : proj_first.shape[1]],
        proj_out[:, proj_first.shape[1] :],
        head_out,
        first_out,
        second_out,
    )


def solution(mesh):
    dp_count = mesh.shape["dp"]
    store_count = mesh.shape["store"]
    split = Mesh(mesh.devices.reshape(dp_count, store_count // 2, 2), ("dp",) + STORE)
    everyone = ("dp",) + STORE
    return jax.shard_map(
        shards,
        mesh=split,
        in_specs=(
            P(everyone, None),
            P(everyone),
            P("dp"),
            P(),
            P(),
            P(),
            P(),
            P(),
            P(),
            P(),
            P(),
            P(),
            P(),
            P(),
            P(None, STORE),
            P(None, STORE),
            P(None, STORE),
            P(STORE, None),
            P("dp", STORE, None, None),
            P("dp", STORE, None, None, None),
            P(everyone, None),
        ),
        out_specs=(
            P(everyone),
            P(everyone, None),
            P(None, STORE, None),
            P(STORE, None),
            P(STORE, None),
            P(STORE, None),
            P(None, STORE),
            P(None, STORE),
            P(None, STORE),
            P(STORE),
            P(STORE, None),
            P(STORE, None),
            P(STORE, None),
            P(None, STORE),
            P(None, STORE),
            P(None, STORE),
        ),
        check_vma=False,
    )
```

```python
import math

import jax
import jax.numpy as jnp
from jax import lax
from jax.experimental import pallas as pl
from jax.experimental.pallas import tpu as pltpu
from jax.sharding import Mesh
from jax.sharding import PartitionSpec as P

HEADS = 16
HD = 64


EPS = 1e-05
NEAR_WEIGHT = 0.25
NEG_FILL = -1e30
HIGH = lax.Precision.HIGHEST
STORE = ("line", "core")
LOW = jnp.bfloat16
WIDE = jnp.float32
SECOND_TILE = 256


def product(left, right):
    return jnp.dot(left, right, preferred_element_type=WIDE)


def product_tn(left, right):
    return lax.dot_general(left, right, (((0,), (0,)), ((), ())), preferred_element_type=WIDE)


def product_nt(left, right):
    return lax.dot_general(left, right, (((1,), (1,)), ((), ())), preferred_element_type=WIDE)


def norm_forward(values, gain_row, shift_row):
    row_mean = jnp.mean(values, axis=-1, keepdims=True)
    centred = values - row_mean
    inverse = lax.rsqrt(jnp.mean(centred * centred, axis=-1, keepdims=True) + EPS)
    unit_rows = centred * inverse
    return (unit_rows * gain_row + shift_row, unit_rows, inverse)


def norm_backward(grad_out, unit_rows, inverse, gain_row):
    scaled = grad_out * gain_row
    grad_in = inverse * (
        scaled
        - jnp.mean(scaled, axis=-1, keepdims=True)
        - unit_rows * jnp.mean(scaled * unit_rows, axis=-1, keepdims=True)
    )
    return (grad_in, jnp.sum(grad_out * unit_rows, axis=0, keepdims=True), jnp.sum(grad_out, axis=0, keepdims=True))


def swap_partner(value, axis, bit):
    count = lax.axis_size(axis)
    return lax.ppermute(value, axis, [(k, k ^ bit) for k in range(count)])


def after(value, *others):
    return lax.optimization_barrier((value, *others))[0]


class Halving:
    def __init__(self, blocks):
        lines = lax.axis_size("line")
        line = lax.axis_index("line")
        self.rest = blocks.shape[1:]
        self.current = blocks.reshape((lines, 2) + self.rest)
        self.steps = [(lax.axis_index("core"), "core", 1)]
        bit = 1
        while bit < lines:
            self.steps.append(((line // bit) & 1, "line", bit))
            bit *= 2
        self.received = None
        self.send()

    def send(self):
        mine, axis, bit = self.steps.pop(0)
        value = self.current
        outgoing = lax.dynamic_index_in_dim(value, 1 - mine, 1, keepdims=False).astype(LOW)
        self.outgoing = outgoing
        self.current = lax.dynamic_index_in_dim(value, mine, 1, keepdims=False)
        self.received = swap_partner(outgoing, axis, bit)

    def add(self, *others):
        received = after(self.received, *others) if others else self.received
        self.current = self.current.astype(WIDE) + received.astype(WIDE)
        if self.steps:
            self.current = self.current.reshape((-1, 2) + self.rest)
            self.send()
        return self.outgoing

    def finish(self, *others):
        while self.steps:
            self.add(*others)
        self.add(*others)
        return self.current[0].astype(LOW)


def grad_tile(left, right_parts):
    blocks = lax.axis_size("line") * 2
    right = right_parts.reshape(left.shape[0], right_parts.shape[2])
    tile = product_tn(left, right).astype(LOW)
    return tile.reshape(blocks, -1, right.shape[1])


def gather_dp(own):
    count = lax.axis_size("dp")
    return [own] + [swap_partner(own, "dp", q) for q in range(1, count)]


def join_pieces(pieces, axis, start, width, join_axis):
    count = len(pieces)
    me = lax.axis_index("dp")
    pieces = [lax.slice_in_dim(piece, start, start + width, axis=axis) for piece in pieces]
    bit = 1
    while bit < count:
        is_set = (me // bit) & 1 == 1
        pieces = [jnp.where(is_set, pieces[k ^ bit], pieces[k]) for k in range(count)]
        bit *= 2
    return jnp.concatenate([piece.astype(WIDE) for piece in pieces], axis=join_axis)


def exchange_columns(value):
    count = lax.axis_size("dp")
    tokens, columns = value.shape
    parts = value.reshape(tokens, count, columns // count).transpose(1, 0, 2)
    return lax.all_to_all(parts, "dp", 0, 0)


def cost(micros):
    return pl.CostEstimate(flops=int(micros * 9e8), transcendentals=0, bytes_accessed=1 << 20)


def head_masks(width):
    lanes = lax.broadcasted_iota(jnp.int32, (1, width), 1)
    return [(lanes // HD) % 2 == half for half in range(2)]


def masked_softmax(scores, allowed):
    scores = jnp.where(allowed, scores * HD ** (-0.5), NEG_FILL)
    exps = jnp.exp(scores - jnp.max(scores, axis=-1, keepdims=True))
    return exps / jnp.sum(exps, axis=-1, keepdims=True)


def seen_keys(tokens, length):
    rows = lax.broadcasted_iota(jnp.int32, (tokens, tokens), 0)
    cols = lax.broadcasted_iota(jnp.int32, (tokens, tokens), 1)
    return (cols <= rows) & (cols < length)


def block_kernel(
    length_ref, in_ref, qkv_ref, out_w_ref, up_bias_ref, gains_ref, shifts_ref, biases_ref,
    group_bias_ref, up_hbm, down_hbm,
    query_ref, key_ref, value_ref, mixed_ref, normed_ref, first_ref, second_ref, act_ref, sum_ref,
    hidden_ref, acc_scr, up_scr, down_scr, sems
):
    step = pl.program_id(0)
    tokens, width = in_ref.shape
    group = query_ref.shape[1]
    groups = width // group
    blocks = up_scr.shape[0]
    block = up_scr.shape[2]

    def fetches(place):
        start = place * block
        return (
            pltpu.make_async_copy(
                up_hbm.at[:, pl.ds(start, block)], up_scr.at[place], sems.at[0, place]
            ),
            pltpu.make_async_copy(
                down_hbm.at[pl.ds(start, block), :], down_scr.at[place], sems.at[1, place]
            ),
        )

    @pl.when(step == 0)
    def _():
        for place in range(blocks):
            for fetch in fetches(place):
                fetch.start()
        block_in = in_ref[...].astype(WIDE)
        normed_ref[...] = norm_forward(block_in, gains_ref[0:1], shifts_ref[0:1])[0].astype(LOW)
        acc_scr[...] = block_in + biases_ref[2:3]

    @pl.when(step < groups)
    def _():
        normed = normed_ref[...]
        query = (product(normed, qkv_ref[0]) + group_bias_ref[0:1]).astype(LOW)
        key = product(normed, qkv_ref[1]).astype(LOW)
        value = (product(normed, qkv_ref[2]) + group_bias_ref[1:2]).astype(LOW)
        query_ref[...] = query
        key_ref[...] = key
        value_ref[...] = value
        allowed = seen_keys(tokens, length_ref[0])
        masks = head_masks(128)
        zero = jnp.zeros((tokens, 128), LOW)
        for pair in range(group // 128):
            cols = slice(pair * 128, (pair + 1) * 128)
            q_pair, k_pair, v_pair = query[:, cols], key[:, cols], value[:, cols]
            mixed = jnp.zeros((tokens, 128), WIDE)
            for mask in masks:
                probs = masked_softmax(product_nt(q_pair, jnp.where(mask, k_pair, zero)), allowed)
                mixed = mixed + product(probs.astype(LOW), jnp.where(mask, v_pair, zero))
            mixed_ref[:, cols] = mixed.astype(LOW)
        acc_scr[...] += product(mixed_ref[...], out_w_ref[...])

    @pl.when(step == groups - 1)
    def _():
        first_sum = acc_scr[...]
        first_ref[...] = first_sum
        second_ref[...] = norm_forward(first_sum, gains_ref[1:2], shifts_ref[1:2])[0].astype(LOW)
        acc_scr[...] = first_sum + biases_ref[3:4]

    @pl.when(step >= groups)
    def _():
        place = step - groups
        for fetch in fetches(place):
            fetch.wait()
        pre_act = product(second_ref[...], up_scr[place]) + up_bias_ref[...]
        act = jnp.maximum(pre_act, 0.0).astype(LOW)
        act_ref[...] = act
        acc_scr[...] += product(act, down_scr[place])

    @pl.when(step == pl.num_programs(0) - 1)
    def _():
        total = acc_scr[...]
        sum_ref[...] = total
        hidden_ref[...] = norm_forward(total, gains_ref[2:3], shifts_ref[2:3])[0].astype(LOW)


def block_forward(
    length, inputs, attn_qkv, attn_out, ffn_up, ffn_down, up_bias, gains, shifts, biases
):
    tokens, width = inputs.shape
    inner = ffn_up.shape[1]
    group = min(256, width)
    groups = width // group
    block = min(1024, inner)
    blocks = inner // block
    full = pl.BlockSpec((tokens, width), lambda g, n: (0, 0))
    part = pl.BlockSpec((tokens, group), lambda g, n: (0, jnp.minimum(g, groups - 1)))
    low = jax.ShapeDtypeStruct((tokens, width), LOW)
    wide = jax.ShapeDtypeStruct((tokens, width), WIDE)
    return pl.pallas_call(
        block_kernel,
        grid_spec=pltpu.PrefetchScalarGridSpec(
            num_scalar_prefetch=1,
            grid=(groups + blocks,),
            in_specs=[
                full,
                pl.BlockSpec((3, width, group), lambda g, n: (0, 0, jnp.minimum(g, groups - 1))),
                pl.BlockSpec((group, width), lambda g, n: (jnp.minimum(g, groups - 1), 0)),
                pl.BlockSpec((1, block), lambda g, n: (0, jnp.maximum(g - groups, 0))),
                pl.BlockSpec(gains.shape, lambda g, n: (0, 0)),
                pl.BlockSpec(shifts.shape, lambda g, n: (0, 0)),
                pl.BlockSpec(biases.shape, lambda g, n: (0, 0)),
                pl.BlockSpec(
                    (biases.shape[0], group), lambda g, n: (0, jnp.minimum(g, groups - 1))
                ),
                pl.BlockSpec(memory_space=pl.ANY),
                pl.BlockSpec(memory_space=pl.ANY),
            ],
            out_specs=[part, part, part, part, full, full, full]
            + [pl.BlockSpec((tokens, block), lambda g, n: (0, jnp.maximum(g - groups, 0)))]
            + [full, full],
            scratch_shapes=[
                pltpu.VMEM((tokens, width), WIDE),
                pltpu.VMEM((blocks, width, block), LOW),
                pltpu.VMEM((blocks, block, width), LOW),
                pltpu.SemaphoreType.DMA((2, blocks)),
            ],
        ),
        out_shape=[low, low, low, low, low, wide, low]
        + [jax.ShapeDtypeStruct((tokens, inner), LOW), wide, low],
        cost_estimate=cost(16),
        name="block_forward",
    )(
        length, inputs, attn_qkv, attn_out, up_bias.reshape(1, inner), gains, shifts, biases,
        biases, ffn_up, ffn_down
    )


def norm_stats(values):
    centred = values - jnp.mean(values, axis=-1, keepdims=True)
    inverse = lax.rsqrt(jnp.mean(centred * centred, axis=-1, keepdims=True) + EPS)
    return centred * inverse, inverse


def attention_back_kernel(
    length_ref, attn_in_ref, out_w_ref, query_ref, key_ref, value_ref, parts_ref, sums_ref,
    attn_t_scr
):
    tokens = attn_in_ref.shape[0]
    width = query_ref.shape[1]

    @pl.when(pl.program_id(0) == 0)
    def _():
        attn_t_scr[...] = attn_in_ref[...].T

    mixed_grad = product(out_w_ref[...], attn_t_scr[...]).T.astype(LOW)
    allowed = seen_keys(tokens, length_ref[0])
    masks = head_masks(128)
    zero = jnp.zeros((tokens, 128), LOW)
    for pair in range(width // 128):
        cols = slice(pair * 128, (pair + 1) * 128)
        q_pair, k_pair, v_pair = query_ref[:, cols], key_ref[:, cols], value_ref[:, cols]
        m_pair = mixed_grad[:, cols]
        totals = [jnp.zeros((tokens, 128), WIDE) for _ in range(3)]
        for mask in masks:
            k_one = jnp.where(mask, k_pair, zero)
            probs = masked_softmax(product_nt(q_pair, k_one), allowed)
            prob_grad = product_nt(m_pair, jnp.where(mask, v_pair, zero))
            delta = jnp.sum(probs * prob_grad, axis=-1, keepdims=True)
            score_grad = (probs * (prob_grad - delta)).astype(LOW)
            totals[0] += product(score_grad, k_one)
            totals[1] += product_tn(score_grad, jnp.where(mask, q_pair, zero))
            totals[2] += product_tn(probs.astype(LOW), jnp.where(mask, m_pair, zero))
        for kind, total in enumerate(totals):
            scale = HD ** (-0.5) if kind < 2 else 1.0
            grad = (total * scale).astype(LOW)
            parts_ref[:, kind * width + pair * 128 : kind * width + (pair + 1) * 128] = grad
            if kind != 1:
                sums_ref[kind : kind + 1, cols] = jnp.sum(
                    grad.astype(WIDE), axis=0, keepdims=True
                )


def attention_back(length, attn_in, attn_out, query, key, value, parts):
    tokens, width = attn_in.shape
    group = width // parts
    part = pl.BlockSpec((tokens, group), lambda g, n: (0, g))
    return pl.pallas_call(
        attention_back_kernel,
        grid_spec=pltpu.PrefetchScalarGridSpec(
            num_scalar_prefetch=1,
            grid=(parts,),
            in_specs=[
                pl.BlockSpec((tokens, width), lambda g, n: (0, 0)),
                pl.BlockSpec((group, width), lambda g, n: (g, 0)),
                part,
                part,
                part,
            ],
            out_specs=[
                pl.BlockSpec((None, tokens, 3 * group), lambda g, n: (g, 0, 0)),
                pl.BlockSpec((8, group), lambda g, n: (0, g)),
            ],
            scratch_shapes=[pltpu.VMEM((width, tokens), LOW)],
        ),
        out_shape=[
            jax.ShapeDtypeStruct((parts, tokens, 3 * group), LOW),
            jax.ShapeDtypeStruct((8, width), WIDE),
        ],
        cost_estimate=cost(9),
        compiler_params=pltpu.CompilerParams(vmem_limit_bytes=10 << 20),
        name="attention_back",
    )(length, attn_in, attn_out, query, key, value)


def to_columns(rows):
    short = 128 - rows.shape[0]
    padded = jnp.concatenate([rows, jnp.zeros((short, rows.shape[1]), rows.dtype)], axis=0)
    return padded.T


def word_columns(words_ref):
    columns = [to_columns(words_ref[k])[:, 0:1] for k in range(words_ref.shape[0])]
    return jnp.concatenate(columns, axis=0).astype(jnp.int32)


def is_word(where_wide, first_col):
    lanes = lax.broadcasted_iota(jnp.int32, (1, where_wide.shape[1]), 1) + first_col
    return where_wide == lanes


def stats_kernel(
    base_ref, rows_ref, words_ref, keys_ref, norms_ref, slots_ref, head_ref, first_ref,
    second_ref, proj_one_ref, proj_two_ref, stats_ref, ones_ref, twos_ref
):
    rows = rows_ref[...]
    pair = words_ref.shape[0]
    tokens = words_ref.shape[2]
    words = word_columns(words_ref)
    ones = product(rows, proj_one_ref[...]).astype(LOW)
    twos = product(rows, proj_two_ref[...]).astype(LOW)
    ones_ref[...] = ones
    twos_ref[...] = twos
    picked = jnp.zeros((rows.shape[0], 1), WIDE)
    sums = []
    for place, (left, words_w) in enumerate(
        ((rows, head_ref), (ones, first_ref), (twos, second_ref))
    ):
        columns = words_w.shape[1]
        tile = SECOND_TILE if columns % SECOND_TILE == 0 else columns
        total = jnp.zeros((rows.shape[0], tile), WIDE)
        chosen = jnp.zeros((rows.shape[0], tile), WIDE)
        where_wide = jnp.broadcast_to(words - base_ref[place], (rows.shape[0], tile))
        for start in range(0, columns, tile):
            logits = product(left, words_w[:, start : start + tile])
            total = total + jnp.exp(logits)
            chosen = jnp.where(is_word(where_wide, start), logits, chosen)
        sums.append(jnp.sum(total, axis=1, keepdims=True))
        picked = picked + jnp.sum(chosen, axis=1, keepdims=True)
    sums.append(picked)
    lanes = lax.broadcasted_iota(jnp.int32, (rows.shape[0], 128), 1)
    table = jnp.zeros((rows.shape[0], 128), WIDE)
    for place, column in enumerate(sums):
        table = jnp.where(lanes == place, column, table)
    slot_count = slots_ref.shape[1]
    scale = 1.0 / math.sqrt(rows.shape[1])
    for k in range(pair):
        keys = keys_ref[k]
        norms = norms_ref[k][:, 0:1]
        scored = product_nt(keys, rows[k * tokens : (k + 1) * tokens]) * scale
        scored = scored - norms * (0.5 * scale)
        ids = lax.broadcasted_iota(jnp.int32, scored.shape, 0)
        for m in range(slot_count):
            hit = ids == slots_ref[k, m : m + 1, :]
            stats_ref[k, m : m + 1, :] = jnp.sum(
                jnp.where(hit, scored, 0.0), axis=0, keepdims=True
            )
        stats_ref[k, slot_count : slot_count + 8, :] = table[k * tokens : (k + 1) * tokens].T[0:8]


def whole_spec(array):
    return pl.BlockSpec(array.shape, lambda *_: (0,) * array.ndim)


def word_stats(base, rows_all, words_f, key_block, norms, slots_t, weights, pair):
    sources, slot_count, tokens = slots_t.shape
    count = key_block.shape[1]
    width = rows_all.shape[1]
    chunk = pair * tokens
    ones = weights[3].shape[1]
    twos = weights[4].shape[1]
    return pl.pallas_call(
        stats_kernel,
        grid_spec=pltpu.PrefetchScalarGridSpec(
            num_scalar_prefetch=1,
            grid=(sources // pair,),
            in_specs=[
                pl.BlockSpec((chunk, width), lambda g, b: (g, 0)),
                pl.BlockSpec((pair, 1, tokens), lambda g, b: (g, 0, 0)),
                pl.BlockSpec((pair, count, width), lambda g, b: (g, 0, 0)),
                pl.BlockSpec((pair, count, 128), lambda g, b: (g, 0, 0)),
                pl.BlockSpec((pair, slot_count, tokens), lambda g, b: (g, 0, 0)),
            ]
            + [whole_spec(w) for w in weights],
            out_specs=[
                pl.BlockSpec((pair, slot_count + 8, tokens), lambda g, b: (g, 0, 0)),
                pl.BlockSpec((chunk, ones), lambda g, b: (g, 0)),
                pl.BlockSpec((chunk, twos), lambda g, b: (g, 0)),
            ],
        ),
        out_shape=[
            jax.ShapeDtypeStruct((sources, slot_count + 8, tokens), WIDE),
            jax.ShapeDtypeStruct((rows_all.shape[0], ones), LOW),
            jax.ShapeDtypeStruct((rows_all.shape[0], twos), LOW),
        ],
        cost_estimate=cost(13),
        name="word_stats",
    )(base, rows_all, words_f, key_block, norms, slots_t, *weights)


def word_grads_kernel(
    order_ref, base_ref, rows_ref, ones_ref, twos_ref, returned_ref, words_ref, keys_ref,
    slots_ref, head_ref, first_ref, second_ref, first_t_ref, second_t_ref, mixed_t_ref, *refs
):
    (
        mine_ref, other_ref, head_g_ref, first_g_ref, second_g_ref, back_ref, terms_scr, mixed_scr
    ) = refs[-8:]
    rows = rows_ref[...]
    pair = words_ref.shape[0]
    tokens = words_ref.shape[2]
    slot_count = slots_ref.shape[1]
    words = word_columns(words_ref)
    coefs = [to_columns(returned_ref[k, slot_count : slot_count + 8, :]) for k in range(pair)]
    coefs = jnp.concatenate(coefs, axis=0)
    weight = coefs[:, 0:1]
    in_first = (words >= base_ref[3]) & (words < base_ref[4])
    in_second = words >= base_ref[4]
    scales = (
        weight,
        jnp.where(in_first, weight, 0.0),
        jnp.where(in_second, weight, 0.0),
    )
    lefts = (rows, ones_ref[...], twos_ref[...])
    for place, (words_w, out_ref) in enumerate(
        ((head_ref, head_g_ref), (first_ref, first_g_ref), (second_ref, second_g_ref))
    ):
        columns = words_w.shape[1]
        tile = SECOND_TILE if columns % SECOND_TILE == 0 else columns
        where_wide = jnp.broadcast_to(words - base_ref[place], (rows.shape[0], tile))
        scale = scales[place]
        log_sum = coefs[:, place + 1 : place + 2] - jnp.log(scale)

        def one_tile(tile_w, start):
            logits = product(lefts[place], tile_w)
            hit = is_word(where_wide, start)
            return (jnp.exp(logits - log_sum) - jnp.where(hit, scale, 0.0)).astype(LOW)

        if columns == tile:
            out_ref[...] = one_tile(words_w[...], 0)
        else:

            for start in range(0, columns, tile):
                out_ref[:, start : start + tile] = one_tile(
                    words_w[:, start : start + tile], start
                )

    ones = ones_ref.shape[1]
    heads = head_g_ref.shape[1]
    mixed_scr[:, ones : ones + heads] = head_g_ref[...]
    back_one = product(first_g_ref[...], first_t_ref[...]).astype(LOW)
    mixed_scr[:, 0:ones] = back_one
    back_ref[:, 0:ones] = back_one
    back_two = product(second_g_ref[...], second_t_ref[...]).astype(LOW)
    mixed_scr[:, ones + heads :] = back_two
    back_ref[:, ones:] = back_two
    term = product(mixed_scr[...], mixed_t_ref[...])
    key_scale = 1.0 / math.sqrt(rows.shape[1])
    count = keys_ref.shape[1]
    ids = lax.broadcasted_iota(jnp.int32, (count, tokens), 0)
    for k in range(pair):
        dense = jnp.zeros((count, tokens), WIDE)
        for m in range(slot_count):
            hit = ids == slots_ref[k, m : m + 1, :]
            dense = jnp.where(hit, returned_ref[k, m : m + 1, :], dense)
        near = product_tn(dense.astype(LOW), keys_ref[k]) * key_scale
        terms_scr[k] = (term[k * tokens : (k + 1) * tokens] + near).astype(LOW)
    if pair == 2:
        core = base_ref[5]
        mine_ref[0] = terms_scr[core]
        other_ref[0] = terms_scr[1 - core]
    else:
        mine_ref[0] = terms_scr[0]
        other_ref[0] = terms_scr[0]


def word_grads(order, base, rows_all, ones_all, twos_all, returned, words_f, key_block, slots_t,
               weights, pair):
    sources, slot_count, tokens = slots_t.shape
    count = key_block.shape[1]
    width = rows_all.shape[1]
    chunk = pair * tokens
    total = rows_all.shape[0]
    steps = order.shape[0]
    sizes = [weights[k].shape[1] for k in range(3)]
    sizes.append(weights[5].shape[0] - sizes[0])

    def by_row(columns):
        return pl.BlockSpec((chunk, columns), lambda g, o, b: (o[g], 0))

    inputs = [rows_all, ones_all, twos_all, returned, words_f, key_block, slots_t, *weights]
    return pl.pallas_call(
        word_grads_kernel,
        grid_spec=pltpu.PrefetchScalarGridSpec(
            num_scalar_prefetch=2,
            grid=(steps,),
            in_specs=[
                by_row(width),
                by_row(ones_all.shape[1]),
                by_row(twos_all.shape[1]),
                pl.BlockSpec((pair, slot_count + 8, tokens), lambda g, o, b: (o[g], 0, 0)),
                pl.BlockSpec((pair, 1, tokens), lambda g, o, b: (o[g], 0, 0)),
                pl.BlockSpec((pair, count, width), lambda g, o, b: (o[g], 0, 0)),
                pl.BlockSpec((pair, slot_count, tokens), lambda g, o, b: (o[g], 0, 0)),
            ]
            + [whole_spec(w) for w in weights],
            out_specs=[
                pl.BlockSpec((1, tokens, width), lambda g, o, b: (g, 0, 0)),
                pl.BlockSpec((1, tokens, width), lambda g, o, b: (g, 0, 0)),
            ]
            + [by_row(size) for size in sizes],
            scratch_shapes=[
                pltpu.VMEM((pair, tokens, width), LOW),
                pltpu.VMEM((chunk, weights[5].shape[0]), LOW),
            ],
        ),
        out_shape=[
            jax.ShapeDtypeStruct((steps, tokens, width), LOW),
            jax.ShapeDtypeStruct((steps, tokens, width), LOW),
        ]
        + [jax.ShapeDtypeStruct((total, size), LOW) for size in sizes],
        cost_estimate=cost(10),
        name="word_grads",
    )(order, base, *inputs)


def word_sums_kernel(
    rows_ref, ones_ref, twos_ref, head_g_ref, first_g_ref, second_g_ref, back_ref,
    packed_ref, proj_ref, *scratch
):
    step = pl.program_id(0)
    pairs = (
        (head_g_ref, rows_ref),
        (ones_ref, first_g_ref),
        (twos_ref, second_g_ref),
        (rows_ref, back_ref),
    )

    @pl.when(step == 0)
    def _():
        for acc in scratch:
            acc[...] = jnp.zeros_like(acc)

    for (left, right), acc in zip(pairs, scratch):
        acc[...] += product_tn(left[...], right[...])

    @pl.when(step == pl.num_programs(0) - 1)
    def _():
        proj_ref[...] = scratch[3][...].astype(LOW)
        place = 0
        for acc in scratch[:3]:
            rows, columns = acc.shape
            for start in range(0, columns, 128):
                packed_ref[place : place + rows, :] = acc[:, start : start + 128].astype(LOW)
                place += rows


def word_sums(rows_all, ones_all, twos_all, grads):
    total = rows_all.shape[0]
    chunk = min(512, total)
    inputs = [rows_all, ones_all, twos_all, *grads]
    shapes = [
        (grads[0].shape[1], rows_all.shape[1]),
        (ones_all.shape[1], grads[1].shape[1]),
        (twos_all.shape[1], grads[2].shape[1]),
        (rows_all.shape[1], grads[3].shape[1]),
    ]
    packed_rows = sum(rows * columns for rows, columns in shapes[:3]) // 128
    out_shapes = [(packed_rows, 128), shapes[3]]
    packed, proj = pl.pallas_call(
        word_sums_kernel,
        grid=(total // chunk,),
        in_specs=[pl.BlockSpec((chunk, item.shape[1]), lambda g: (g, 0)) for item in inputs],
        out_specs=[pl.BlockSpec(shape, lambda g: (0, 0)) for shape in out_shapes],
        out_shape=[jax.ShapeDtypeStruct(shape, LOW) for shape in out_shapes],
        scratch_shapes=[pltpu.VMEM(shape, WIDE) for shape in shapes],
        cost_estimate=cost(10),
        name="word_sums",
    )(*inputs)
    return packed, proj, shapes[:3]


def unpack_kernel(me_ref, parts_ref, *outs):
    count, part_rows, _ = parts_ref.shape
    me = me_ref[0]
    place = 0
    for out in outs:
        rows, columns = out.shape
        for start in range(0, columns, 128):
            done = 0
            while done < rows:
                part, offset = divmod(place + done, part_rows)
                size = min(rows - done, part_rows - offset)
                out[done : done + size, start : start + 128] = parts_ref[
                    part ^ me, offset : offset + size, :
                ].astype(WIDE)
                done += size
            place += rows


def unpack_words(parts, shapes):
    return pl.pallas_call(
        unpack_kernel,
        grid_spec=pltpu.PrefetchScalarGridSpec(
            num_scalar_prefetch=1,
            grid=(1,),
            in_specs=[whole_spec(parts)],
            out_specs=[pl.BlockSpec(shape, lambda *_: (0, 0)) for shape in shapes],
        ),
        out_shape=[jax.ShapeDtypeStruct(shape, WIDE) for shape in shapes],
        cost_estimate=cost(3),
        compiler_params=pltpu.CompilerParams(vmem_limit_bytes=12 << 20),
        name="unpack_words",
    )(lax.axis_index("dp").astype(jnp.int32).reshape(1), parts)


def key_norms_kernel(keys_ref, norms_ref):
    for k in range(keys_ref.shape[0]):
        wide = keys_ref[k].astype(WIDE)
        norms = jnp.sum(wide * wide, axis=1, keepdims=True)
        norms_ref[k] = jnp.broadcast_to(norms, norms_ref.shape[1:])


def key_norms(key_block):
    sources, count, width = key_block.shape
    pair = min(2, sources)
    return pl.pallas_call(
        key_norms_kernel,
        grid=(sources // pair,),
        in_specs=[pl.BlockSpec((pair, count, width), lambda g: (g, 0, 0))],
        out_specs=pl.BlockSpec((pair, count, 128), lambda g: (g, 0, 0)),
        out_shape=jax.ShapeDtypeStruct((sources, count, 128), WIDE),
        cost_estimate=cost(20),
        compiler_params=pltpu.CompilerParams(vmem_limit_bytes=8 << 20),
        name="key_norms",
    )(key_block)


def input_back_kernel(
    parts_ref, qkv_ref, in_ref, grad_ref, gains_ref, input_grad_ref, sums_ref, acc_scr
):
    step = pl.program_id(0)

    @pl.when(step == 0)
    def _():
        acc_scr[...] = jnp.zeros_like(acc_scr)

    group = qkv_ref.shape[2]
    total = acc_scr[...]
    for kind in range(3):
        total = total + product(
            qkv_ref[kind], parts_ref[:, kind * group : (kind + 1) * group].T
        )
    acc_scr[...] = total

    @pl.when(step == pl.num_programs(0) - 1)
    def _():
        unit_rows, inverse = norm_stats(in_ref[...].astype(WIDE))
        back, gain, shift = norm_backward(acc_scr[...].T, unit_rows, inverse, gains_ref[0:1])
        input_grad_ref[...] = grad_ref[...] + back
        sums_ref[0:1] = gain
        sums_ref[1:2] = shift


def input_back(parts, attn_qkv, inputs, first_grad, gains):
    count, tokens, _ = parts.shape
    width = inputs.shape[1]
    group = width // count
    full = pl.BlockSpec((tokens, width), lambda g: (0, 0))
    return pl.pallas_call(
        input_back_kernel,
        grid=(count,),
        in_specs=[
            pl.BlockSpec((None, tokens, 3 * group), lambda g: (g, 0, 0)),
            pl.BlockSpec((3, width, group), lambda g: (0, 0, g)),
            full,
            full,
            pl.BlockSpec(gains.shape, lambda g: (0, 0)),
        ],
        out_specs=[full, pl.BlockSpec((8, width), lambda g: (0, 0))],
        out_shape=[
            jax.ShapeDtypeStruct((tokens, width), WIDE),
            jax.ShapeDtypeStruct((8, width), WIDE),
        ],
        scratch_shapes=[pltpu.VMEM((width, tokens), WIDE)],
        cost_estimate=cost(7),
        compiler_params=pltpu.CompilerParams(vmem_limit_bytes=12 << 20),
        name="input_back",
    )(parts, attn_qkv, inputs, first_grad, gains)


def shards(
    inputs,
    lengths,
    targets,
    attn_qkv,
    attn_out,
    ffn_up,
    ffn_down,
    norm_gains,
    norm_shifts,
    biases,
    up_bias,
    cluster_proj,
    proj_first,
    proj_second,
    head_words,
    tail_first,
    tail_second,
    store_keys,
    block_rows,
    near_slots,
    near_words,
):
    tokens_here = inputs.shape[0]
    d_model = inputs.shape[1]
    dp_count = lax.axis_size("dp")
    sources = lax.axis_size("line") * 2
    my_index = lax.axis_index("line") * 2 + lax.axis_index("core")
    group_rows = tokens_here * sources
    head_cols = head_words.shape[1]
    first_cols = tail_first.shape[1]
    second_cols = tail_second.shape[1]
    head_total = head_cols * sources
    first_total = first_cols * sources
    ff_width = ffn_up.shape[1]
    valid_mask = (jnp.arange(tokens_here) < lengths[0]).astype(WIDE)

    (
        query_low, key_low, value_low, mixed_low, normed_low, first_sum, second_low, act_low,
        second_sum, hidden_low
    ) = block_forward(
        lengths, inputs, attn_qkv, attn_out, ffn_up, ffn_down, up_bias, norm_gains, norm_shifts,
        biases
    )
    cluster_logits = lax.dot_general(
        cluster_proj, hidden_low, (((0,), (1,)), ((), ())), preferred_element_type=WIDE
    )

    rows_all = lax.all_gather(hidden_low, STORE, axis=0, tiled=True)

    key_block = jnp.take(store_keys, block_rows[0, 0].reshape(-1), axis=0, mode="clip")
    key_block = key_block.reshape(sources, -1, d_model)
    slots_t = near_slots[0, 0].transpose(1, 2, 0)
    slot_count = slots_t.shape[1]
    words_t = near_words.T

    weights = (head_words, tail_first, tail_second, proj_first, proj_second)
    back_weights = weights[:3] + (
        tail_first.T,
        tail_second.T,
        jnp.concatenate([proj_first.T, head_words.T, proj_second.T], axis=0),
    )
    norms = key_norms(key_block)

    left_low = jnp.concatenate([act_low, second_low, mixed_low, normed_low], axis=1)
    late_weights = back_weights[3:]
    left_low, rows_all, norms, slots_t, words_t, late_weights = lax.optimization_barrier(
        (left_low, rows_all, norms, slots_t, words_t, late_weights)
    )
    back_weights = weights[:3] + late_weights
    left_all = lax.all_gather(left_low, "dp", axis=0, tiled=True)

    core = lax.axis_index("core")
    words_f = targets.astype(WIDE).reshape(sources, 1, tokens_here)
    base = jnp.stack(
        [
            my_index * head_cols,
            head_total + my_index * first_cols,
            head_total + first_total + my_index * second_cols,
            jnp.int32(head_total),
            jnp.int32(head_total + first_total),
            core,
        ]
    ).astype(jnp.int32)
    outgoing, ones_all, twos_all = word_stats(
        base, rows_all, words_f, key_block, norms, slots_t, back_weights[:3] + weights[3:], 4
    )
    incoming = lax.all_to_all(outgoing, STORE, 0, 0)

    near_scores = incoming[:, :slot_count].reshape(sources * slot_count, tokens_here)
    own_stats = jnp.sum(incoming[:, slot_count : slot_count + 4], axis=0)
    own_words = lax.dynamic_slice_in_dim(targets, my_index * tokens_here, tokens_here, 0)
    in_first = ((own_words >= head_total) & (own_words < head_total + first_total)).astype(WIDE)
    in_second = (own_words >= head_total + first_total).astype(WIDE)
    head_sum = own_stats[0] + jnp.sum(jnp.exp(cluster_logits), axis=0)
    log_head = jnp.log(head_sum)
    log_first = jnp.log(own_stats[1])
    log_second = jnp.log(own_stats[2])
    log_model = (
        own_stats[3]
        - log_head
        + in_first * (cluster_logits[0] - log_first)
        + in_second * (cluster_logits[1] - log_second)
    )
    near_top = jnp.max(near_scores, axis=0, keepdims=True)
    near_exp = jnp.exp(near_scores - near_top)
    near_probs = near_exp / jnp.sum(near_exp, axis=0, keepdims=True)
    matched = (words_t == own_words[None, :]).astype(WIDE)
    near_mass = jnp.sum(near_probs * matched, axis=0)
    model_prob = jnp.exp(log_model)
    mixture = NEAR_WEIGHT * near_mass + (1.0 - NEAR_WEIGHT) * model_prob
    token_loss = -valid_mask * jnp.log(mixture)
    model_weight = valid_mask * (1.0 - NEAR_WEIGHT) * model_prob / mixture
    near_weight = valid_mask * NEAR_WEIGHT / mixture
    score_grad = -near_weight[None, :] * near_probs * (matched - near_mass[None, :])
    coef = jnp.stack([model_weight, log_head, log_first, log_second] + 4 * [model_weight])
    returning = jnp.concatenate(
        [
            score_grad.reshape(sources, slot_count, tokens_here),
            jnp.broadcast_to(coef[None], (sources,) + coef.shape),
        ],
        axis=1,
    )
    returned = lax.all_to_all(returning, STORE, 0, 0)

    lines = lax.axis_size("line")
    mine, other, *word_terms = word_grads(
        jnp.arange(lines, dtype=jnp.int32),
        base,
        rows_all,
        ones_all,
        twos_all,
        returned,
        words_f,
        key_block,
        slots_t,
        back_weights,
        2,
    )
    both = (mine.astype(WIDE) + swap_partner(other, "core", 1).astype(WIDE)).astype(LOW)
    row_parts = lax.all_to_all(both, "line", 0, 0)
    row_back = jnp.sum(row_parts.astype(WIDE), axis=0)
    word_terms, both = lax.optimization_barrier((word_terms, both))
    word_packed, proj_acc, word_shapes = word_sums(rows_all, ones_all, twos_all, word_terms)

    own_rows = d_model // sources
    proj_width = proj_acc.shape[1]
    sub_rows = own_rows // dp_count
    proj_parts = proj_acc.reshape(sources, dp_count, sub_rows, proj_width).transpose(1, 0, 2, 3)
    dp_index = lax.axis_index("dp")
    proj_sum = lax.dynamic_index_in_dim(proj_parts, dp_index, 0, keepdims=False).astype(WIDE)
    for q in range(1, dp_count):
        part = lax.dynamic_index_in_dim(proj_parts, dp_index ^ q, 0, keepdims=False)
        proj_sum = proj_sum + swap_partner(part, "dp", q).astype(WIDE)
    cluster_rows = model_weight[None, :] * (
        jnp.exp(cluster_logits - log_head[None, :]) - jnp.stack([in_first, in_second])
    )
    hidden_grad = row_back + lax.dot_general(
        cluster_rows, cluster_proj.astype(WIDE), (((0,), (1,)), ((), ())), precision=HIGH
    )
    cluster_acc = jnp.dot(cluster_rows, hidden_low.astype(WIDE), precision=HIGH)
    unit_three, inv_three = norm_stats(second_sum)
    second_grad, gain_three, shift_three = norm_backward(
        hidden_grad, unit_three, inv_three, norm_gains[2]
    )
    down_in = second_grad.astype(LOW)
    down_parts = exchange_columns(down_in)
    bias_down = jnp.sum(down_in.astype(WIDE), axis=0, keepdims=True)
    act_grad = product_nt(down_in, ffn_down)
    pre_grad = jnp.where(act_low.astype(WIDE) > 0, act_grad, 0.0).astype(LOW)
    up_bias_acc = jnp.sum(pre_grad.astype(WIDE), axis=0, keepdims=True)
    marks = [0, ff_width, ff_width + d_model, ff_width + 2 * d_model, ff_width + 3 * d_model]
    lefts = [left_all[:, a:b] for a, b in zip(marks[:-1], marks[1:])]
    down = Halving(grad_tile(lefts[0], after(down_parts, pre_grad)))
    norm_two_grad = product_nt(after(pre_grad, down.outgoing), ffn_up)
    unit_two, inv_two = norm_stats(first_sum)
    back_second, gain_two, shift_two = norm_backward(
        norm_two_grad, unit_two, inv_two, norm_gains[1]
    )
    first_grad_sum = second_grad + back_second
    attn_in = first_grad_sum.astype(LOW)
    bias_attn = jnp.sum(attn_in.astype(WIDE), axis=0, keepdims=True)
    mark = down.add(attn_in)
    up_width = ff_width // dp_count
    head_width = d_model // dp_count
    up_send = jnp.stack(
        [
            jnp.concatenate(
                [
                    pre_grad[:, k * up_width : (k + 1) * up_width],
                    attn_in[:, k * head_width : (k + 1) * head_width],
                ],
                axis=1,
            )
            for k in range(dp_count)
        ]
    )
    up_parts = lax.all_to_all(up_send, "dp", 0, 0)
    stacked_parts, sums_three = attention_back(
        lengths, after(attn_in, up_send, mark), attn_out, query_low, key_low, value_low, dp_count
    )
    mark = down.add(stacked_parts)
    qkv_parts = lax.all_to_all(after(stacked_parts, up_parts), "dp", 0, 0)
    word_send = after(word_packed.reshape(dp_count, -1, 128), qkv_parts)
    word_parts = lax.all_to_all(word_send, "dp", 0, 0)
    proj_rows = sub_rows * proj_width // (up_width + head_width)
    proj_block = proj_sum.astype(LOW).reshape(sources, proj_rows, up_width + head_width)
    up_parts = after(up_parts, mark)
    up = Halving(
        jnp.concatenate(
            [
                jnp.concatenate(
                    [
                        grad_tile(lefts[1], up_parts[:, :, :up_width]),
                        grad_tile(lefts[2], up_parts[:, :, up_width:]),
                    ],
                    axis=2,
                ),
                proj_block,
            ],
            axis=1,
        )
    )
    input_grad, sums_one = input_back(
        after(stacked_parts, up.outgoing, qkv_parts), attn_qkv, inputs, first_grad_sum, norm_gains
    )
    down_own = down.finish(input_grad)
    mark = up.add(input_grad, down_own)

    def by_store(value):
        rows = value.shape[0]
        return value.reshape(rows, sources, -1).transpose(1, 0, 2).reshape(sources, -1)

    small = jnp.concatenate(
        [
            by_store(jnp.concatenate([sums_one[0:1], gain_two, gain_three])),
            by_store(jnp.concatenate([sums_one[1:2], shift_two, shift_three])),
            by_store(jnp.concatenate([sums_three[0:1], sums_three[2:3], bias_attn, bias_down])),
            by_store(up_bias_acc),
            by_store(cluster_acc),
        ],
        axis=1,
    )
    small_count = small.shape[1]
    small_rows = -(-small_count // (3 * head_width))
    if own_rows % 128 == 0:
        small_rows = -(-small_rows // 8) * 8
    small = jnp.pad(small, ((0, 0), (0, small_rows * 3 * head_width - small_count)))
    small = small.reshape(sources, small_rows, 3 * head_width).astype(LOW)
    qkv = Halving(
        jnp.concatenate([grad_tile(lefts[3], after(qkv_parts, mark)), small], axis=1)
    )
    down_pieces = gather_dp(down_own)
    mark = qkv.add(qkv.outgoing)
    mark = up.add(mark)
    word_own = jnp.sum(after(word_parts, mark).astype(WIDE), axis=0).astype(LOW)
    mark = qkv.add(word_own)
    word_pieces = gather_dp(word_own)
    down_out = join_pieces(after(down_pieces, mark), 1, 0, head_width, 1)
    up_own = up.finish(down_out)
    up_pieces = gather_dp(up_own)
    word_pieces = after(word_pieces, up_own)
    head_t, first_out, second_out = unpack_words(jnp.stack(word_pieces), word_shapes)
    head_out = head_t.T
    qkv_own = qkv.finish(head_t)
    qkv_pieces = gather_dp(qkv_own)
    up_pieces = after(up_pieces, qkv_own)
    up_main = [piece[:own_rows] for piece in up_pieces]
    up_out = join_pieces(up_main, 1, 0, up_width, 1)
    out_out = join_pieces(up_main, 1, up_width, head_width, 1)
    proj_out = join_pieces(
        [piece[own_rows:].reshape(sub_rows, proj_width) for piece in up_pieces],
        0,
        0,
        sub_rows,
        0,
    )
    qkv_main = [piece[:own_rows] for piece in qkv_pieces]
    qkv_out = jnp.stack(
        [join_pieces(qkv_main, 1, kind * head_width, head_width, 1) for kind in range(3)]
    )
    small_sum = sum(piece[own_rows:].astype(WIDE) for piece in qkv_pieces).reshape(-1)
    sizes = [3 * own_rows, 3 * own_rows, 4 * own_rows, ff_width // sources, 2 * own_rows]
    ends = [0]
    for size in sizes:
        ends.append(ends[-1] + size)
    gains_out, shifts_out, biases_out, upb_out, cluster_out = (
        small_sum[a:b] for a, b in zip(ends[:-1], ends[1:])
    )
    return (
        token_loss,
        input_grad,
        qkv_out,
        out_out,
        up_out,
        down_out,
        gains_out.reshape(3, own_rows),
        shifts_out.reshape(3, own_rows),
        biases_out.reshape(4, own_rows),
        upb_out,
        cluster_out.reshape(2, own_rows).T,
        proj_out[:, : proj_first.shape[1]],
        proj_out[:, proj_first.shape[1] :],
        head_out,
        first_out,
        second_out,
    )


def solution(mesh):
    dp_count = mesh.shape["dp"]
    store_count = mesh.shape["store"]
    split = Mesh(mesh.devices.reshape(dp_count, store_count // 2, 2), ("dp",) + STORE)
    everyone = ("dp",) + STORE
    return jax.shard_map(
        shards,
        mesh=split,
        in_specs=(
            P(everyone, None),
            P(everyone),
            P("dp"),
            P(),
            P(),
            P(),
            P(),
            P(),
            P(),
            P(),
            P(),
            P(),
            P(),
            P(),
            P(None, STORE),
            P(None, STORE),
            P(None, STORE),
            P(STORE, None),
            P("dp", STORE, None, None),
            P("dp", STORE, None, None, None),
            P(everyone, None),
        ),
        out_specs=(
            P(everyone),
            P(everyone, None),
            P(None, STORE, None),
            P(STORE, None),
            P(STORE, None),
            P(STORE, None),
            P(None, STORE),
            P(None, STORE),
            P(None, STORE),
            P(STORE),
            P(STORE, None),
            P(STORE, None),
            P(STORE, None),
            P(None, STORE),
            P(None, STORE),
            P(None, STORE),
        ),
        check_vma=False,
    )
```

```python
import math

import jax
import jax.numpy as jnp
from jax import lax
from jax.experimental import pallas as pl
from jax.experimental.pallas import tpu as pltpu
from jax.sharding import Mesh
from jax.sharding import PartitionSpec as P

HEADS = 16
HD = 64


EPS = 1e-05
NEAR_WEIGHT = 0.25
NEG_FILL = -1e30
HIGH = lax.Precision.HIGHEST
STORE = ("line", "core")
LOW = jnp.bfloat16
WIDE = jnp.float32
SECOND_TILE = 256


def product(left, right):
    return jnp.dot(left, right, preferred_element_type=WIDE)


def product_tn(left, right):
    return lax.dot_general(left, right, (((0,), (0,)), ((), ())), preferred_element_type=WIDE)


def product_nt(left, right):
    return lax.dot_general(left, right, (((1,), (1,)), ((), ())), preferred_element_type=WIDE)


def norm_forward(values, gain_row, shift_row):
    row_mean = jnp.mean(values, axis=-1, keepdims=True)
    centred = values - row_mean
    inverse = lax.rsqrt(jnp.mean(centred * centred, axis=-1, keepdims=True) + EPS)
    unit_rows = centred * inverse
    return (unit_rows * gain_row + shift_row, unit_rows, inverse)


def norm_backward(grad_out, unit_rows, inverse, gain_row):
    scaled = grad_out * gain_row
    grad_in = inverse * (
        scaled
        - jnp.mean(scaled, axis=-1, keepdims=True)
        - unit_rows * jnp.mean(scaled * unit_rows, axis=-1, keepdims=True)
    )
    return (grad_in, jnp.sum(grad_out * unit_rows, axis=0, keepdims=True), jnp.sum(grad_out, axis=0, keepdims=True))


def swap_partner(value, axis, bit):
    count = lax.axis_size(axis)
    return lax.ppermute(value, axis, [(k, k ^ bit) for k in range(count)])


def after(value, *others):
    return lax.optimization_barrier((value, *others))[0]


class Halving:
    def __init__(self, blocks):
        lines = lax.axis_size("line")
        line = lax.axis_index("line")
        self.rest = blocks.shape[1:]
        self.current = blocks.reshape((lines, 2) + self.rest)
        self.steps = [(lax.axis_index("core"), "core", 1)]
        bit = 1
        while bit < lines:
            self.steps.append(((line // bit) & 1, "line", bit))
            bit *= 2
        self.received = None
        self.send()

    def send(self):
        mine, axis, bit = self.steps.pop(0)
        value = self.current
        outgoing = lax.dynamic_index_in_dim(value, 1 - mine, 1, keepdims=False).astype(LOW)
        self.outgoing = outgoing
        self.current = lax.dynamic_index_in_dim(value, mine, 1, keepdims=False)
        self.received = swap_partner(outgoing, axis, bit)

    def add(self, *others):
        received = after(self.received, *others) if others else self.received
        self.current = self.current.astype(WIDE) + received.astype(WIDE)
        if self.steps:
            self.current = self.current.reshape((-1, 2) + self.rest)
            self.send()
        return self.outgoing

    def finish(self, *others):
        while self.steps:
            self.add(*others)
        self.add(*others)
        return self.current[0].astype(LOW)


def grad_tile(left, right_parts):
    blocks = lax.axis_size("line") * 2
    right = right_parts.reshape(left.shape[0], right_parts.shape[2])
    tile = product_tn(left, right).astype(LOW)
    return tile.reshape(blocks, -1, right.shape[1])


def gather_dp(own):
    count = lax.axis_size("dp")
    return [own] + [swap_partner(own, "dp", q) for q in range(1, count)]


def join_pieces(pieces, axis, start, width, join_axis):
    count = len(pieces)
    me = lax.axis_index("dp")
    pieces = [lax.slice_in_dim(piece, start, start + width, axis=axis) for piece in pieces]
    bit = 1
    while bit < count:
        is_set = (me // bit) & 1 == 1
        pieces = [jnp.where(is_set, pieces[k ^ bit], pieces[k]) for k in range(count)]
        bit *= 2
    return jnp.concatenate([piece.astype(WIDE) for piece in pieces], axis=join_axis)


def exchange_columns(value):
    count = lax.axis_size("dp")
    tokens, columns = value.shape
    parts = value.reshape(tokens, count, columns // count).transpose(1, 0, 2)
    return lax.all_to_all(parts, "dp", 0, 0)


def cost(micros):
    return pl.CostEstimate(flops=int(micros * 9e8), transcendentals=0, bytes_accessed=1 << 20)


def head_masks(width):
    lanes = lax.broadcasted_iota(jnp.int32, (1, width), 1)
    return [(lanes // HD) % 2 == half for half in range(2)]


def masked_softmax(scores, allowed):
    scores = jnp.where(allowed, scores * HD ** (-0.5), NEG_FILL)
    exps = jnp.exp(scores - jnp.max(scores, axis=-1, keepdims=True))
    return exps / jnp.sum(exps, axis=-1, keepdims=True)


def seen_keys(tokens, length):
    rows = lax.broadcasted_iota(jnp.int32, (tokens, tokens), 0)
    cols = lax.broadcasted_iota(jnp.int32, (tokens, tokens), 1)
    return (cols <= rows) & (cols < length)


def block_kernel(
    length_ref, in_ref, qkv_ref, out_w_ref, up_bias_ref, gains_ref, shifts_ref, biases_ref,
    group_bias_ref, up_hbm, down_hbm,
    query_ref, key_ref, value_ref, mixed_ref, normed_ref, first_ref, second_ref, act_ref, sum_ref,
    hidden_ref, acc_scr, up_scr, down_scr, sems
):
    step = pl.program_id(0)
    tokens, width = in_ref.shape
    group = query_ref.shape[1]
    groups = width // group
    blocks = up_scr.shape[0]
    block = up_scr.shape[2]

    def fetches(place):
        start = place * block
        return (
            pltpu.make_async_copy(
                up_hbm.at[:, pl.ds(start, block)], up_scr.at[place], sems.at[0, place]
            ),
            pltpu.make_async_copy(
                down_hbm.at[pl.ds(start, block), :], down_scr.at[place], sems.at[1, place]
            ),
        )

    @pl.when(step == 0)
    def _():
        for place in range(blocks):
            for fetch in fetches(place):
                fetch.start()
        block_in = in_ref[...].astype(WIDE)
        normed_ref[...] = norm_forward(block_in, gains_ref[0:1], shifts_ref[0:1])[0].astype(LOW)
        acc_scr[...] = block_in + biases_ref[2:3]

    @pl.when(step < groups)
    def _():
        normed = normed_ref[...]
        query = (product(normed, qkv_ref[0]) + group_bias_ref[0:1]).astype(LOW)
        key = product(normed, qkv_ref[1]).astype(LOW)
        value = (product(normed, qkv_ref[2]) + group_bias_ref[1:2]).astype(LOW)
        query_ref[...] = query
        key_ref[...] = key
        value_ref[...] = value
        allowed = seen_keys(tokens, length_ref[0])
        masks = head_masks(128)
        zero = jnp.zeros((tokens, 128), LOW)
        for pair in range(group // 128):
            cols = slice(pair * 128, (pair + 1) * 128)
            q_pair, k_pair, v_pair = query[:, cols], key[:, cols], value[:, cols]
            mixed = jnp.zeros((tokens, 128), WIDE)
            for mask in masks:
                probs = masked_softmax(product_nt(q_pair, jnp.where(mask, k_pair, zero)), allowed)
                mixed = mixed + product(probs.astype(LOW), jnp.where(mask, v_pair, zero))
            mixed_ref[:, cols] = mixed.astype(LOW)
        acc_scr[...] += product(mixed_ref[...], out_w_ref[...])

    @pl.when(step == groups - 1)
    def _():
        first_sum = acc_scr[...]
        first_ref[...] = first_sum
        second_ref[...] = norm_forward(first_sum, gains_ref[1:2], shifts_ref[1:2])[0].astype(LOW)
        acc_scr[...] = first_sum + biases_ref[3:4]

    @pl.when(step >= groups)
    def _():
        place = step - groups
        for fetch in fetches(place):
            fetch.wait()
        pre_act = product(second_ref[...], up_scr[place]) + up_bias_ref[...]
        act = jnp.maximum(pre_act, 0.0).astype(LOW)
        act_ref[...] = act
        acc_scr[...] += product(act, down_scr[place])

    @pl.when(step == pl.num_programs(0) - 1)
    def _():
        total = acc_scr[...]
        sum_ref[...] = total
        hidden_ref[...] = norm_forward(total, gains_ref[2:3], shifts_ref[2:3])[0].astype(LOW)


def block_forward(
    length, inputs, attn_qkv, attn_out, ffn_up, ffn_down, up_bias, gains, shifts, biases
):
    tokens, width = inputs.shape
    inner = ffn_up.shape[1]
    group = min(256, width)
    groups = width // group
    block = min(1024, inner)
    blocks = inner // block
    full = pl.BlockSpec((tokens, width), lambda g, n: (0, 0))
    part = pl.BlockSpec((tokens, group), lambda g, n: (0, jnp.minimum(g, groups - 1)))
    low = jax.ShapeDtypeStruct((tokens, width), LOW)
    wide = jax.ShapeDtypeStruct((tokens, width), WIDE)
    return pl.pallas_call(
        block_kernel,
        grid_spec=pltpu.PrefetchScalarGridSpec(
            num_scalar_prefetch=1,
            grid=(groups + blocks,),
            in_specs=[
                full,
                pl.BlockSpec((3, width, group), lambda g, n: (0, 0, jnp.minimum(g, groups - 1))),
                pl.BlockSpec((group, width), lambda g, n: (jnp.minimum(g, groups - 1), 0)),
                pl.BlockSpec((1, block), lambda g, n: (0, jnp.maximum(g - groups, 0))),
                pl.BlockSpec(gains.shape, lambda g, n: (0, 0)),
                pl.BlockSpec(shifts.shape, lambda g, n: (0, 0)),
                pl.BlockSpec(biases.shape, lambda g, n: (0, 0)),
                pl.BlockSpec(
                    (biases.shape[0], group), lambda g, n: (0, jnp.minimum(g, groups - 1))
                ),
                pl.BlockSpec(memory_space=pl.ANY),
                pl.BlockSpec(memory_space=pl.ANY),
            ],
            out_specs=[part, part, part, part, full, full, full]
            + [pl.BlockSpec((tokens, block), lambda g, n: (0, jnp.maximum(g - groups, 0)))]
            + [full, full],
            scratch_shapes=[
                pltpu.VMEM((tokens, width), WIDE),
                pltpu.VMEM((blocks, width, block), LOW),
                pltpu.VMEM((blocks, block, width), LOW),
                pltpu.SemaphoreType.DMA((2, blocks)),
            ],
        ),
        out_shape=[low, low, low, low, low, wide, low]
        + [jax.ShapeDtypeStruct((tokens, inner), LOW), wide, low],
        cost_estimate=cost(16),
        name="block_forward",
    )(
        length, inputs, attn_qkv, attn_out, up_bias.reshape(1, inner), gains, shifts, biases,
        biases, ffn_up, ffn_down
    )


def norm_stats(values):
    centred = values - jnp.mean(values, axis=-1, keepdims=True)
    inverse = lax.rsqrt(jnp.mean(centred * centred, axis=-1, keepdims=True) + EPS)
    return centred * inverse, inverse


def attention_back_kernel(
    length_ref, attn_in_ref, out_w_ref, query_ref, key_ref, value_ref, parts_ref, sums_ref,
    attn_t_scr
):
    tokens = attn_in_ref.shape[0]
    width = query_ref.shape[1]

    @pl.when(pl.program_id(0) == 0)
    def _():
        attn_t_scr[...] = attn_in_ref[...].T

    mixed_grad = product(out_w_ref[...], attn_t_scr[...]).T.astype(LOW)
    allowed = seen_keys(tokens, length_ref[0])
    masks = head_masks(128)
    zero = jnp.zeros((tokens, 128), LOW)
    for pair in range(width // 128):
        cols = slice(pair * 128, (pair + 1) * 128)
        q_pair, k_pair, v_pair = query_ref[:, cols], key_ref[:, cols], value_ref[:, cols]
        m_pair = mixed_grad[:, cols]
        totals = [jnp.zeros((tokens, 128), WIDE) for _ in range(3)]
        for mask in masks:
            k_one = jnp.where(mask, k_pair, zero)
            probs = masked_softmax(product_nt(q_pair, k_one), allowed)
            prob_grad = product_nt(m_pair, jnp.where(mask, v_pair, zero))
            delta = jnp.sum(probs * prob_grad, axis=-1, keepdims=True)
            score_grad = (probs * (prob_grad - delta)).astype(LOW)
            totals[0] += product(score_grad, k_one)
            totals[1] += product_tn(score_grad, jnp.where(mask, q_pair, zero))
            totals[2] += product_tn(probs.astype(LOW), jnp.where(mask, m_pair, zero))
        for kind, total in enumerate(totals):
            scale = HD ** (-0.5) if kind < 2 else 1.0
            grad = (total * scale).astype(LOW)
            parts_ref[:, kind * width + pair * 128 : kind * width + (pair + 1) * 128] = grad
            if kind != 1:
                sums_ref[kind : kind + 1, cols] = jnp.sum(
                    grad.astype(WIDE), axis=0, keepdims=True
                )


def attention_back(length, attn_in, attn_out, query, key, value, parts):
    tokens, width = attn_in.shape
    group = width // parts
    part = pl.BlockSpec((tokens, group), lambda g, n: (0, g))
    return pl.pallas_call(
        attention_back_kernel,
        grid_spec=pltpu.PrefetchScalarGridSpec(
            num_scalar_prefetch=1,
            grid=(parts,),
            in_specs=[
                pl.BlockSpec((tokens, width), lambda g, n: (0, 0)),
                pl.BlockSpec((group, width), lambda g, n: (g, 0)),
                part,
                part,
                part,
            ],
            out_specs=[
                pl.BlockSpec((None, tokens, 3 * group), lambda g, n: (g, 0, 0)),
                pl.BlockSpec((8, group), lambda g, n: (0, g)),
            ],
            scratch_shapes=[pltpu.VMEM((width, tokens), LOW)],
        ),
        out_shape=[
            jax.ShapeDtypeStruct((parts, tokens, 3 * group), LOW),
            jax.ShapeDtypeStruct((8, width), WIDE),
        ],
        cost_estimate=cost(9),
        compiler_params=pltpu.CompilerParams(vmem_limit_bytes=10 << 20),
        name="attention_back",
    )(length, attn_in, attn_out, query, key, value)


def to_columns(rows):
    short = 128 - rows.shape[0]
    padded = jnp.concatenate([rows, jnp.zeros((short, rows.shape[1]), rows.dtype)], axis=0)
    return padded.T


def word_columns(words_ref):
    columns = [to_columns(words_ref[k])[:, 0:1] for k in range(words_ref.shape[0])]
    return jnp.concatenate(columns, axis=0).astype(jnp.int32)


def is_word(where_wide, first_col):
    lanes = lax.broadcasted_iota(jnp.int32, (1, where_wide.shape[1]), 1) + first_col
    return where_wide == lanes


def stats_kernel(
    base_ref, rows_ref, words_ref, keys_ref, norms_ref, slots_ref, head_ref, first_ref,
    second_ref, proj_one_ref, proj_two_ref, stats_ref, ones_ref, twos_ref
):
    rows = rows_ref[...]
    pair = words_ref.shape[0]
    tokens = words_ref.shape[2]
    words = word_columns(words_ref)
    ones = product(rows, proj_one_ref[...]).astype(LOW)
    twos = product(rows, proj_two_ref[...]).astype(LOW)
    ones_ref[...] = ones
    twos_ref[...] = twos
    picked = jnp.zeros((rows.shape[0], 1), WIDE)
    sums = []
    for place, (left, words_w) in enumerate(
        ((rows, head_ref), (ones, first_ref), (twos, second_ref))
    ):
        columns = words_w.shape[1]
        tile = SECOND_TILE if columns % SECOND_TILE == 0 else columns
        total = jnp.zeros((rows.shape[0], tile), WIDE)
        chosen = jnp.zeros((rows.shape[0], tile), WIDE)
        where_wide = jnp.broadcast_to(words - base_ref[place], (rows.shape[0], tile))
        for start in range(0, columns, tile):
            logits = product(left, words_w[:, start : start + tile])
            total = total + jnp.exp(logits)
            chosen = jnp.where(is_word(where_wide, start), logits, chosen)
        sums.append(jnp.sum(total, axis=1, keepdims=True))
        picked = picked + jnp.sum(chosen, axis=1, keepdims=True)
    sums.append(picked)
    lanes = lax.broadcasted_iota(jnp.int32, (rows.shape[0], 128), 1)
    table = jnp.zeros((rows.shape[0], 128), WIDE)
    for place, column in enumerate(sums):
        table = jnp.where(lanes == place, column, table)
    slot_count = slots_ref.shape[1]
    scale = 1.0 / math.sqrt(rows.shape[1])
    for k in range(pair):
        keys = keys_ref[k]
        norms = norms_ref[k][:, 0:1]
        scored = product_nt(keys, rows[k * tokens : (k + 1) * tokens]) * scale
        scored = scored - norms * (0.5 * scale)
        ids = lax.broadcasted_iota(jnp.int32, scored.shape, 0)
        for m in range(slot_count):
            hit = ids == slots_ref[k, m : m + 1, :]
            stats_ref[k, m : m + 1, :] = jnp.sum(
                jnp.where(hit, scored, 0.0), axis=0, keepdims=True
            )
        stats_ref[k, slot_count : slot_count + 8, :] = table[k * tokens : (k + 1) * tokens].T[0:8]


def whole_spec(array):
    return pl.BlockSpec(array.shape, lambda *_: (0,) * array.ndim)


def word_stats(base, rows_all, words_f, key_block, norms, slots_t, weights, pair):
    sources, slot_count, tokens = slots_t.shape
    count = key_block.shape[1]
    width = rows_all.shape[1]
    chunk = pair * tokens
    ones = weights[3].shape[1]
    twos = weights[4].shape[1]
    return pl.pallas_call(
        stats_kernel,
        grid_spec=pltpu.PrefetchScalarGridSpec(
            num_scalar_prefetch=1,
            grid=(sources // pair,),
            in_specs=[
                pl.BlockSpec((chunk, width), lambda g, b: (g, 0)),
                pl.BlockSpec((pair, 1, tokens), lambda g, b: (g, 0, 0)),
                pl.BlockSpec((pair, count, width), lambda g, b: (g, 0, 0)),
                pl.BlockSpec((pair, count, 128), lambda g, b: (g, 0, 0)),
                pl.BlockSpec((pair, slot_count, tokens), lambda g, b: (g, 0, 0)),
            ]
            + [whole_spec(w) for w in weights],
            out_specs=[
                pl.BlockSpec((pair, slot_count + 8, tokens), lambda g, b: (g, 0, 0)),
                pl.BlockSpec((chunk, ones), lambda g, b: (g, 0)),
                pl.BlockSpec((chunk, twos), lambda g, b: (g, 0)),
            ],
        ),
        out_shape=[
            jax.ShapeDtypeStruct((sources, slot_count + 8, tokens), WIDE),
            jax.ShapeDtypeStruct((rows_all.shape[0], ones), LOW),
            jax.ShapeDtypeStruct((rows_all.shape[0], twos), LOW),
        ],
        cost_estimate=cost(13),
        name="word_stats",
    )(base, rows_all, words_f, key_block, norms, slots_t, *weights)


def word_grads_kernel(
    order_ref, base_ref, rows_ref, ones_ref, twos_ref, returned_ref, words_ref, keys_ref,
    slots_ref, head_ref, first_ref, second_ref, first_t_ref, second_t_ref, mixed_t_ref, *refs
):
    (
        mine_ref, other_ref, head_g_ref, first_g_ref, second_g_ref, back_ref, terms_scr, mixed_scr
    ) = refs[-8:]
    rows = rows_ref[...]
    pair = words_ref.shape[0]
    tokens = words_ref.shape[2]
    slot_count = slots_ref.shape[1]
    words = word_columns(words_ref)
    coefs = [to_columns(returned_ref[k, slot_count : slot_count + 8, :]) for k in range(pair)]
    coefs = jnp.concatenate(coefs, axis=0)
    weight = coefs[:, 0:1]
    in_first = (words >= base_ref[3]) & (words < base_ref[4])
    in_second = words >= base_ref[4]
    scales = (
        weight,
        jnp.where(in_first, weight, 0.0),
        jnp.where(in_second, weight, 0.0),
    )
    lefts = (rows, ones_ref[...], twos_ref[...])
    for place, (words_w, out_ref) in enumerate(
        ((head_ref, head_g_ref), (first_ref, first_g_ref), (second_ref, second_g_ref))
    ):
        columns = words_w.shape[1]
        tile = SECOND_TILE if columns % SECOND_TILE == 0 else columns
        where_wide = jnp.broadcast_to(words - base_ref[place], (rows.shape[0], tile))
        scale = scales[place]
        log_sum = coefs[:, place + 1 : place + 2] - jnp.log(scale)

        def one_tile(tile_w, start):
            logits = product(lefts[place], tile_w)
            hit = is_word(where_wide, start)
            return (jnp.exp(logits - log_sum) - jnp.where(hit, scale, 0.0)).astype(LOW)

        if columns == tile:
            out_ref[...] = one_tile(words_w[...], 0)
        else:

            for start in range(0, columns, tile):
                out_ref[:, start : start + tile] = one_tile(
                    words_w[:, start : start + tile], start
                )

    ones = ones_ref.shape[1]
    heads = head_g_ref.shape[1]
    mixed_scr[:, ones : ones + heads] = head_g_ref[...]
    back_one = product(first_g_ref[...], first_t_ref[...]).astype(LOW)
    mixed_scr[:, 0:ones] = back_one
    back_ref[:, 0:ones] = back_one
    back_two = product(second_g_ref[...], second_t_ref[...]).astype(LOW)
    mixed_scr[:, ones + heads :] = back_two
    back_ref[:, ones:] = back_two
    term = product(mixed_scr[...], mixed_t_ref[...])
    key_scale = 1.0 / math.sqrt(rows.shape[1])
    count = keys_ref.shape[1]
    ids = lax.broadcasted_iota(jnp.int32, (count, tokens), 0)
    for k in range(pair):
        dense = jnp.zeros((count, tokens), WIDE)
        for m in range(slot_count):
            hit = ids == slots_ref[k, m : m + 1, :]
            dense = jnp.where(hit, returned_ref[k, m : m + 1, :], dense)
        near = product_tn(dense.astype(LOW), keys_ref[k]) * key_scale
        terms_scr[k] = (term[k * tokens : (k + 1) * tokens] + near).astype(LOW)
    if pair == 2:
        core = base_ref[5]
        mine_ref[0] = terms_scr[core]
        other_ref[0] = terms_scr[1 - core]
    else:
        mine_ref[0] = terms_scr[0]
        other_ref[0] = terms_scr[0]


def word_grads(order, base, rows_all, ones_all, twos_all, returned, words_f, key_block, slots_t,
               weights, pair):
    sources, slot_count, tokens = slots_t.shape
    count = key_block.shape[1]
    width = rows_all.shape[1]
    chunk = pair * tokens
    total = rows_all.shape[0]
    steps = order.shape[0]
    sizes = [weights[k].shape[1] for k in range(3)]
    sizes.append(weights[5].shape[0] - sizes[0])

    def by_row(columns):
        return pl.BlockSpec((chunk, columns), lambda g, o, b: (o[g], 0))

    inputs = [rows_all, ones_all, twos_all, returned, words_f, key_block, slots_t, *weights]
    return pl.pallas_call(
        word_grads_kernel,
        grid_spec=pltpu.PrefetchScalarGridSpec(
            num_scalar_prefetch=2,
            grid=(steps,),
            in_specs=[
                by_row(width),
                by_row(ones_all.shape[1]),
                by_row(twos_all.shape[1]),
                pl.BlockSpec((pair, slot_count + 8, tokens), lambda g, o, b: (o[g], 0, 0)),
                pl.BlockSpec((pair, 1, tokens), lambda g, o, b: (o[g], 0, 0)),
                pl.BlockSpec((pair, count, width), lambda g, o, b: (o[g], 0, 0)),
                pl.BlockSpec((pair, slot_count, tokens), lambda g, o, b: (o[g], 0, 0)),
            ]
            + [whole_spec(w) for w in weights],
            out_specs=[
                pl.BlockSpec((1, tokens, width), lambda g, o, b: (g, 0, 0)),
                pl.BlockSpec((1, tokens, width), lambda g, o, b: (g, 0, 0)),
            ]
            + [by_row(size) for size in sizes],
            scratch_shapes=[
                pltpu.VMEM((pair, tokens, width), LOW),
                pltpu.VMEM((chunk, weights[5].shape[0]), LOW),
            ],
        ),
        out_shape=[
            jax.ShapeDtypeStruct((steps, tokens, width), LOW),
            jax.ShapeDtypeStruct((steps, tokens, width), LOW),
        ]
        + [jax.ShapeDtypeStruct((total, size), LOW) for size in sizes],
        cost_estimate=cost(10),
        name="word_grads",
    )(order, base, *inputs)


def word_sums_kernel(
    rows_ref, ones_ref, twos_ref, head_g_ref, first_g_ref, second_g_ref, back_ref,
    packed_ref, proj_ref, *scratch
):
    step = pl.program_id(0)
    pairs = (
        (head_g_ref, rows_ref),
        (ones_ref, first_g_ref),
        (twos_ref, second_g_ref),
        (rows_ref, back_ref),
    )

    @pl.when(step == 0)
    def _():
        for acc in scratch:
            acc[...] = jnp.zeros_like(acc)

    for (left, right), acc in zip(pairs, scratch):
        acc[...] += product_tn(left[...], right[...])

    @pl.when(step == pl.num_programs(0) - 1)
    def _():
        proj_ref[...] = scratch[3][...].astype(LOW)
        place = 0
        for acc in scratch[:3]:
            rows, columns = acc.shape
            for start in range(0, columns, 128):
                packed_ref[place : place + rows, :] = acc[:, start : start + 128].astype(LOW)
                place += rows


def word_sums(rows_all, ones_all, twos_all, grads):
    total = rows_all.shape[0]
    chunk = min(512, total)
    inputs = [rows_all, ones_all, twos_all, *grads]
    shapes = [
        (grads[0].shape[1], rows_all.shape[1]),
        (ones_all.shape[1], grads[1].shape[1]),
        (twos_all.shape[1], grads[2].shape[1]),
        (rows_all.shape[1], grads[3].shape[1]),
    ]
    packed_rows = sum(rows * columns for rows, columns in shapes[:3]) // 128
    out_shapes = [(packed_rows, 128), shapes[3]]
    packed, proj = pl.pallas_call(
        word_sums_kernel,
        grid=(total // chunk,),
        in_specs=[pl.BlockSpec((chunk, item.shape[1]), lambda g: (g, 0)) for item in inputs],
        out_specs=[pl.BlockSpec(shape, lambda g: (0, 0)) for shape in out_shapes],
        out_shape=[jax.ShapeDtypeStruct(shape, LOW) for shape in out_shapes],
        scratch_shapes=[pltpu.VMEM(shape, WIDE) for shape in shapes],
        cost_estimate=cost(10),
        name="word_sums",
    )(*inputs)
    return packed, proj, shapes[:3]


def unpack_kernel(me_ref, parts_ref, *outs):
    count, part_rows, _ = parts_ref.shape
    me = me_ref[0]
    place = 0
    for out in outs:
        rows, columns = out.shape
        for start in range(0, columns, 128):
            done = 0
            while done < rows:
                part, offset = divmod(place + done, part_rows)
                size = min(rows - done, part_rows - offset)
                out[done : done + size, start : start + 128] = parts_ref[
                    part ^ me, offset : offset + size, :
                ].astype(WIDE)
                done += size
            place += rows


def unpack_words(parts, shapes):
    return pl.pallas_call(
        unpack_kernel,
        grid_spec=pltpu.PrefetchScalarGridSpec(
            num_scalar_prefetch=1,
            grid=(1,),
            in_specs=[whole_spec(parts)],
            out_specs=[pl.BlockSpec(shape, lambda *_: (0, 0)) for shape in shapes],
        ),
        out_shape=[jax.ShapeDtypeStruct(shape, WIDE) for shape in shapes],
        cost_estimate=cost(3),
        compiler_params=pltpu.CompilerParams(vmem_limit_bytes=12 << 20),
        name="unpack_words",
    )(lax.axis_index("dp").astype(jnp.int32).reshape(1), parts)


def key_norms_kernel(keys_ref, norms_ref):
    for k in range(keys_ref.shape[0]):
        wide = keys_ref[k].astype(WIDE)
        norms = jnp.sum(wide * wide, axis=1, keepdims=True)
        norms_ref[k] = jnp.broadcast_to(norms, norms_ref.shape[1:])


def key_norms(key_block):
    sources, count, width = key_block.shape
    pair = min(2, sources)
    return pl.pallas_call(
        key_norms_kernel,
        grid=(sources // pair,),
        in_specs=[pl.BlockSpec((pair, count, width), lambda g: (g, 0, 0))],
        out_specs=pl.BlockSpec((pair, count, 128), lambda g: (g, 0, 0)),
        out_shape=jax.ShapeDtypeStruct((sources, count, 128), WIDE),
        cost_estimate=cost(20),
        compiler_params=pltpu.CompilerParams(vmem_limit_bytes=8 << 20),
        name="key_norms",
    )(key_block)


def input_back_kernel(
    parts_ref, qkv_ref, in_ref, grad_ref, gains_ref, input_grad_ref, sums_ref, acc_scr
):
    step = pl.program_id(0)

    @pl.when(step == 0)
    def _():
        acc_scr[...] = jnp.zeros_like(acc_scr)

    group = qkv_ref.shape[2]
    total = acc_scr[...]
    for kind in range(3):
        total = total + product(
            qkv_ref[kind], parts_ref[:, kind * group : (kind + 1) * group].T
        )
    acc_scr[...] = total

    @pl.when(step == pl.num_programs(0) - 1)
    def _():
        unit_rows, inverse = norm_stats(in_ref[...].astype(WIDE))
        back, gain, shift = norm_backward(acc_scr[...].T, unit_rows, inverse, gains_ref[0:1])
        input_grad_ref[...] = grad_ref[...] + back
        sums_ref[0:1] = gain
        sums_ref[1:2] = shift


def input_back(parts, attn_qkv, inputs, first_grad, gains):
    count, tokens, _ = parts.shape
    width = inputs.shape[1]
    group = width // count
    full = pl.BlockSpec((tokens, width), lambda g: (0, 0))
    return pl.pallas_call(
        input_back_kernel,
        grid=(count,),
        in_specs=[
            pl.BlockSpec((None, tokens, 3 * group), lambda g: (g, 0, 0)),
            pl.BlockSpec((3, width, group), lambda g: (0, 0, g)),
            full,
            full,
            pl.BlockSpec(gains.shape, lambda g: (0, 0)),
        ],
        out_specs=[full, pl.BlockSpec((8, width), lambda g: (0, 0))],
        out_shape=[
            jax.ShapeDtypeStruct((tokens, width), WIDE),
            jax.ShapeDtypeStruct((8, width), WIDE),
        ],
        scratch_shapes=[pltpu.VMEM((width, tokens), WIDE)],
        cost_estimate=cost(7),
        compiler_params=pltpu.CompilerParams(vmem_limit_bytes=12 << 20),
        name="input_back",
    )(parts, attn_qkv, inputs, first_grad, gains)


def shards(
    inputs,
    lengths,
    targets,
    attn_qkv,
    attn_out,
    ffn_up,
    ffn_down,
    norm_gains,
    norm_shifts,
    biases,
    up_bias,
    cluster_proj,
    proj_first,
    proj_second,
    head_words,
    tail_first,
    tail_second,
    store_keys,
    block_rows,
    near_slots,
    near_words,
):
    tokens_here = inputs.shape[0]
    d_model = inputs.shape[1]
    dp_count = lax.axis_size("dp")
    sources = lax.axis_size("line") * 2
    my_index = lax.axis_index("line") * 2 + lax.axis_index("core")
    group_rows = tokens_here * sources
    head_cols = head_words.shape[1]
    first_cols = tail_first.shape[1]
    second_cols = tail_second.shape[1]
    head_total = head_cols * sources
    first_total = first_cols * sources
    ff_width = ffn_up.shape[1]
    valid_mask = (jnp.arange(tokens_here) < lengths[0]).astype(WIDE)

    (
        query_low, key_low, value_low, mixed_low, normed_low, first_sum, second_low, act_low,
        second_sum, hidden_low
    ) = block_forward(
        lengths, inputs, attn_qkv, attn_out, ffn_up, ffn_down, up_bias, norm_gains, norm_shifts,
        biases
    )
    cluster_logits = lax.dot_general(
        cluster_proj, hidden_low, (((0,), (1,)), ((), ())), preferred_element_type=WIDE
    )

    rows_all = lax.all_gather(hidden_low, STORE, axis=0, tiled=True)

    key_block = jnp.take(store_keys, block_rows[0, 0].reshape(-1), axis=0, mode="clip")
    key_block = key_block.reshape(sources, -1, d_model)
    slots_t = near_slots[0, 0].transpose(1, 2, 0)
    slot_count = slots_t.shape[1]
    words_t = near_words.T

    weights = (head_words, tail_first, tail_second, proj_first, proj_second)
    back_weights = weights[:3] + (
        tail_first.T,
        tail_second.T,
        jnp.concatenate([proj_first.T, head_words.T, proj_second.T], axis=0),
    )
    norms = key_norms(key_block)

    left_low = jnp.concatenate([act_low, second_low, mixed_low, normed_low], axis=1)
    left_low, rows_all, norms, slots_t, words_t, back_weights = lax.optimization_barrier(
        (left_low, rows_all, norms, slots_t, words_t, back_weights)
    )
    left_all = lax.all_gather(left_low, "dp", axis=0, tiled=True)

    core = lax.axis_index("core")
    words_f = targets.astype(WIDE).reshape(sources, 1, tokens_here)
    base = jnp.stack(
        [
            my_index * head_cols,
            head_total + my_index * first_cols,
            head_total + first_total + my_index * second_cols,
            jnp.int32(head_total),
            jnp.int32(head_total + first_total),
            core,
        ]
    ).astype(jnp.int32)
    outgoing, ones_all, twos_all = word_stats(
        base, rows_all, words_f, key_block, norms, slots_t, back_weights[:3] + weights[3:], 2
    )
    incoming = lax.all_to_all(outgoing, STORE, 0, 0)

    near_scores = incoming[:, :slot_count].reshape(sources * slot_count, tokens_here)
    own_stats = jnp.sum(incoming[:, slot_count : slot_count + 4], axis=0)
    own_words = lax.dynamic_slice_in_dim(targets, my_index * tokens_here, tokens_here, 0)
    in_first = ((own_words >= head_total) & (own_words < head_total + first_total)).astype(WIDE)
    in_second = (own_words >= head_total + first_total).astype(WIDE)
    head_sum = own_stats[0] + jnp.sum(jnp.exp(cluster_logits), axis=0)
    log_head = jnp.log(head_sum)
    log_first = jnp.log(own_stats[1])
    log_second = jnp.log(own_stats[2])
    log_model = (
        own_stats[3]
        - log_head
        + in_first * (cluster_logits[0] - log_first)
        + in_second * (cluster_logits[1] - log_second)
    )
    near_top = jnp.max(near_scores, axis=0, keepdims=True)
    near_exp = jnp.exp(near_scores - near_top)
    near_probs = near_exp / jnp.sum(near_exp, axis=0, keepdims=True)
    matched = (words_t == own_words[None, :]).astype(WIDE)
    near_mass = jnp.sum(near_probs * matched, axis=0)
    model_prob = jnp.exp(log_model)
    mixture = NEAR_WEIGHT * near_mass + (1.0 - NEAR_WEIGHT) * model_prob
    token_loss = -valid_mask * jnp.log(mixture)
    model_weight = valid_mask * (1.0 - NEAR_WEIGHT) * model_prob / mixture
    near_weight = valid_mask * NEAR_WEIGHT / mixture
    score_grad = -near_weight[None, :] * near_probs * (matched - near_mass[None, :])
    coef = jnp.stack([model_weight, log_head, log_first, log_second] + 4 * [model_weight])
    returning = jnp.concatenate(
        [
            score_grad.reshape(sources, slot_count, tokens_here),
            jnp.broadcast_to(coef[None], (sources,) + coef.shape),
        ],
        axis=1,
    )
    returned = lax.all_to_all(returning, STORE, 0, 0)

    lines = lax.axis_size("line")
    mine, other, *word_terms = word_grads(
        jnp.arange(lines, dtype=jnp.int32),
        base,
        rows_all,
        ones_all,
        twos_all,
        returned,
        words_f,
        key_block,
        slots_t,
        back_weights,
        2,
    )
    both = (mine.astype(WIDE) + swap_partner(other, "core", 1).astype(WIDE)).astype(LOW)
    row_parts = lax.all_to_all(both, "line", 0, 0)
    row_back = jnp.sum(row_parts.astype(WIDE), axis=0)
    word_terms, both = lax.optimization_barrier((word_terms, both))
    word_packed, proj_acc, word_shapes = word_sums(rows_all, ones_all, twos_all, word_terms)

    own_rows = d_model // sources
    proj_width = proj_acc.shape[1]
    sub_rows = own_rows // dp_count
    proj_parts = proj_acc.reshape(sources, dp_count, sub_rows, proj_width).transpose(1, 0, 2, 3)
    dp_index = lax.axis_index("dp")
    proj_sum = lax.dynamic_index_in_dim(proj_parts, dp_index, 0, keepdims=False).astype(WIDE)
    for q in range(1, dp_count):
        part = lax.dynamic_index_in_dim(proj_parts, dp_index ^ q, 0, keepdims=False)
        proj_sum = proj_sum + swap_partner(part, "dp", q).astype(WIDE)
    cluster_rows = model_weight[None, :] * (
        jnp.exp(cluster_logits - log_head[None, :]) - jnp.stack([in_first, in_second])
    )
    hidden_grad = row_back + lax.dot_general(
        cluster_rows, cluster_proj.astype(WIDE), (((0,), (1,)), ((), ())), precision=HIGH
    )
    cluster_acc = jnp.dot(cluster_rows, hidden_low.astype(WIDE), precision=HIGH)
    unit_three, inv_three = norm_stats(second_sum)
    second_grad, gain_three, shift_three = norm_backward(
        hidden_grad, unit_three, inv_three, norm_gains[2]
    )
    down_in = second_grad.astype(LOW)
    down_parts = exchange_columns(down_in)
    bias_down = jnp.sum(down_in.astype(WIDE), axis=0, keepdims=True)
    act_grad = product_nt(down_in, ffn_down)
    pre_grad = jnp.where(act_low.astype(WIDE) > 0, act_grad, 0.0).astype(LOW)
    up_bias_acc = jnp.sum(pre_grad.astype(WIDE), axis=0, keepdims=True)
    marks = [0, ff_width, ff_width + d_model, ff_width + 2 * d_model, ff_width + 3 * d_model]
    lefts = [left_all[:, a:b] for a, b in zip(marks[:-1], marks[1:])]
    down = Halving(grad_tile(lefts[0], after(down_parts, pre_grad)))
    norm_two_grad = product_nt(after(pre_grad, down.outgoing), ffn_up)
    unit_two, inv_two = norm_stats(first_sum)
    back_second, gain_two, shift_two = norm_backward(
        norm_two_grad, unit_two, inv_two, norm_gains[1]
    )
    first_grad_sum = second_grad + back_second
    attn_in = first_grad_sum.astype(LOW)
    bias_attn = jnp.sum(attn_in.astype(WIDE), axis=0, keepdims=True)
    mark = down.add(attn_in)
    up_width = ff_width // dp_count
    head_width = d_model // dp_count
    up_send = jnp.stack(
        [
            jnp.concatenate(
                [
                    pre_grad[:, k * up_width : (k + 1) * up_width],
                    attn_in[:, k * head_width : (k + 1) * head_width],
                ],
                axis=1,
            )
            for k in range(dp_count)
        ]
    )
    up_parts = lax.all_to_all(up_send, "dp", 0, 0)
    stacked_parts, sums_three = attention_back(
        lengths, after(attn_in, up_send, mark), attn_out, query_low, key_low, value_low, dp_count
    )
    mark = down.add(stacked_parts)
    qkv_parts = lax.all_to_all(after(stacked_parts, up_parts), "dp", 0, 0)
    word_send = after(word_packed.reshape(dp_count, -1, 128), qkv_parts)
    word_parts = lax.all_to_all(word_send, "dp", 0, 0)
    proj_rows = sub_rows * proj_width // (up_width + head_width)
    proj_block = proj_sum.astype(LOW).reshape(sources, proj_rows, up_width + head_width)
    up_parts = after(up_parts, mark)
    up = Halving(
        jnp.concatenate(
            [
                jnp.concatenate(
                    [
                        grad_tile(lefts[1], up_parts[:, :, :up_width]),
                        grad_tile(lefts[2], up_parts[:, :, up_width:]),
                    ],
                    axis=2,
                ),
                proj_block,
            ],
            axis=1,
        )
    )
    input_grad, sums_one = input_back(
        after(stacked_parts, up.outgoing, qkv_parts), attn_qkv, inputs, first_grad_sum, norm_gains
    )
    down_own = down.finish(input_grad)
    mark = up.add(input_grad, down_own)

    def by_store(value):
        rows = value.shape[0]
        return value.reshape(rows, sources, -1).transpose(1, 0, 2).reshape(sources, -1)

    small = jnp.concatenate(
        [
            by_store(jnp.concatenate([sums_one[0:1], gain_two, gain_three])),
            by_store(jnp.concatenate([sums_one[1:2], shift_two, shift_three])),
            by_store(jnp.concatenate([sums_three[0:1], sums_three[2:3], bias_attn, bias_down])),
            by_store(up_bias_acc),
            by_store(cluster_acc),
        ],
        axis=1,
    )
    small_count = small.shape[1]
    small_rows = -(-small_count // (3 * head_width))
    if own_rows % 128 == 0:
        small_rows = -(-small_rows // 8) * 8
    small = jnp.pad(small, ((0, 0), (0, small_rows * 3 * head_width - small_count)))
    small = small.reshape(sources, small_rows, 3 * head_width).astype(LOW)
    qkv = Halving(
        jnp.concatenate([grad_tile(lefts[3], after(qkv_parts, mark)), small], axis=1)
    )
    down_pieces = gather_dp(down_own)
    mark = qkv.add(qkv.outgoing)
    mark = up.add(mark)
    word_own = jnp.sum(after(word_parts, mark).astype(WIDE), axis=0).astype(LOW)
    mark = qkv.add(word_own)
    word_pieces = gather_dp(word_own)
    down_out = join_pieces(after(down_pieces, mark), 1, 0, head_width, 1)
    up_own = up.finish(down_out)
    up_pieces = gather_dp(up_own)
    word_pieces = after(word_pieces, up_own)
    head_t, first_out, second_out = unpack_words(jnp.stack(word_pieces), word_shapes)
    head_out = head_t.T
    qkv_own = qkv.finish(head_t)
    qkv_pieces = gather_dp(qkv_own)
    up_pieces = after(up_pieces, qkv_own)
    up_main = [piece[:own_rows] for piece in up_pieces]
    up_out = join_pieces(up_main, 1, 0, up_width, 1)
    out_out = join_pieces(up_main, 1, up_width, head_width, 1)
    proj_out = join_pieces(
        [piece[own_rows:].reshape(sub_rows, proj_width) for piece in up_pieces],
        0,
        0,
        sub_rows,
        0,
    )
    qkv_main = [piece[:own_rows] for piece in qkv_pieces]
    qkv_out = jnp.stack(
        [join_pieces(qkv_main, 1, kind * head_width, head_width, 1) for kind in range(3)]
    )
    small_sum = sum(piece[own_rows:].astype(WIDE) for piece in qkv_pieces).reshape(-1)
    sizes = [3 * own_rows, 3 * own_rows, 4 * own_rows, ff_width // sources, 2 * own_rows]
    ends = [0]
    for size in sizes:
        ends.append(ends[-1] + size)
    gains_out, shifts_out, biases_out, upb_out, cluster_out = (
        small_sum[a:b] for a, b in zip(ends[:-1], ends[1:])
    )
    return (
        token_loss,
        input_grad,
        qkv_out,
        out_out,
        up_out,
        down_out,
        gains_out.reshape(3, own_rows),
        shifts_out.reshape(3, own_rows),
        biases_out.reshape(4, own_rows),
        upb_out,
        cluster_out.reshape(2, own_rows).T,
        proj_out[:, : proj_first.shape[1]],
        proj_out[:, proj_first.shape[1] :],
        head_out,
        first_out,
        second_out,
    )


def solution(mesh):
    dp_count = mesh.shape["dp"]
    store_count = mesh.shape["store"]
    split = Mesh(mesh.devices.reshape(dp_count, store_count // 2, 2), ("dp",) + STORE)
    everyone = ("dp",) + STORE
    return jax.shard_map(
        shards,
        mesh=split,
        in_specs=(
            P(everyone, None),
            P(everyone),
            P("dp"),
            P(),
            P(),
            P(),
            P(),
            P(),
            P(),
            P(),
            P(),
            P(),
            P(),
            P(),
            P(None, STORE),
            P(None, STORE),
            P(None, STORE),
            P(STORE, None),
            P("dp", STORE, None, None),
            P("dp", STORE, None, None, None),
            P(everyone, None),
        ),
        out_specs=(
            P(everyone),
            P(everyone, None),
            P(None, STORE, None),
            P(STORE, None),
            P(STORE, None),
            P(STORE, None),
            P(None, STORE),
            P(None, STORE),
            P(None, STORE),
            P(STORE),
            P(STORE, None),
            P(STORE, None),
            P(STORE, None),
            P(None, STORE),
            P(None, STORE),
            P(None, STORE),
        ),
        check_vma=False,
    )
```

```python
import math

import jax
import jax.numpy as jnp
from jax import lax
from jax.experimental import pallas as pl
from jax.experimental.pallas import tpu as pltpu
from jax.sharding import Mesh
from jax.sharding import PartitionSpec as P

HEADS = 16
HD = 64


EPS = 1e-05
NEAR_WEIGHT = 0.25
NEG_FILL = -1e30
HIGH = lax.Precision.HIGHEST
STORE = ("line", "core")
LOW = jnp.bfloat16
WIDE = jnp.float32
SECOND_TILE = 256


def product(left, right):
    return jnp.dot(left, right, preferred_element_type=WIDE)


def product_tn(left, right):
    return lax.dot_general(left, right, (((0,), (0,)), ((), ())), preferred_element_type=WIDE)


def product_nt(left, right):
    return lax.dot_general(left, right, (((1,), (1,)), ((), ())), preferred_element_type=WIDE)


def norm_forward(values, gain_row, shift_row):
    row_mean = jnp.mean(values, axis=-1, keepdims=True)
    centred = values - row_mean
    inverse = lax.rsqrt(jnp.mean(centred * centred, axis=-1, keepdims=True) + EPS)
    unit_rows = centred * inverse
    return (unit_rows * gain_row + shift_row, unit_rows, inverse)


def norm_backward(grad_out, unit_rows, inverse, gain_row):
    scaled = grad_out * gain_row
    grad_in = inverse * (
        scaled
        - jnp.mean(scaled, axis=-1, keepdims=True)
        - unit_rows * jnp.mean(scaled * unit_rows, axis=-1, keepdims=True)
    )
    return (grad_in, jnp.sum(grad_out * unit_rows, axis=0, keepdims=True), jnp.sum(grad_out, axis=0, keepdims=True))


def swap_partner(value, axis, bit):
    count = lax.axis_size(axis)
    return lax.ppermute(value, axis, [(k, k ^ bit) for k in range(count)])


def after(value, *others):
    return lax.optimization_barrier((value, *others))[0]


class Halving:
    def __init__(self, blocks):
        lines = lax.axis_size("line")
        line = lax.axis_index("line")
        self.rest = blocks.shape[1:]
        self.current = blocks.reshape((lines, 2) + self.rest)
        self.steps = [(lax.axis_index("core"), "core", 1)]
        bit = 1
        while bit < lines:
            self.steps.append(((line // bit) & 1, "line", bit))
            bit *= 2
        self.received = None
        self.send()

    def send(self):
        mine, axis, bit = self.steps.pop(0)
        value = self.current
        outgoing = lax.dynamic_index_in_dim(value, 1 - mine, 1, keepdims=False).astype(LOW)
        self.outgoing = outgoing
        self.current = lax.dynamic_index_in_dim(value, mine, 1, keepdims=False)
        self.received = swap_partner(outgoing, axis, bit)

    def add(self, *others):
        received = after(self.received, *others) if others else self.received
        self.current = self.current.astype(WIDE) + received.astype(WIDE)
        if self.steps:
            self.current = self.current.reshape((-1, 2) + self.rest)
            self.send()
        return self.outgoing

    def finish(self, *others):
        while self.steps:
            self.add(*others)
        self.add(*others)
        return self.current[0].astype(LOW)


def grad_tile(left, right_parts):
    blocks = lax.axis_size("line") * 2
    right = right_parts.reshape(left.shape[0], right_parts.shape[2])
    tile = product_tn(left, right).astype(LOW)
    return tile.reshape(blocks, -1, right.shape[1])


def gather_dp(own):
    count = lax.axis_size("dp")
    return [own] + [swap_partner(own, "dp", q) for q in range(1, count)]


def join_pieces(pieces, axis, start, width, join_axis):
    count = len(pieces)
    me = lax.axis_index("dp")
    pieces = [lax.slice_in_dim(piece, start, start + width, axis=axis) for piece in pieces]
    bit = 1
    while bit < count:
        is_set = (me // bit) & 1 == 1
        pieces = [jnp.where(is_set, pieces[k ^ bit], pieces[k]) for k in range(count)]
        bit *= 2
    return jnp.concatenate([piece.astype(WIDE) for piece in pieces], axis=join_axis)


def exchange_columns(value):
    count = lax.axis_size("dp")
    tokens, columns = value.shape
    parts = value.reshape(tokens, count, columns // count).transpose(1, 0, 2)
    return lax.all_to_all(parts, "dp", 0, 0)


def cost(micros):
    return pl.CostEstimate(flops=int(micros * 9e8), transcendentals=0, bytes_accessed=1 << 20)


def head_masks(width):
    lanes = lax.broadcasted_iota(jnp.int32, (1, width), 1)
    return [(lanes // HD) % 2 == half for half in range(2)]


def masked_softmax(scores, allowed):
    scores = jnp.where(allowed, scores * HD ** (-0.5), NEG_FILL)
    exps = jnp.exp(scores - jnp.max(scores, axis=-1, keepdims=True))
    return exps / jnp.sum(exps, axis=-1, keepdims=True)


def seen_keys(tokens, length):
    rows = lax.broadcasted_iota(jnp.int32, (tokens, tokens), 0)
    cols = lax.broadcasted_iota(jnp.int32, (tokens, tokens), 1)
    return (cols <= rows) & (cols < length)


def block_kernel(
    length_ref, in_ref, qkv_ref, out_w_ref, up_bias_ref, gains_ref, shifts_ref, biases_ref,
    group_bias_ref, up_hbm, down_hbm,
    query_ref, key_ref, value_ref, mixed_ref, normed_ref, first_ref, second_ref, act_ref, sum_ref,
    hidden_ref, acc_scr, up_scr, down_scr, sems
):
    step = pl.program_id(0)
    tokens, width = in_ref.shape
    group = query_ref.shape[1]
    groups = width // group
    blocks = up_scr.shape[0]
    block = up_scr.shape[2]

    def fetches(place):
        start = place * block
        return (
            pltpu.make_async_copy(
                up_hbm.at[:, pl.ds(start, block)], up_scr.at[place], sems.at[0, place]
            ),
            pltpu.make_async_copy(
                down_hbm.at[pl.ds(start, block), :], down_scr.at[place], sems.at[1, place]
            ),
        )

    @pl.when(step == 0)
    def _():
        for place in range(blocks):
            for fetch in fetches(place):
                fetch.start()
        block_in = in_ref[...].astype(WIDE)
        normed_ref[...] = norm_forward(block_in, gains_ref[0:1], shifts_ref[0:1])[0].astype(LOW)
        acc_scr[...] = block_in + biases_ref[2:3]

    @pl.when(step < groups)
    def _():
        normed = normed_ref[...]
        query = (product(normed, qkv_ref[0]) + group_bias_ref[0:1]).astype(LOW)
        key = product(normed, qkv_ref[1]).astype(LOW)
        value = (product(normed, qkv_ref[2]) + group_bias_ref[1:2]).astype(LOW)
        query_ref[...] = query
        key_ref[...] = key
        value_ref[...] = value
        allowed = seen_keys(tokens, length_ref[0])
        masks = head_masks(128)
        zero = jnp.zeros((tokens, 128), LOW)
        for pair in range(group // 128):
            cols = slice(pair * 128, (pair + 1) * 128)
            q_pair, k_pair, v_pair = query[:, cols], key[:, cols], value[:, cols]
            mixed = jnp.zeros((tokens, 128), WIDE)
            for mask in masks:
                probs = masked_softmax(product_nt(q_pair, jnp.where(mask, k_pair, zero)), allowed)
                mixed = mixed + product(probs.astype(LOW), jnp.where(mask, v_pair, zero))
            mixed_ref[:, cols] = mixed.astype(LOW)
        acc_scr[...] += product(mixed_ref[...], out_w_ref[...])

    @pl.when(step == groups - 1)
    def _():
        first_sum = acc_scr[...]
        first_ref[...] = first_sum
        second_ref[...] = norm_forward(first_sum, gains_ref[1:2], shifts_ref[1:2])[0].astype(LOW)
        acc_scr[...] = first_sum + biases_ref[3:4]

    @pl.when(step >= groups)
    def _():
        place = step - groups
        for fetch in fetches(place):
            fetch.wait()
        pre_act = product(second_ref[...], up_scr[place]) + up_bias_ref[...]
        act = jnp.maximum(pre_act, 0.0).astype(LOW)
        act_ref[...] = act
        acc_scr[...] += product(act, down_scr[place])

    @pl.when(step == pl.num_programs(0) - 1)
    def _():
        total = acc_scr[...]
        sum_ref[...] = total
        hidden_ref[...] = norm_forward(total, gains_ref[2:3], shifts_ref[2:3])[0].astype(LOW)


def block_forward(
    length, inputs, attn_qkv, attn_out, ffn_up, ffn_down, up_bias, gains, shifts, biases
):
    tokens, width = inputs.shape
    inner = ffn_up.shape[1]
    group = min(256, width)
    groups = width // group
    block = min(1024, inner)
    blocks = inner // block
    full = pl.BlockSpec((tokens, width), lambda g, n: (0, 0))
    part = pl.BlockSpec((tokens, group), lambda g, n: (0, jnp.minimum(g, groups - 1)))
    low = jax.ShapeDtypeStruct((tokens, width), LOW)
    wide = jax.ShapeDtypeStruct((tokens, width), WIDE)
    return pl.pallas_call(
        block_kernel,
        grid_spec=pltpu.PrefetchScalarGridSpec(
            num_scalar_prefetch=1,
            grid=(groups + blocks,),
            in_specs=[
                full,
                pl.BlockSpec((3, width, group), lambda g, n: (0, 0, jnp.minimum(g, groups - 1))),
                pl.BlockSpec((group, width), lambda g, n: (jnp.minimum(g, groups - 1), 0)),
                pl.BlockSpec((1, block), lambda g, n: (0, jnp.maximum(g - groups, 0))),
                pl.BlockSpec(gains.shape, lambda g, n: (0, 0)),
                pl.BlockSpec(shifts.shape, lambda g, n: (0, 0)),
                pl.BlockSpec(biases.shape, lambda g, n: (0, 0)),
                pl.BlockSpec(
                    (biases.shape[0], group), lambda g, n: (0, jnp.minimum(g, groups - 1))
                ),
                pl.BlockSpec(memory_space=pl.ANY),
                pl.BlockSpec(memory_space=pl.ANY),
            ],
            out_specs=[part, part, part, part, full, full, full]
            + [pl.BlockSpec((tokens, block), lambda g, n: (0, jnp.maximum(g - groups, 0)))]
            + [full, full],
            scratch_shapes=[
                pltpu.VMEM((tokens, width), WIDE),
                pltpu.VMEM((blocks, width, block), LOW),
                pltpu.VMEM((blocks, block, width), LOW),
                pltpu.SemaphoreType.DMA((2, blocks)),
            ],
        ),
        out_shape=[low, low, low, low, low, wide, low]
        + [jax.ShapeDtypeStruct((tokens, inner), LOW), wide, low],
        cost_estimate=cost(16),
        name="block_forward",
    )(
        length, inputs, attn_qkv, attn_out, up_bias.reshape(1, inner), gains, shifts, biases,
        biases, ffn_up, ffn_down
    )


def norm_stats(values):
    centred = values - jnp.mean(values, axis=-1, keepdims=True)
    inverse = lax.rsqrt(jnp.mean(centred * centred, axis=-1, keepdims=True) + EPS)
    return centred * inverse, inverse


def attention_back_kernel(
    length_ref, attn_in_ref, out_w_ref, query_ref, key_ref, value_ref, parts_ref, sums_ref,
    attn_t_scr
):
    tokens = attn_in_ref.shape[0]
    width = query_ref.shape[1]

    @pl.when(pl.program_id(0) == 0)
    def _():
        attn_t_scr[...] = attn_in_ref[...].T

    mixed_grad = product(out_w_ref[...], attn_t_scr[...]).T.astype(LOW)
    allowed = seen_keys(tokens, length_ref[0])
    masks = head_masks(128)
    zero = jnp.zeros((tokens, 128), LOW)
    for pair in range(width // 128):
        cols = slice(pair * 128, (pair + 1) * 128)
        q_pair, k_pair, v_pair = query_ref[:, cols], key_ref[:, cols], value_ref[:, cols]
        m_pair = mixed_grad[:, cols]
        totals = [jnp.zeros((tokens, 128), WIDE) for _ in range(3)]
        for mask in masks:
            k_one = jnp.where(mask, k_pair, zero)
            probs = masked_softmax(product_nt(q_pair, k_one), allowed)
            prob_grad = product_nt(m_pair, jnp.where(mask, v_pair, zero))
            delta = jnp.sum(probs * prob_grad, axis=-1, keepdims=True)
            score_grad = (probs * (prob_grad - delta)).astype(LOW)
            totals[0] += product(score_grad, k_one)
            totals[1] += product_tn(score_grad, jnp.where(mask, q_pair, zero))
            totals[2] += product_tn(probs.astype(LOW), jnp.where(mask, m_pair, zero))
        for kind, total in enumerate(totals):
            scale = HD ** (-0.5) if kind < 2 else 1.0
            grad = (total * scale).astype(LOW)
            parts_ref[:, kind * width + pair * 128 : kind * width + (pair + 1) * 128] = grad
            if kind != 1:
                sums_ref[kind : kind + 1, cols] = jnp.sum(
                    grad.astype(WIDE), axis=0, keepdims=True
                )


def attention_back(length, attn_in, attn_out, query, key, value, parts):
    tokens, width = attn_in.shape
    group = width // parts
    part = pl.BlockSpec((tokens, group), lambda g, n: (0, g))
    return pl.pallas_call(
        attention_back_kernel,
        grid_spec=pltpu.PrefetchScalarGridSpec(
            num_scalar_prefetch=1,
            grid=(parts,),
            in_specs=[
                pl.BlockSpec((tokens, width), lambda g, n: (0, 0)),
                pl.BlockSpec((group, width), lambda g, n: (g, 0)),
                part,
                part,
                part,
            ],
            out_specs=[
                pl.BlockSpec((None, tokens, 3 * group), lambda g, n: (g, 0, 0)),
                pl.BlockSpec((8, group), lambda g, n: (0, g)),
            ],
            scratch_shapes=[pltpu.VMEM((width, tokens), LOW)],
        ),
        out_shape=[
            jax.ShapeDtypeStruct((parts, tokens, 3 * group), LOW),
            jax.ShapeDtypeStruct((8, width), WIDE),
        ],
        cost_estimate=cost(9),
        compiler_params=pltpu.CompilerParams(vmem_limit_bytes=10 << 20),
        name="attention_back",
    )(length, attn_in, attn_out, query, key, value)


def to_columns(rows):
    short = 128 - rows.shape[0]
    padded = jnp.concatenate([rows, jnp.zeros((short, rows.shape[1]), rows.dtype)], axis=0)
    return padded.T


def word_columns(words_ref):
    columns = [to_columns(words_ref[k])[:, 0:1] for k in range(words_ref.shape[0])]
    return jnp.concatenate(columns, axis=0).astype(jnp.int32)


def is_word(where_wide, first_col):
    lanes = lax.broadcasted_iota(jnp.int32, (1, where_wide.shape[1]), 1) + first_col
    return where_wide == lanes


def stats_kernel(
    base_ref, rows_ref, words_ref, keys_ref, norms_ref, slots_ref, head_ref, first_ref,
    second_ref, proj_one_ref, proj_two_ref, stats_ref, ones_ref, twos_ref
):
    rows = rows_ref[...]
    pair = words_ref.shape[0]
    tokens = words_ref.shape[2]
    words = word_columns(words_ref)
    ones = product(rows, proj_one_ref[...]).astype(LOW)
    twos = product(rows, proj_two_ref[...]).astype(LOW)
    ones_ref[...] = ones
    twos_ref[...] = twos
    picked = jnp.zeros((rows.shape[0], 1), WIDE)
    sums = []
    for place, (left, words_w) in enumerate(
        ((rows, head_ref), (ones, first_ref), (twos, second_ref))
    ):
        columns = words_w.shape[1]
        tile = SECOND_TILE if columns % SECOND_TILE == 0 else columns
        total = jnp.zeros((rows.shape[0], tile), WIDE)
        chosen = jnp.zeros((rows.shape[0], tile), WIDE)
        where_wide = jnp.broadcast_to(words - base_ref[place], (rows.shape[0], tile))
        for start in range(0, columns, tile):
            logits = product(left, words_w[:, start : start + tile])
            total = total + jnp.exp(logits)
            chosen = jnp.where(is_word(where_wide, start), logits, chosen)
        sums.append(jnp.sum(total, axis=1, keepdims=True))
        picked = picked + jnp.sum(chosen, axis=1, keepdims=True)
    sums.append(picked)
    lanes = lax.broadcasted_iota(jnp.int32, (rows.shape[0], 128), 1)
    table = jnp.zeros((rows.shape[0], 128), WIDE)
    for place, column in enumerate(sums):
        table = jnp.where(lanes == place, column, table)
    slot_count = slots_ref.shape[1]
    scale = 1.0 / math.sqrt(rows.shape[1])
    for k in range(pair):
        keys = keys_ref[k]
        norms = norms_ref[k][:, 0:1]
        scored = product_nt(keys, rows[k * tokens : (k + 1) * tokens]) * scale
        scored = scored - norms * (0.5 * scale)
        ids = lax.broadcasted_iota(jnp.int32, scored.shape, 0)
        for m in range(slot_count):
            hit = ids == slots_ref[k, m : m + 1, :]
            stats_ref[k, m : m + 1, :] = jnp.sum(
                jnp.where(hit, scored, 0.0), axis=0, keepdims=True
            )
        stats_ref[k, slot_count : slot_count + 8, :] = table[k * tokens : (k + 1) * tokens].T[0:8]


def whole_spec(array):
    return pl.BlockSpec(array.shape, lambda *_: (0,) * array.ndim)


def word_stats(base, rows_all, words_f, key_block, norms, slots_t, weights, pair):
    sources, slot_count, tokens = slots_t.shape
    count = key_block.shape[1]
    width = rows_all.shape[1]
    chunk = pair * tokens
    ones = weights[3].shape[1]
    twos = weights[4].shape[1]
    return pl.pallas_call(
        stats_kernel,
        grid_spec=pltpu.PrefetchScalarGridSpec(
            num_scalar_prefetch=1,
            grid=(sources // pair,),
            in_specs=[
                pl.BlockSpec((chunk, width), lambda g, b: (g, 0)),
                pl.BlockSpec((pair, 1, tokens), lambda g, b: (g, 0, 0)),
                pl.BlockSpec((pair, count, width), lambda g, b: (g, 0, 0)),
                pl.BlockSpec((pair, count, 128), lambda g, b: (g, 0, 0)),
                pl.BlockSpec((pair, slot_count, tokens), lambda g, b: (g, 0, 0)),
            ]
            + [whole_spec(w) for w in weights],
            out_specs=[
                pl.BlockSpec((pair, slot_count + 8, tokens), lambda g, b: (g, 0, 0)),
                pl.BlockSpec((chunk, ones), lambda g, b: (g, 0)),
                pl.BlockSpec((chunk, twos), lambda g, b: (g, 0)),
            ],
        ),
        out_shape=[
            jax.ShapeDtypeStruct((sources, slot_count + 8, tokens), WIDE),
            jax.ShapeDtypeStruct((rows_all.shape[0], ones), LOW),
            jax.ShapeDtypeStruct((rows_all.shape[0], twos), LOW),
        ],
        cost_estimate=cost(13),
        name="word_stats",
    )(base, rows_all, words_f, key_block, norms, slots_t, *weights)


def word_grads_kernel(
    order_ref, base_ref, rows_ref, ones_ref, twos_ref, returned_ref, words_ref, keys_ref,
    slots_ref, head_ref, first_ref, second_ref, first_t_ref, second_t_ref, mixed_t_ref, *refs
):
    (
        mine_ref, other_ref, head_g_ref, first_g_ref, second_g_ref, back_ref, terms_scr, mixed_scr
    ) = refs[-8:]
    rows = rows_ref[...]
    pair = words_ref.shape[0]
    tokens = words_ref.shape[2]
    slot_count = slots_ref.shape[1]
    words = word_columns(words_ref)
    coefs = [to_columns(returned_ref[k, slot_count : slot_count + 8, :]) for k in range(pair)]
    coefs = jnp.concatenate(coefs, axis=0)
    weight = coefs[:, 0:1]
    in_first = (words >= base_ref[3]) & (words < base_ref[4])
    in_second = words >= base_ref[4]
    scales = (
        weight,
        jnp.where(in_first, weight, 0.0),
        jnp.where(in_second, weight, 0.0),
    )
    lefts = (rows, ones_ref[...], twos_ref[...])
    for place, (words_w, out_ref) in enumerate(
        ((head_ref, head_g_ref), (first_ref, first_g_ref), (second_ref, second_g_ref))
    ):
        columns = words_w.shape[1]
        tile = SECOND_TILE if columns % SECOND_TILE == 0 else columns
        where_wide = jnp.broadcast_to(words - base_ref[place], (rows.shape[0], tile))
        scale = scales[place]
        log_sum = coefs[:, place + 1 : place + 2] - jnp.log(scale)

        def one_tile(tile_w, start):
            logits = product(lefts[place], tile_w)
            hit = is_word(where_wide, start)
            return (jnp.exp(logits - log_sum) - jnp.where(hit, scale, 0.0)).astype(LOW)

        if columns == tile:
            out_ref[...] = one_tile(words_w[...], 0)
        else:

            for start in range(0, columns, tile):
                out_ref[:, start : start + tile] = one_tile(
                    words_w[:, start : start + tile], start
                )

    ones = ones_ref.shape[1]
    heads = head_g_ref.shape[1]
    mixed_scr[:, ones : ones + heads] = head_g_ref[...]
    back_one = product(first_g_ref[...], first_t_ref[...]).astype(LOW)
    mixed_scr[:, 0:ones] = back_one
    back_ref[:, 0:ones] = back_one
    back_two = product(second_g_ref[...], second_t_ref[...]).astype(LOW)
    mixed_scr[:, ones + heads :] = back_two
    back_ref[:, ones:] = back_two
    term = product(mixed_scr[...], mixed_t_ref[...])
    key_scale = 1.0 / math.sqrt(rows.shape[1])
    count = keys_ref.shape[1]
    ids = lax.broadcasted_iota(jnp.int32, (count, tokens), 0)
    for k in range(pair):
        dense = jnp.zeros((count, tokens), WIDE)
        for m in range(slot_count):
            hit = ids == slots_ref[k, m : m + 1, :]
            dense = jnp.where(hit, returned_ref[k, m : m + 1, :], dense)
        near = product_tn(dense.astype(LOW), keys_ref[k]) * key_scale
        terms_scr[k] = (term[k * tokens : (k + 1) * tokens] + near).astype(LOW)
    if pair == 2:
        core = base_ref[5]
        mine_ref[0] = terms_scr[core]
        other_ref[0] = terms_scr[1 - core]
    else:
        mine_ref[0] = terms_scr[0]
        other_ref[0] = terms_scr[0]


def word_grads(order, base, rows_all, ones_all, twos_all, returned, words_f, key_block, slots_t,
               weights, pair):
    sources, slot_count, tokens = slots_t.shape
    count = key_block.shape[1]
    width = rows_all.shape[1]
    chunk = pair * tokens
    total = rows_all.shape[0]
    steps = order.shape[0]
    sizes = [weights[k].shape[1] for k in range(3)]
    sizes.append(weights[5].shape[0] - sizes[0])

    def by_row(columns):
        return pl.BlockSpec((chunk, columns), lambda g, o, b: (o[g], 0))

    inputs = [rows_all, ones_all, twos_all, returned, words_f, key_block, slots_t, *weights]
    return pl.pallas_call(
        word_grads_kernel,
        grid_spec=pltpu.PrefetchScalarGridSpec(
            num_scalar_prefetch=2,
            grid=(steps,),
            in_specs=[
                by_row(width),
                by_row(ones_all.shape[1]),
                by_row(twos_all.shape[1]),
                pl.BlockSpec((pair, slot_count + 8, tokens), lambda g, o, b: (o[g], 0, 0)),
                pl.BlockSpec((pair, 1, tokens), lambda g, o, b: (o[g], 0, 0)),
                pl.BlockSpec((pair, count, width), lambda g, o, b: (o[g], 0, 0)),
                pl.BlockSpec((pair, slot_count, tokens), lambda g, o, b: (o[g], 0, 0)),
            ]
            + [whole_spec(w) for w in weights],
            out_specs=[
                pl.BlockSpec((1, tokens, width), lambda g, o, b: (g, 0, 0)),
                pl.BlockSpec((1, tokens, width), lambda g, o, b: (g, 0, 0)),
            ]
            + [by_row(size) for size in sizes],
            scratch_shapes=[
                pltpu.VMEM((pair, tokens, width), LOW),
                pltpu.VMEM((chunk, weights[5].shape[0]), LOW),
            ],
        ),
        out_shape=[
            jax.ShapeDtypeStruct((steps, tokens, width), LOW),
            jax.ShapeDtypeStruct((steps, tokens, width), LOW),
        ]
        + [jax.ShapeDtypeStruct((total, size), LOW) for size in sizes],
        cost_estimate=cost(10),
        name="word_grads",
    )(order, base, *inputs)


def word_sums_kernel(
    rows_ref, ones_ref, twos_ref, head_g_ref, first_g_ref, second_g_ref, back_ref,
    packed_ref, proj_ref, *scratch
):
    step = pl.program_id(0)
    pairs = (
        (head_g_ref, rows_ref),
        (ones_ref, first_g_ref),
        (twos_ref, second_g_ref),
        (rows_ref, back_ref),
    )

    @pl.when(step == 0)
    def _():
        for acc in scratch:
            acc[...] = jnp.zeros_like(acc)

    for (left, right), acc in zip(pairs, scratch):
        acc[...] += product_tn(left[...], right[...])

    @pl.when(step == pl.num_programs(0) - 1)
    def _():
        proj_ref[...] = scratch[3][...].astype(LOW)
        place = 0
        for acc in scratch[:3]:
            rows, columns = acc.shape
            for start in range(0, columns, 128):
                packed_ref[place : place + rows, :] = acc[:, start : start + 128].astype(LOW)
                place += rows


def word_sums(rows_all, ones_all, twos_all, grads):
    total = rows_all.shape[0]
    chunk = min(512, total)
    inputs = [rows_all, ones_all, twos_all, *grads]
    shapes = [
        (grads[0].shape[1], rows_all.shape[1]),
        (ones_all.shape[1], grads[1].shape[1]),
        (twos_all.shape[1], grads[2].shape[1]),
        (rows_all.shape[1], grads[3].shape[1]),
    ]
    packed_rows = sum(rows * columns for rows, columns in shapes[:3]) // 128
    out_shapes = [(packed_rows, 128), shapes[3]]
    packed, proj = pl.pallas_call(
        word_sums_kernel,
        grid=(total // chunk,),
        in_specs=[pl.BlockSpec((chunk, item.shape[1]), lambda g: (g, 0)) for item in inputs],
        out_specs=[pl.BlockSpec(shape, lambda g: (0, 0)) for shape in out_shapes],
        out_shape=[jax.ShapeDtypeStruct(shape, LOW) for shape in out_shapes],
        scratch_shapes=[pltpu.VMEM(shape, WIDE) for shape in shapes],
        cost_estimate=cost(10),
        name="word_sums",
    )(*inputs)
    return packed, proj, shapes[:3]


def unpack_kernel(me_ref, parts_ref, *outs):
    count, part_rows, _ = parts_ref.shape
    me = me_ref[0]
    place = 0
    for out in outs:
        rows, columns = out.shape
        for start in range(0, columns, 128):
            done = 0
            while done < rows:
                part, offset = divmod(place + done, part_rows)
                size = min(rows - done, part_rows - offset)
                out[done : done + size, start : start + 128] = parts_ref[
                    part ^ me, offset : offset + size, :
                ].astype(WIDE)
                done += size
            place += rows


def unpack_words(parts, shapes):
    return pl.pallas_call(
        unpack_kernel,
        grid_spec=pltpu.PrefetchScalarGridSpec(
            num_scalar_prefetch=1,
            grid=(1,),
            in_specs=[whole_spec(parts)],
            out_specs=[pl.BlockSpec(shape, lambda *_: (0, 0)) for shape in shapes],
        ),
        out_shape=[jax.ShapeDtypeStruct(shape, WIDE) for shape in shapes],
        cost_estimate=cost(3),
        compiler_params=pltpu.CompilerParams(vmem_limit_bytes=12 << 20),
        name="unpack_words",
    )(lax.axis_index("dp").astype(jnp.int32).reshape(1), parts)


def key_norms_kernel(keys_ref, norms_ref):
    for k in range(keys_ref.shape[0]):
        wide = keys_ref[k].astype(WIDE)
        norms = jnp.sum(wide * wide, axis=1, keepdims=True)
        norms_ref[k] = jnp.broadcast_to(norms, norms_ref.shape[1:])


def key_norms(key_block):
    sources, count, width = key_block.shape
    pair = min(2, sources)
    return pl.pallas_call(
        key_norms_kernel,
        grid=(sources // pair,),
        in_specs=[pl.BlockSpec((pair, count, width), lambda g: (g, 0, 0))],
        out_specs=pl.BlockSpec((pair, count, 128), lambda g: (g, 0, 0)),
        out_shape=jax.ShapeDtypeStruct((sources, count, 128), WIDE),
        cost_estimate=cost(20),
        compiler_params=pltpu.CompilerParams(vmem_limit_bytes=8 << 20),
        name="key_norms",
    )(key_block)


def input_back_kernel(
    parts_ref, qkv_ref, in_ref, grad_ref, gains_ref, input_grad_ref, sums_ref, acc_scr
):
    step = pl.program_id(0)

    @pl.when(step == 0)
    def _():
        acc_scr[...] = jnp.zeros_like(acc_scr)

    group = qkv_ref.shape[2]
    total = acc_scr[...]
    for kind in range(3):
        total = total + product(
            qkv_ref[kind], parts_ref[:, kind * group : (kind + 1) * group].T
        )
    acc_scr[...] = total

    @pl.when(step == pl.num_programs(0) - 1)
    def _():
        unit_rows, inverse = norm_stats(in_ref[...].astype(WIDE))
        back, gain, shift = norm_backward(acc_scr[...].T, unit_rows, inverse, gains_ref[0:1])
        input_grad_ref[...] = grad_ref[...] + back
        sums_ref[0:1] = gain
        sums_ref[1:2] = shift


def input_back(parts, attn_qkv, inputs, first_grad, gains):
    count, tokens, _ = parts.shape
    width = inputs.shape[1]
    group = width // count
    full = pl.BlockSpec((tokens, width), lambda g: (0, 0))
    return pl.pallas_call(
        input_back_kernel,
        grid=(count,),
        in_specs=[
            pl.BlockSpec((None, tokens, 3 * group), lambda g: (g, 0, 0)),
            pl.BlockSpec((3, width, group), lambda g: (0, 0, g)),
            full,
            full,
            pl.BlockSpec(gains.shape, lambda g: (0, 0)),
        ],
        out_specs=[full, pl.BlockSpec((8, width), lambda g: (0, 0))],
        out_shape=[
            jax.ShapeDtypeStruct((tokens, width), WIDE),
            jax.ShapeDtypeStruct((8, width), WIDE),
        ],
        scratch_shapes=[pltpu.VMEM((width, tokens), WIDE)],
        cost_estimate=cost(7),
        compiler_params=pltpu.CompilerParams(vmem_limit_bytes=12 << 20),
        name="input_back",
    )(parts, attn_qkv, inputs, first_grad, gains)


def shards(
    inputs,
    lengths,
    targets,
    attn_qkv,
    attn_out,
    ffn_up,
    ffn_down,
    norm_gains,
    norm_shifts,
    biases,
    up_bias,
    cluster_proj,
    proj_first,
    proj_second,
    head_words,
    tail_first,
    tail_second,
    store_keys,
    block_rows,
    near_slots,
    near_words,
):
    tokens_here = inputs.shape[0]
    d_model = inputs.shape[1]
    dp_count = lax.axis_size("dp")
    sources = lax.axis_size("line") * 2
    my_index = lax.axis_index("line") * 2 + lax.axis_index("core")
    group_rows = tokens_here * sources
    head_cols = head_words.shape[1]
    first_cols = tail_first.shape[1]
    second_cols = tail_second.shape[1]
    head_total = head_cols * sources
    first_total = first_cols * sources
    ff_width = ffn_up.shape[1]
    valid_mask = (jnp.arange(tokens_here) < lengths[0]).astype(WIDE)

    (
        query_low, key_low, value_low, mixed_low, normed_low, first_sum, second_low, act_low,
        second_sum, hidden_low
    ) = block_forward(
        lengths, inputs, attn_qkv, attn_out, ffn_up, ffn_down, up_bias, norm_gains, norm_shifts,
        biases
    )
    cluster_logits = lax.dot_general(
        cluster_proj, hidden_low, (((0,), (1,)), ((), ())), preferred_element_type=WIDE
    )

    rows_all = lax.all_gather(hidden_low, STORE, axis=0, tiled=True)

    key_block = jnp.take(store_keys, block_rows[0, 0].reshape(-1), axis=0, mode="clip")
    key_block = key_block.reshape(sources, -1, d_model)
    slots_t = near_slots[0, 0].transpose(1, 2, 0)
    slot_count = slots_t.shape[1]
    words_t = near_words.T

    weights = (head_words, tail_first, tail_second, proj_first, proj_second)
    back_weights = weights[:3] + (
        tail_first.T,
        tail_second.T,
        jnp.concatenate([proj_first.T, head_words.T, proj_second.T], axis=0),
    )
    norms = key_norms(key_block)

    left_low = jnp.concatenate([act_low, second_low, mixed_low, normed_low], axis=1)
    late_weights = back_weights[3:]
    left_low, rows_all, norms, slots_t, words_t, late_weights = lax.optimization_barrier(
        (left_low, rows_all, norms, slots_t, words_t, late_weights)
    )
    back_weights = weights[:3] + late_weights
    left_all = lax.all_gather(left_low, "dp", axis=0, tiled=True)

    core = lax.axis_index("core")
    words_f = targets.astype(WIDE).reshape(sources, 1, tokens_here)
    base = jnp.stack(
        [
            my_index * head_cols,
            head_total + my_index * first_cols,
            head_total + first_total + my_index * second_cols,
            jnp.int32(head_total),
            jnp.int32(head_total + first_total),
            core,
        ]
    ).astype(jnp.int32)
    outgoing, ones_all, twos_all = word_stats(
        base, rows_all, words_f, key_block, norms, slots_t, back_weights[:3] + weights[3:], 2
    )
    incoming = lax.all_to_all(outgoing, STORE, 0, 0)

    near_scores = incoming[:, :slot_count].reshape(sources * slot_count, tokens_here)
    own_stats = jnp.sum(incoming[:, slot_count : slot_count + 4], axis=0)
    own_words = lax.dynamic_slice_in_dim(targets, my_index * tokens_here, tokens_here, 0)
    in_first = ((own_words >= head_total) & (own_words < head_total + first_total)).astype(WIDE)
    in_second = (own_words >= head_total + first_total).astype(WIDE)
    head_sum = own_stats[0] + jnp.sum(jnp.exp(cluster_logits), axis=0)
    log_head = jnp.log(head_sum)
    log_first = jnp.log(own_stats[1])
    log_second = jnp.log(own_stats[2])
    log_model = (
        own_stats[3]
        - log_head
        + in_first * (cluster_logits[0] - log_first)
        + in_second * (cluster_logits[1] - log_second)
    )
    near_top = jnp.max(near_scores, axis=0, keepdims=True)
    near_exp = jnp.exp(near_scores - near_top)
    near_probs = near_exp / jnp.sum(near_exp, axis=0, keepdims=True)
    matched = (words_t == own_words[None, :]).astype(WIDE)
    near_mass = jnp.sum(near_probs * matched, axis=0)
    model_prob = jnp.exp(log_model)
    mixture = NEAR_WEIGHT * near_mass + (1.0 - NEAR_WEIGHT) * model_prob
    token_loss = -valid_mask * jnp.log(mixture)
    model_weight = valid_mask * (1.0 - NEAR_WEIGHT) * model_prob / mixture
    near_weight = valid_mask * NEAR_WEIGHT / mixture
    score_grad = -near_weight[None, :] * near_probs * (matched - near_mass[None, :])
    coef = jnp.stack([model_weight, log_head, log_first, log_second] + 4 * [model_weight])
    returning = jnp.concatenate(
        [
            score_grad.reshape(sources, slot_count, tokens_here),
            jnp.broadcast_to(coef[None], (sources,) + coef.shape),
        ],
        axis=1,
    )
    returned = lax.all_to_all(returning, STORE, 0, 0)

    lines = lax.axis_size("line")
    mine, other, *word_terms = word_grads(
        jnp.arange(lines, dtype=jnp.int32),
        base,
        rows_all,
        ones_all,
        twos_all,
        returned,
        words_f,
        key_block,
        slots_t,
        back_weights,
        2,
    )
    both = (mine.astype(WIDE) + swap_partner(other, "core", 1).astype(WIDE)).astype(LOW)
    row_parts = lax.all_to_all(both, "line", 0, 0)
    row_back = jnp.sum(row_parts.astype(WIDE), axis=0)
    word_terms, both = lax.optimization_barrier((word_terms, both))
    word_packed, proj_acc, word_shapes = word_sums(rows_all, ones_all, twos_all, word_terms)

    own_rows = d_model // sources
    proj_width = proj_acc.shape[1]
    sub_rows = own_rows // dp_count
    proj_parts = proj_acc.reshape(sources, dp_count, sub_rows, proj_width).transpose(1, 0, 2, 3)
    dp_index = lax.axis_index("dp")
    proj_sum = lax.dynamic_index_in_dim(proj_parts, dp_index, 0, keepdims=False).astype(WIDE)
    for q in range(1, dp_count):
        part = lax.dynamic_index_in_dim(proj_parts, dp_index ^ q, 0, keepdims=False)
        proj_sum = proj_sum + swap_partner(part, "dp", q).astype(WIDE)
    cluster_rows = model_weight[None, :] * (
        jnp.exp(cluster_logits - log_head[None, :]) - jnp.stack([in_first, in_second])
    )
    hidden_grad = row_back + lax.dot_general(
        cluster_rows, cluster_proj.astype(WIDE), (((0,), (1,)), ((), ())), precision=HIGH
    )
    cluster_acc = jnp.dot(cluster_rows, hidden_low.astype(WIDE), precision=HIGH)
    unit_three, inv_three = norm_stats(second_sum)
    second_grad, gain_three, shift_three = norm_backward(
        hidden_grad, unit_three, inv_three, norm_gains[2]
    )
    down_in = second_grad.astype(LOW)
    down_parts = exchange_columns(down_in)
    bias_down = jnp.sum(down_in.astype(WIDE), axis=0, keepdims=True)
    act_grad = product_nt(down_in, ffn_down)
    pre_grad = jnp.where(act_low.astype(WIDE) > 0, act_grad, 0.0).astype(LOW)
    up_bias_acc = jnp.sum(pre_grad.astype(WIDE), axis=0, keepdims=True)
    marks = [0, ff_width, ff_width + d_model, ff_width + 2 * d_model, ff_width + 3 * d_model]
    lefts = [left_all[:, a:b] for a, b in zip(marks[:-1], marks[1:])]
    down = Halving(grad_tile(lefts[0], after(down_parts, pre_grad)))
    norm_two_grad = product_nt(after(pre_grad, down.outgoing), ffn_up)
    unit_two, inv_two = norm_stats(first_sum)
    back_second, gain_two, shift_two = norm_backward(
        norm_two_grad, unit_two, inv_two, norm_gains[1]
    )
    first_grad_sum = second_grad + back_second
    attn_in = first_grad_sum.astype(LOW)
    bias_attn = jnp.sum(attn_in.astype(WIDE), axis=0, keepdims=True)
    mark = down.add(attn_in)
    up_width = ff_width // dp_count
    head_width = d_model // dp_count
    up_send = jnp.stack(
        [
            jnp.concatenate(
                [
                    pre_grad[:, k * up_width : (k + 1) * up_width],
                    attn_in[:, k * head_width : (k + 1) * head_width],
                ],
                axis=1,
            )
            for k in range(dp_count)
        ]
    )
    up_parts = lax.all_to_all(up_send, "dp", 0, 0)
    stacked_parts, sums_three = attention_back(
        lengths, after(attn_in, up_send, mark), attn_out, query_low, key_low, value_low, dp_count
    )
    mark = down.add(stacked_parts)
    qkv_parts = lax.all_to_all(after(stacked_parts, up_parts), "dp", 0, 0)
    word_send = after(word_packed.reshape(dp_count, -1, 128), qkv_parts)
    word_parts = lax.all_to_all(word_send, "dp", 0, 0)
    proj_rows = sub_rows * proj_width // (up_width + head_width)
    proj_block = proj_sum.astype(LOW).reshape(sources, proj_rows, up_width + head_width)
    up_parts = after(up_parts, mark)
    up = Halving(
        jnp.concatenate(
            [
                jnp.concatenate(
                    [
                        grad_tile(lefts[1], up_parts[:, :, :up_width]),
                        grad_tile(lefts[2], up_parts[:, :, up_width:]),
                    ],
                    axis=2,
                ),
                proj_block,
            ],
            axis=1,
        )
    )
    input_grad, sums_one = input_back(
        after(stacked_parts, up.outgoing, qkv_parts), attn_qkv, inputs, first_grad_sum, norm_gains
    )
    down_own = down.finish(input_grad)
    mark = up.add(input_grad, down_own)

    def by_store(value):
        rows = value.shape[0]
        return value.reshape(rows, sources, -1).transpose(1, 0, 2).reshape(sources, -1)

    small = jnp.concatenate(
        [
            by_store(jnp.concatenate([sums_one[0:1], gain_two, gain_three])),
            by_store(jnp.concatenate([sums_one[1:2], shift_two, shift_three])),
            by_store(jnp.concatenate([sums_three[0:1], sums_three[2:3], bias_attn, bias_down])),
            by_store(up_bias_acc),
            by_store(cluster_acc),
        ],
        axis=1,
    )
    small_count = small.shape[1]
    small_rows = -(-small_count // (3 * head_width))
    if own_rows % 128 == 0:
        small_rows = -(-small_rows // 8) * 8
    small = jnp.pad(small, ((0, 0), (0, small_rows * 3 * head_width - small_count)))
    small = small.reshape(sources, small_rows, 3 * head_width).astype(LOW)
    qkv = Halving(
        jnp.concatenate([grad_tile(lefts[3], after(qkv_parts, mark)), small], axis=1)
    )
    down_pieces = gather_dp(down_own)
    mark = qkv.add(qkv.outgoing)
    mark = up.add(mark)
    word_own = jnp.sum(after(word_parts, mark).astype(WIDE), axis=0).astype(LOW)
    mark = qkv.add(word_own)
    word_pieces = gather_dp(word_own)
    down_out = join_pieces(after(down_pieces, mark), 1, 0, head_width, 1)
    up_own = up.finish(down_out)
    up_pieces = gather_dp(up_own)
    word_pieces = after(word_pieces, up_own)
    head_t, first_out, second_out = unpack_words(jnp.stack(word_pieces), word_shapes)
    head_out = head_t.T
    qkv_own = qkv.finish(head_t)
    qkv_pieces = gather_dp(qkv_own)
    up_pieces = after(up_pieces, qkv_own)
    up_main = [piece[:own_rows] for piece in up_pieces]
    up_out = join_pieces(up_main, 1, 0, up_width, 1)
    out_out = join_pieces(up_main, 1, up_width, head_width, 1)
    proj_out = join_pieces(
        [piece[own_rows:].reshape(sub_rows, proj_width) for piece in up_pieces],
        0,
        0,
        sub_rows,
        0,
    )
    qkv_main = [piece[:own_rows] for piece in qkv_pieces]
    qkv_out = jnp.stack(
        [join_pieces(qkv_main, 1, kind * head_width, head_width, 1) for kind in range(3)]
    )
    small_sum = sum(piece[own_rows:].astype(WIDE) for piece in qkv_pieces).reshape(-1)
    sizes = [3 * own_rows, 3 * own_rows, 4 * own_rows, ff_width // sources, 2 * own_rows]
    ends = [0]
    for size in sizes:
        ends.append(ends[-1] + size)
    gains_out, shifts_out, biases_out, upb_out, cluster_out = (
        small_sum[a:b] for a, b in zip(ends[:-1], ends[1:])
    )
    return (
        token_loss,
        input_grad,
        qkv_out,
        out_out,
        up_out,
        down_out,
        gains_out.reshape(3, own_rows),
        shifts_out.reshape(3, own_rows),
        biases_out.reshape(4, own_rows),
        upb_out,
        cluster_out.reshape(2, own_rows).T,
        proj_out[:, : proj_first.shape[1]],
        proj_out[:, proj_first.shape[1] :],
        head_out,
        first_out,
        second_out,
    )


def solution(mesh):
    dp_count = mesh.shape["dp"]
    store_count = mesh.shape["store"]
    split = Mesh(mesh.devices.reshape(dp_count, store_count // 2, 2), ("dp",) + STORE)
    everyone = ("dp",) + STORE
    return jax.shard_map(
        shards,
        mesh=split,
        in_specs=(
            P(everyone, None),
            P(everyone),
            P("dp"),
            P(),
            P(),
            P(),
            P(),
            P(),
            P(),
            P(),
            P(),
            P(),
            P(),
            P(),
            P(None, STORE),
            P(None, STORE),
            P(None, STORE),
            P(STORE, None),
            P("dp", STORE, None, None),
            P("dp", STORE, None, None, None),
            P(everyone, None),
        ),
        out_specs=(
            P(everyone),
            P(everyone, None),
            P(None, STORE, None),
            P(STORE, None),
            P(STORE, None),
            P(STORE, None),
            P(None, STORE),
            P(None, STORE),
            P(None, STORE),
            P(STORE),
            P(STORE, None),
            P(STORE, None),
            P(STORE, None),
            P(None, STORE),
            P(None, STORE),
            P(None, STORE),
        ),
        check_vma=False,
    )
```
